128 devices in a mesh: gx: 8 (over x_hi, y), gy: 16 (over x_lo, z, core).
Axes of the slice: x: 4 (x_hi: 2, x_lo: 2; x = x_hi * 2 + x_lo), y: 4, z: 4, core: 2. Of those that a mesh axis runs over, the one named last changes fastest.
Arguments:
- conductivity: float32 [16, 2048, 2048], P(None, 'gx', 'gy'), may hold values from 0.5 to 5
- source: float32 [16, 2048, 2048], P(None, 'gx', 'gy'), may hold values from -24 to 24
- potential_start: float32 [16, 2048, 2048], P(None, 'gx', 'gy'), may hold values from -3 to 3
- shell_to_depth: float32 [1024, 16], replicated, may hold values from -1.5 to 1.5
- shell_to_girth: float32 [64, 512], replicated, may hold values from -0.75 to 0.75
- pile_resistance: float32 [128], P(('gx', 'gy')), may hold values from 0.3 to 3
- coating_mask: int32 [128, 1024, 512], P(('gx', 'gy')), may hold values 0 or 1
- pile_tile: int32 [128], replicated, may hold values from 0 to 127, as said below
- pile_block: int32 [128], replicated, may hold values from 0 to 511
Outputs:
- potential_end: float32 [16, 2048, 2048], P(None, 'gx', 'gy')
- surface_current: float32 [128, 1024, 512], P(('gx', 'gy'))
The draws below stay inside these ranges and needn't reach their ends.
Inputs may be any that keep to these rules, and one draw needn't show every extreme that they name: `pile_tile`: at most 4 piles lie in one tile, and some tile holds exactly 4.
All inputs are finite; a program needn't handle non-finite values. No bound on the sum of `coating_mask` on one device may be relied on, other than what follows from the above.
Results may differ from the reference program's by a relative error of at most 0.0003.
Values sent between devices are 32-bit elements; how exact they have to be, the bound alone decides.
No kernel may reach another device: no remote copies, remote signals or barrier semaphores. Data moves between devices by JAX's collectives and lax.ppermute only.
A program may use at most 192 MiB of HBM per device.

```python
import math
import jax
import jax.numpy as jnp
from jax import lax

DEPTH = 16
CX = 256
CY = 128
BLK = 8
PILE_DEV = 1
GIRTH = 512
PD = 1024
SWEEPS = 4
NEWTON = 3
NX = 2048
NY = 2048
PILES = 128
NBLK = 512
N_GY = 16


def draw_pile_tile(key, part):
    first_key, second_key = jax.random.split(jax.random.fold_in(key, 17))
    pile_ids = jnp.arange(PILES)
    half = PILES // 2
    quarter = PILES // 4
    groups = jnp.where(pile_ids < half, pile_ids // 4, jnp.where(pile_ids < half + quarter, PILES // 8 + (pile_ids - half) // 2, PILES // 4 + (pile_ids - half - quarter)))
    tiles = jax.random.permutation(first_key, PILES // PILE_DEV)
    shuffled = jax.random.permutation(second_key, PILES)
    return tiles[groups[shuffled]].astype(jnp.int32)


def touch_ends(result, stream_key, smallest, top_value):
    spot = [jax.random.randint(jax.random.fold_in(stream_key, axis), (), 0, length) for axis, length in enumerate(result.shape)]
    longest = result.shape.index(max(result.shape))
    neighbour = spot[:longest] + [(spot[longest] + 1) % result.shape[longest]] + spot[longest + 1:]
    return result.at[tuple(spot)].set(smallest).at[tuple(neighbour)].set(top_value)


def shard_levels(rng, dims, shards, low, largest):
    level, own = 1.0, jax.random.fold_in(rng, 6)
    for position, parts in shards:
        steps = jnp.exp(jax.random.uniform(jax.random.fold_in(own, position), (parts,), jnp.float32, low / len(shards), largest / len(shards)))
        level = level * jnp.repeat(steps, dims[position] // parts).reshape([-1 if axis == position else 1 for axis in range(len(dims))])
    return level


def centred(key, shape, width, most, cuts=(), dtype=jnp.bfloat16):
    entries = width * jax.random.normal(key, shape, jnp.float32)
    if cuts:
        entries = entries * shard_levels(key, shape, cuts, -0.22, 0.18)
    return jnp.clip(entries, -most, most).astype(dtype)


def setup_inputs(seed: int = 0) -> dict:
    keys = jax.random.split(jax.random.key(seed), 10)
    return {
        "conductivity": jnp.clip(jnp.exp(math.log(5.0) - 2.3025851 * jax.random.uniform(keys[0], (DEPTH, NX, NY), jnp.float32) ** shard_levels(keys[0], (DEPTH, NX, NY), ((1, 8), (2, 16)), -0.2, 0.2)), 0.5, 5.0),
        "source": centred(keys[1], (DEPTH, NX, NY), 4.0, 24.0, ((1, 8), (2, 16)), jnp.float32),
        "potential_start": centred(keys[2], (DEPTH, NX, NY), 0.5, 3.0, ((1, 8), (2, 16)), jnp.float32),
        "shell_to_depth": centred(keys[3], (PD, DEPTH), DEPTH ** -0.5, 1.5, (), jnp.float32),
        "shell_to_girth": centred(keys[4], (BLK * BLK, GIRTH), (BLK * BLK) ** -0.5, 0.75, (), jnp.float32),
        "pile_resistance": jnp.clip(jnp.exp(math.log(3.0) - 2.3025851 * jax.random.uniform(keys[5], (PILES,), jnp.float32) ** shard_levels(keys[5], (PILES,), ((0, 128),), -0.2, 0.2)), 0.3, 3.0),
        "coating_mask": touch_ends((jax.random.randint(keys[6], (PILES, PD, GIRTH), 0, 3) < 1).astype(jnp.int32), jax.random.fold_in(keys[6], 1), 0, 1),
        "pile_tile": draw_pile_tile(jax.random.fold_in(keys[9], 71), 0),
        "pile_block": touch_ends(jax.random.randint(keys[8], (PILES,), 0, NBLK), jax.random.fold_in(keys[8], 1), 0, NBLK - 1).astype(jnp.int32),
    }


vertical_ratio = 0.25
inject_gain = 0.5
anodic_slope = 1.2
cathodic_slope = 0.8
coated_conductance = 0.05

def relax_sweep(padded_potential, padded_conduct, source):
    conduct = padded_conduct[:, 1:-1, 1:-1]
    centre = padded_potential[:, 1:-1, 1:-1]
    w_north = 0.5 * (conduct + padded_conduct[:, :-2, 1:-1])
    w_south = 0.5 * (conduct + padded_conduct[:, 2:, 1:-1])
    w_west = 0.5 * (conduct + padded_conduct[:, 1:-1, :-2])
    w_east = 0.5 * (conduct + padded_conduct[:, 1:-1, 2:])
    summed = source + w_north * padded_potential[:, :-2, 1:-1] + w_south * padded_potential[:, 2:, 1:-1]
    summed = summed + w_west * padded_potential[:, 1:-1, :-2] + w_east * padded_potential[:, 1:-1, 2:]
    weight = w_north + w_south + w_west + w_east
    vertical = vertical_ratio * 0.5 * (conduct[1:] + conduct[:-1])
    zero_layer = jnp.zeros_like(conduct[:1])
    w_upper = jnp.concatenate([vertical, zero_layer], axis=0)
    w_lower = jnp.concatenate([zero_layer, vertical], axis=0)
    summed = summed + w_upper * jnp.concatenate([centre[1:], zero_layer], axis=0)
    summed = summed + w_lower * jnp.concatenate([zero_layer, centre[:-1]], axis=0)
    weight = weight + w_upper + w_lower
    return summed / weight

def polarize(shell, resist, bare, to_depth, to_girth):
    highest = lax.Precision.HIGHEST
    near_field = jnp.dot(shell, to_girth, precision=highest)
    driving = jnp.dot(to_depth, near_field, precision=highest)
    bare_float = bare.astype(jnp.float32)
    polarized = driving
    for step in range(NEWTON):
        anodic = jnp.exp(polarized / anodic_slope)
        cathodic = jnp.exp(-polarized / cathodic_slope)
        current = bare_float * (anodic - cathodic) + (1.0 - bare_float) * coated_conductance * polarized
        derivative = bare_float * (anodic / anodic_slope + cathodic / cathodic_slope) + (1.0 - bare_float) * coated_conductance
        polarized = polarized - (polarized - driving + resist * current) / (1.0 + resist * derivative)
    anodic = jnp.exp(polarized / anodic_slope)
    cathodic = jnp.exp(-polarized / cathodic_slope)
    current = bare_float * (anodic - cathodic) + (1.0 - bare_float) * coated_conductance * polarized
    back_scale = math.sqrt(shell.shape[0] * shell.shape[1] / (current.shape[0] * current.shape[1]))
    returned = jnp.dot(jnp.dot(to_depth.T, current, precision=highest), to_girth.T, precision=highest) * back_scale
    return (current, returned)

def reference(conductivity, source, potential_start, shell_to_depth, shell_to_girth, pile_resistance, coating_mask, pile_tile, pile_block):
    pads = ((0, 0), (1, 1), (1, 1))
    padded_conduct = jnp.pad(conductivity, pads)
    potential = potential_start
    for sweep in range(SWEEPS):
        potential = relax_sweep(jnp.pad(potential, pads), padded_conduct, source)
    per_row = CY // BLK
    start_x = (pile_tile // N_GY * CX + pile_block // per_row * BLK).astype(jnp.int32)
    start_y = (pile_tile % N_GY * CY + pile_block % per_row * BLK).astype(jnp.int32)
    zero_index = jnp.zeros((), jnp.int32)

    def extract(sx, sy):
        return lax.dynamic_slice(potential, (zero_index, sx, sy), (DEPTH, BLK, BLK)).reshape(DEPTH, BLK * BLK)
    shells = jax.vmap(extract)(start_x, start_y)

    def one_pile(items):
        return polarize(items[0], items[1], items[2], shell_to_depth, shell_to_girth)
    currents, returned = lax.map(one_pile, (shells, pile_resistance, coating_mask))

    def add_one(i, accumulated):
        patch = returned[i].reshape(DEPTH, BLK, BLK)
        block_now = lax.dynamic_slice(accumulated, (zero_index, start_x[i], start_y[i]), (DEPTH, BLK, BLK))
        return lax.dynamic_update_slice(accumulated, block_now + patch, (zero_index, start_x[i], start_y[i]))
    injected = lax.fori_loop(0, PILES, add_one, jnp.zeros_like(potential))
    return (potential - inject_gain * injected, currents)
```

```python
import math

import jax
import jax.numpy as jnp
from jax import lax
from jax.sharding import PartitionSpec as P

BLK = 8
CAP = 4
PILE_DEV = 1
SWEEPS = 4
NEWTON = 3


vertical_ratio = 0.25
inject_gain = 0.5
anodic_slope = 1.2
cathodic_slope = 0.8
coated_conductance = 0.05


def with_halo(block, sides, width):
    for axis, dim in sides:
        count = lax.axis_size(axis)
        forward = [(i, i + 1) for i in range(count - 1)]
        backward = [(target, source) for source, target in forward]
        low = lax.ppermute(
            lax.slice_in_dim(block, block.shape[dim] - width, None, axis=dim), axis, forward
        )
        high = lax.ppermute(lax.slice_in_dim(block, 0, width, axis=dim), axis, backward)
        block = jnp.concatenate([low, block, high], axis=dim)
    return block


def relax_sweep(padded_potential, padded_conduct, source):
    conduct = padded_conduct[:, 1:-1, 1:-1]
    centre = padded_potential[:, 1:-1, 1:-1]
    w_north = 0.5 * (conduct + padded_conduct[:, :-2, 1:-1])
    w_south = 0.5 * (conduct + padded_conduct[:, 2:, 1:-1])
    w_west = 0.5 * (conduct + padded_conduct[:, 1:-1, :-2])
    w_east = 0.5 * (conduct + padded_conduct[:, 1:-1, 2:])
    summed = (
        source + w_north * padded_potential[:, :-2, 1:-1] + w_south * padded_potential[:, 2:, 1:-1]
    )
    summed = (
        summed + w_west * padded_potential[:, 1:-1, :-2] + w_east * padded_potential[:, 1:-1, 2:]
    )
    weight = w_north + w_south + w_west + w_east
    vertical = vertical_ratio * 0.5 * (conduct[1:] + conduct[:-1])
    zero_layer = jnp.zeros_like(conduct[:1])
    w_upper = jnp.concatenate([vertical, zero_layer], axis=0)
    w_lower = jnp.concatenate([zero_layer, vertical], axis=0)
    summed = summed + w_upper * jnp.concatenate([centre[1:], zero_layer], axis=0)
    summed = summed + w_lower * jnp.concatenate([zero_layer, centre[:-1]], axis=0)
    weight = weight + w_upper + w_lower
    return summed / weight


def polarize(shell, resist, bare, to_depth, to_girth):
    highest = lax.Precision.HIGHEST
    near_field = jnp.dot(shell, to_girth, precision=highest)
    driving = jnp.dot(to_depth, near_field, precision=highest)
    bare_float = bare.astype(jnp.float32)
    polarized = driving
    for step in range(NEWTON):
        anodic = jnp.exp(polarized / anodic_slope)
        cathodic = jnp.exp(-polarized / cathodic_slope)
        current = (
            bare_float * (anodic - cathodic) + (1.0 - bare_float) * coated_conductance * polarized
        )
        derivative = (
            bare_float * (anodic / anodic_slope + cathodic / cathodic_slope)
            + (1.0 - bare_float) * coated_conductance
        )
        polarized = polarized - (polarized - driving + resist * current) / (
            1.0 + resist * derivative
        )
    anodic = jnp.exp(polarized / anodic_slope)
    cathodic = jnp.exp(-polarized / cathodic_slope)
    current = bare_float * (anodic - cathodic) + (1.0 - bare_float) * coated_conductance * polarized
    back_scale = math.sqrt(shell.shape[0] * shell.shape[1] / (current.shape[0] * current.shape[1]))
    returned = (
        jnp.dot(jnp.dot(to_depth.T, current, precision=highest), to_girth.T, precision=highest)
        * back_scale
    )
    return (current, returned)


def on_device(
    conductivity,
    source,
    potential_start,
    shell_to_depth,
    shell_to_girth,
    pile_resistance,
    coating_mask,
    pile_tile,
    pile_block,
):
    layers, tile_rows, tile_cols = conductivity.shape
    padded_conduct = with_halo(conductivity, (("gx", 1), ("gy", 2)), 1)
    potential = potential_start
    for sweep in range(SWEEPS):
        padded_potential = with_halo(potential, (("gx", 1), ("gy", 2)), 1)
        potential = relax_sweep(padded_potential, padded_conduct, source)
    my_tile = lax.axis_index("gx") * lax.axis_size("gy") + lax.axis_index("gy")
    piles = pile_tile.shape[0]
    pile_ids = jnp.arange(piles, dtype=jnp.int32)
    same_tile = pile_tile[:, None] == pile_tile[None, :]
    earlier = pile_ids[:, None] > pile_ids[None, :]
    slot_of = jnp.sum((same_tile & earlier).astype(jnp.int32), axis=1)
    per_row = tile_cols // BLK
    shell_cells = layers * BLK * BLK
    zero_index = jnp.zeros((), jnp.int32)
    slot_piles = []
    slot_filled = []
    slot_starts = []
    shells = []
    for j in range(CAP):
        selected = (pile_tile == my_tile) & (slot_of == j)
        filled = jnp.any(selected)
        pile_id = jnp.sum(jnp.where(selected, pile_ids, 0))
        block_id = pile_block[pile_id]
        start_x = block_id // per_row * BLK
        start_y = block_id % per_row * BLK
        patch = lax.dynamic_slice(potential, (zero_index, start_x, start_y), (layers, BLK, BLK))
        shells.append(jnp.where(filled, patch.reshape(shell_cells), 0.0))
        slot_piles.append(pile_id)
        slot_filled.append(filled)
        slot_starts.append((start_x, start_y))
    sent = jnp.zeros((piles, 8, shell_cells // 8), jnp.float32)
    for j in range(CAP):
        chosen = (pile_tile == my_tile) & (slot_of == j)
        sent = jnp.where(chosen[:, None, None], shells[j].reshape(1, 8, shell_cells // 8), sent)
    received = lax.all_to_all(sent, ("gx", "gy"), 0, 0, tiled=True)
    own_shells = [
        lax.dynamic_slice_in_dim(received, pile_tile[my_tile], 1, 0)[0].reshape(shell_cells)
    ]
    q = 0
    current, returned = polarize(
        own_shells[q].reshape(layers, BLK * BLK),
        pile_resistance[q],
        coating_mask[q],
        shell_to_depth,
        shell_to_girth,
    )
    currents = [current]
    returns = [returned.reshape(shell_cells)]
    surface_current = jnp.stack(currents)
    own_return = returns[0].reshape(1, 8, shell_cells // 8)
    every_return = lax.all_to_all(
        jnp.broadcast_to(own_return, (piles, 8, shell_cells // 8)), ("gx", "gy"), 0, 0, tiled=True
    )
    injected = jnp.zeros_like(potential)
    for j in range(CAP):
        start_x, start_y = slot_starts[j]
        vector = lax.dynamic_slice_in_dim(every_return, slot_piles[j], 1, 0)[0].reshape(shell_cells)
        patch = jnp.where(slot_filled[j], vector, 0.0).reshape(layers, BLK, BLK)
        block_now = lax.dynamic_slice(injected, (zero_index, start_x, start_y), (layers, BLK, BLK))
        injected = lax.dynamic_update_slice(
            injected, block_now + patch, (zero_index, start_x, start_y)
        )
    return (potential - inject_gain * injected, surface_current)


def solution(mesh):
    placed = (
        P(None, "gx", "gy"),
        P(None, "gx", "gy"),
        P(None, "gx", "gy"),
        P(),
        P(),
        P(("gx", "gy")),
        P(("gx", "gy"), None, None),
        P(),
        P(),
    )
    return jax.shard_map(
        on_device,
        mesh=mesh,
        in_specs=placed,
        out_specs=(P(None, "gx", "gy"), P(("gx", "gy"), None, None)),
        check_vma=False,
    )
```

```python
import math

import jax
import jax.numpy as jnp
from jax import lax
from jax.experimental import pallas as pl
from jax.experimental.pallas import tpu as pltpu
from jax.sharding import PartitionSpec as P

BLK = 8
CAP = 4
SWEEPS = 4
NEWTON = 3
LANES = 128
SUB = 8
VMEM_LIMIT = 56 << 20

vertical_ratio = 0.25
inject_gain = 0.5
anodic_slope = 1.2
cathodic_slope = 0.8
coated_conductance = 0.05


def turn(x, shift):
    return pltpu.roll(x, shift % LANES, 1)


def lane_ids(rows=SUB):
    return lax.broadcasted_iota(jnp.int32, (rows, LANES), 1)


def pack_rows(load, layers):
    lane = lane_ids()
    packed = jnp.zeros((SUB, LANES), jnp.float32)
    for l in range(layers):
        near = ((lane + 4) % LANES) // BLK == l
        packed = jnp.where(near, turn(load(l), BLK * l), packed)
    return packed


def pack_kernel(tile_ref, me_ref, p_ref, c_ref, s_ref, out_ref, table_ref):
    layers, rows, _ = p_ref.shape

    @pl.when(pl.program_id(0) == 0)
    def _():
        for j in range(CAP):
            table_ref[j] = -1

        def look(k, count):
            mine = tile_ref[k] == me_ref[0]

            @pl.when(mine & (count < CAP))
            def _():
                table_ref[count] = k

            return count + mine.astype(jnp.int32)

        lax.fori_loop(0, tile_ref.shape[0], look, jnp.int32(0))

    def body(t, carry):
        at = pl.ds(pl.multiple_of(t * SUB, SUB), SUB)
        for i, ref in enumerate((p_ref, c_ref, s_ref)):
            out_ref[i, at, :] = pack_rows(lambda l: ref[l, at, :], layers)
        return carry

    lax.fori_loop(0, rows // SUB, body, 0)


def pack_edge_kernel(top_ref, bottom_ref, packed_ref, out_ref):
    layers = top_ref.shape[1]
    first = pl.program_id(0) == 0
    for i in range(3):
        out_ref[i] = pack_rows(
            lambda l: jnp.where(first, top_ref[i, l], bottom_ref[i, l]), layers
        )


def sweep_kernel(
    table_ref,
    block_ref,
    p_hbm,
    c_hbm,
    s_hbm,
    top_hbm,
    bottom_hbm,
    left_ref,
    right_ref,
    out_ref,
    sent_ref,
    c_v,
    s_v,
    pa_v,
    pb_v,
    we_v,
    ws_v,
    wu_v,
    inv_v,
    strip_v,
    sem,
):
    layers, tile_rows, _ = p_hbm.shape
    tiles = tile_rows // SUB
    first, last = 1, tiles + 2
    lane = lane_ids()
    in_group = lane % BLK
    arrays = (pa_v, c_v, s_v)
    copies = []
    for i, (src, dst) in enumerate(zip((p_hbm, c_hbm, s_hbm), arrays)):
        copies.append(
            pltpu.make_async_copy(src, dst.at[:, pl.ds(2 * SUB, tile_rows), :], sem.at[i, 0])
        )
        copies.append(
            pltpu.make_async_copy(top_hbm.at[i], dst.at[:, pl.ds(SUB, SUB), :], sem.at[i, 1])
        )
        copies.append(
            pltpu.make_async_copy(
                bottom_hbm.at[i], dst.at[:, pl.ds(last * SUB, SUB), :], sem.at[i, 2]
            )
        )
    for copy in copies:
        copy.start()
    zero = jnp.zeros((SUB, LANES), jnp.float32)
    for t in (0, last + 1):
        for ref in (c_v, pa_v, pb_v, ws_v):
            for l in range(layers):
                ref[l, t * SUB : (t + 1) * SUB, :] = zero
        for i in range(strip_v.shape[0]):
            strip_v[i, t * SUB : (t + 1) * SUB, :] = zero
    psa, cs, ss, psb, wes, wss, wus, invs = (strip_v.at[i] for i in range(8))

    def at(t, shift=0):
        if shift:
            return pl.ds(t * SUB + shift, SUB)
        return pl.ds(pl.multiple_of(t * SUB, SUB), SUB)

    def gather_strips(t, carry):
        src = jnp.where(t == first, tiles, jnp.where(t == last, tiles + 1, t - 2))
        src = pl.ds(pl.multiple_of(src * SUB, SUB), SUB)
        for i, dst in enumerate((psa, cs, ss)):
            dst[at(t), :] = jnp.where(
                in_group < 4, right_ref[i, src, :], turn(left_ref[i, src, :], BLK)
            )
        return carry

    lax.fori_loop(first, last + 1, gather_strips, 0)
    for copy in copies:
        copy.wait()

    def inverse(c, weight):
        inside = c > 0.0
        return jnp.where(inside, 1.0 / jnp.where(inside, weight, 1.0), 0.0)

    def prepare(t, carry):
        c_strip = cs[at(t), :]
        spread = jnp.where(in_group == 0, c_strip, turn(c_strip, -6))
        border = zero
        below = None
        here = c_v[0, at(t), :]
        for l in range(layers):
            side = turn(spread, LANES - 1 - BLK * l)
            we = 0.5 * (here + jnp.where(lane == LANES - 1, side, turn(here, -1)))
            ww = jnp.where(lane == 0, 0.5 * (here + side), turn(we, 1))
            ws = 0.5 * (here + c_v[l, at(t, 1), :])
            wn = 0.5 * (here + c_v[l, at(t, -1), :])
            weight = we + ww + ws + wn
            if l + 1 < layers:
                above = c_v[l + 1, at(t), :]
                wu = (0.5 * vertical_ratio) * (here + above)
                wu_v[l, at(t), :] = wu
                weight = weight + wu
            if l:
                weight = weight + below
            we_v[l, at(t), :] = we
            ws_v[l, at(t), :] = ws
            inv_v[l, at(t), :] = inverse(here, weight)
            border = jnp.where(lane // BLK == l, turn(here, BLK * l + 1), border)
            if l + 1 < layers:
                below, here = wu, above
        we = 0.5 * (
            c_strip + jnp.where(in_group == BLK - 1, turn(border, 6), turn(c_strip, -1))
        )
        ww = jnp.where(in_group == 0, 0.5 * (c_strip + border), turn(we, 1))
        ws = 0.5 * (c_strip + cs[at(t, 1), :])
        wn = 0.5 * (c_strip + cs[at(t, -1), :])
        wu = jnp.where(
            lane < LANES - BLK, (0.5 * vertical_ratio) * (c_strip + turn(c_strip, -BLK)), 0.0
        )
        wes[at(t), :] = we
        wss[at(t), :] = ws
        wus[at(t), :] = wu
        invs[at(t), :] = inverse(c_strip, we + ww + ws + wn + wu + turn(wu, BLK))
        return carry

    lax.fori_loop(first, last + 1, prepare, 0)

    def make_sweep(old, old_strip, store, new_strip):
        def sweep(t, carry):
            p_strip = old_strip[at(t), :]
            we_strip = wes[at(t), :]
            flux_strip = we_strip * p_strip
            spread = jnp.where(in_group == 0, p_strip, turn(flux_strip, -6))
            border = zero
            below = None
            wu_below = None
            here = old[0, at(t), :]
            for l in range(layers):
                side = turn(spread, LANES - 1 - BLK * l)
                we = we_v[l, at(t), :]
                flux = we * here
                total = s_v[l, at(t), :] + we * jnp.where(lane == LANES - 1, side, turn(here, -1))
                total = total + jnp.where(lane == 0, side, turn(flux, 1))
                total = total + ws_v[l, at(t), :] * old[l, at(t, 1), :]
                total = total + ws_v[l, at(t, -1), :] * old[l, at(t, -1), :]
                if l:
                    total = total + wu_below * below
                if new_strip is not None:
                    mixed = jnp.where(lane == LANES - 1, flux, here)
                    border = jnp.where(lane // BLK == l, turn(mixed, BLK * l + 1), border)
                if l + 1 < layers:
                    above = old[l + 1, at(t), :]
                    wu = wu_v[l, at(t), :]
                    total = total + wu * above
                    below, here, wu_below = here, above, wu
                store(l, t, total * inv_v[l, at(t), :])
            if new_strip is not None:
                wu = wus[at(t), :]
                east = jnp.where(in_group == BLK - 1, turn(border, 6), turn(p_strip, -1))
                total = ss[at(t), :] + we_strip * east
                total = total + jnp.where(in_group == 0, border, turn(flux_strip, 1))
                total = total + wss[at(t), :] * old_strip[at(t, 1), :]
                total = total + wss[at(t, -1), :] * old_strip[at(t, -1), :]
                total = total + wu * turn(p_strip, -BLK) + turn(wu * p_strip, BLK)
                new_strip[at(t), :] = total * invs[at(t), :]
            return carry

        return sweep

    pairs = ((pa_v, psa), (pb_v, psb))
    for k in range(SWEEPS - 1):
        old, old_strip = pairs[k % 2]
        new, new_strip = pairs[(k + 1) % 2]

        def store(l, t, value, new=new):
            new[l, at(t), :] = value

        lax.fori_loop(first, last + 1, make_sweep(old, old_strip, store, new_strip), 0)

    def store_out(l, t, value):
        out_ref[l, pl.ds(pl.multiple_of(t * SUB - 2 * SUB, SUB), SUB), :] = value

    old, old_strip = pairs[(SWEEPS - 1) % 2]
    lax.fori_loop(first + 1, last, make_sweep(old, old_strip, store_out, None), 0)

    sent_ref[...] = jnp.zeros_like(sent_ref)
    for j in range(CAP):
        k = table_ref[j]

        @pl.when(k >= 0)
        def _():
            block = block_ref[k]
            per_row = LANES // BLK
            rows = pl.ds(pl.multiple_of(block // per_row * BLK, BLK), BLK)
            start = block % per_row * BLK
            packet = zero
            for l in range(layers):
                group = layers - 1 - l
                moved = pltpu.roll(out_ref[l, rows, :], (BLK * group + LANES - start) % LANES, 1)
                packet = jnp.where(lane // BLK == group, moved, packet)
            sent_ref[k] = packet


def polarize_kernel(
    source_ref, resist_ref, got_ref, depth_ref, girth_ref, bare_ref, current_ref, sent_ref, near_v, drive_v, sum_v
):
    layers = depth_ref.shape[1]
    rows, girth = bare_ref.shape[1:]
    step = pl.program_id(0)
    highest = lax.Precision.HIGHEST
    resist = resist_ref[0]
    lane = lane_ids(layers)
    row = lax.broadcasted_iota(jnp.int32, (layers, LANES), 0)

    @pl.when(step == 0)
    def _():
        packet = got_ref[source_ref[0]]
        shell = jnp.zeros((layers, LANES), jnp.float32)
        for x in range(BLK):
            spread = jnp.broadcast_to(packet[x : x + 1, :], (layers, LANES))
            spread = pltpu.roll(spread, 0, 1, stride=BLK, stride_axis=0)
            spread = turn(spread, BLK * (x + 1) - BLK * layers)
            shell = jnp.where(lane // BLK == x, spread, shell)
        near_v[...] = jnp.dot(
            shell[:, : BLK * BLK],
            girth_ref[...],
            precision=highest,
            preferred_element_type=jnp.float32,
        )
        sum_v[...] = jnp.zeros_like(sum_v)

    drive_v[...] = jnp.dot(
        depth_ref[...], near_v[...], precision=highest, preferred_element_type=jnp.float32
    )
    up = math.log2(math.e) / anodic_slope
    down = -math.log2(math.e) / cathodic_slope
    steep = resist / anodic_slope
    steep_down = resist / cathodic_slope
    coated = coated_conductance / (1.0 + coated_conductance * resist)
    chunk = 16

    def body(i, carry):
        at = pl.ds(pl.multiple_of(i * chunk, chunk), chunk)
        driving = drive_v[at, :]
        value = driving
        for n in range(NEWTON):
            anodic = jnp.exp2(value * up)
            cathodic = jnp.exp2(value * down)
            excess = resist * (anodic - cathodic)
            if n:
                excess = excess + (value - driving)
            slope = 1.0 + (steep * anodic + steep_down * cathodic)
            value = value - excess / slope
        bare_current = jnp.exp2(value * up) - jnp.exp2(value * down)
        current_ref[0, at, :] = jnp.where(bare_ref[0, at, :] != 0, bare_current, coated * driving)
        return carry

    lax.fori_loop(0, rows // chunk, body, 0)
    sum_v[...] += lax.dot_general(
        depth_ref[...],
        current_ref[0],
        (((0,), (0,)), ((), ())),
        precision=highest,
        preferred_element_type=jnp.float32,
    )

    @pl.when(step == pl.num_programs(0) - 1)
    def _():
        cells = layers * BLK * BLK
        scale = math.sqrt(cells / (rows * girth * pl.num_programs(0)))
        back = scale * lax.dot_general(
            sum_v[...],
            girth_ref[...],
            (((1,), (1,)), ((), ())),
            precision=highest,
            preferred_element_type=jnp.float32,
        )
        back = jnp.concatenate([back, jnp.zeros_like(back)], axis=1)
        lines = []
        for x in range(BLK):
            spread = turn(back, -BLK * x) if x else back
            spread = pltpu.roll(spread, 0, 1, stride=BLK, stride_axis=0)
            spread = jnp.where(lane // BLK == row, spread, 0.0)
            lines.append(jnp.sum(spread, axis=0, keepdims=True))
        sent_ref[...] = jnp.broadcast_to(jnp.concatenate(lines, axis=0)[None], sent_ref.shape)


def inject_kernel(table_ref, block_ref, got_ref, p_hbm, out_hbm, work_v, sem):
    layers = p_hbm.shape[0]
    per_row = LANES // BLK
    lane = lane_ids()
    piles = [table_ref[j] for j in range(CAP)]
    blocks = [block_ref[jnp.maximum(k, 0)] for k in piles]
    def window(ref, j):
        return ref.at[:, pl.ds(pl.multiple_of(blocks[j] // per_row * BLK, BLK), BLK), :]

    heads = []
    for j in range(CAP):
        head = piles[j] >= 0
        for i in range(j):
            head = head & jnp.logical_not(
                (piles[i] >= 0) & (blocks[i] // per_row == blocks[j] // per_row)
            )
        heads.append(head)
    for j in range(CAP):

        @pl.when(heads[j])
        def _():
            pltpu.make_async_copy(window(p_hbm, j), work_v.at[j], sem.at[0, j]).start()

    for j in range(CAP):

        @pl.when(heads[j])
        def _():
            pltpu.make_async_copy(window(p_hbm, j), work_v.at[j], sem.at[0, j]).wait()
            for i in range(j, CAP):

                @pl.when((piles[i] >= 0) & (blocks[i] // per_row == blocks[j] // per_row))
                def _():
                    start = blocks[i] % per_row * BLK
                    packet = inject_gain * got_ref[jnp.maximum(piles[i], 0)]
                    for l in range(layers):
                        moved = pltpu.roll(packet, (start + LANES - BLK * l) % LANES, 1)
                        inside = (lane >= start) & (lane < start + BLK)
                        work_v[j, l] = work_v[j, l] - jnp.where(inside, moved, 0.0)

            pltpu.make_async_copy(work_v.at[j], window(out_hbm, j), sem.at[1, j]).start()

    for j in range(CAP):

        @pl.when(heads[j])
        def _():
            pltpu.make_async_copy(work_v.at[j], window(out_hbm, j), sem.at[1, j]).wait()


def on_device(
    conductivity,
    source,
    potential_start,
    shell_to_depth,
    shell_to_girth,
    pile_resistance,
    coating_mask,
    pile_tile,
    pile_block,
):
    layers, rows, cols = conductivity.shape
    piles = pile_tile.shape[0]
    depth_cells, girth = coating_mask.shape[1:]
    both = ("gx", "gy")
    me = (lax.axis_index("gx") * lax.axis_size("gy") + lax.axis_index("gy")).astype(jnp.int32)
    me = me.reshape(1)
    smem = pl.BlockSpec(memory_space=pltpu.SMEM)
    vmem = pl.BlockSpec(memory_space=pltpu.VMEM)
    anywhere = pl.BlockSpec(memory_space=pl.ANY)
    f32 = jnp.float32
    three = (potential_start, conductivity, source)

    def pass_on(value, axis, up):
        count = lax.axis_size(axis)
        pairs = [(i, i + 1) for i in range(count - 1)]
        return lax.ppermute(value, axis, pairs if up else [(b, a) for a, b in pairs])

    top = pass_on(jnp.stack([a[:, rows - SUB :, :] for a in three]), "gx", True)
    bottom = pass_on(jnp.stack([a[:, :SUB, :] for a in three]), "gx", False)

    steps = 4
    packed_rows = rows + 2 * SUB
    part = pl.BlockSpec((layers, rows // steps, cols), lambda i: (0, i, 0))
    packed, table = pl.pallas_call(
        pack_kernel,
        grid=(steps,),
        in_specs=[smem, smem, part, part, part],
        out_specs=[pl.BlockSpec((3, rows // steps, cols), lambda i: (0, i, 0)), smem],
        out_shape=[
            jax.ShapeDtypeStruct((3, packed_rows, cols), f32),
            jax.ShapeDtypeStruct((SUB,), jnp.int32),
        ],
        cost_estimate=pl.CostEstimate(
            flops=6 * rows * cols * layers, bytes_accessed=14 * rows * cols * layers, transcendentals=0
        ),
        name="pack_strips",
    )(pile_tile, me, *three)
    whole = pl.BlockSpec((3, layers, SUB, cols), lambda i: (0, 0, 0, 0))
    packed = pl.pallas_call(
        pack_edge_kernel,
        grid=(2,),
        in_specs=[whole, whole, anywhere],
        out_specs=pl.BlockSpec((3, SUB, cols), lambda i: (0, rows // SUB + i, 0)),
        out_shape=jax.ShapeDtypeStruct((3, packed_rows, cols), f32),
        input_output_aliases={2: 0},
        name="pack_edges",
    )(top, bottom, packed)
    left = pass_on(packed, "gy", True)
    right = pass_on(packed, "gy", False)

    padded = pltpu.VMEM((layers, rows + 4 * SUB, cols), f32)
    potential, sent = pl.pallas_call(
        sweep_kernel,
        in_specs=[smem, smem] + [anywhere] * 5 + [vmem, vmem],
        out_specs=[vmem, vmem],
        out_shape=[
            jax.ShapeDtypeStruct((layers, rows, cols), f32),
            jax.ShapeDtypeStruct((piles, SUB, LANES), f32),
        ],
        scratch_shapes=[padded] * 8
        + [pltpu.VMEM((8, rows + 4 * SUB, cols), f32), pltpu.SemaphoreType.DMA((3, 3))],
        compiler_params=pltpu.CompilerParams(vmem_limit_bytes=VMEM_LIMIT),
        name="sweeps",
    )(table, pile_block, *three, top, bottom, left, right)

    got = lax.all_to_all(sent, both, 0, 0, tiled=True)

    steps = 4
    part = pl.BlockSpec((1, depth_cells // steps, girth), lambda i: (0, i, 0))

    def full(*shape):
        return pl.BlockSpec(shape, lambda i: (0,) * len(shape))

    current, sent_back = pl.pallas_call(
        polarize_kernel,
        grid=(steps,),
        in_specs=[
            smem,
            smem,
            full(piles, SUB, LANES),
            pl.BlockSpec((depth_cells // steps, layers), lambda i: (i, 0)),
            full(BLK * BLK, girth),
            part,
        ],
        out_specs=[part, full(piles, SUB, LANES)],
        out_shape=[
            jax.ShapeDtypeStruct((1, depth_cells, girth), f32),
            jax.ShapeDtypeStruct((piles, SUB, LANES), f32),
        ],
        scratch_shapes=[
            pltpu.VMEM((layers, girth), f32),
            pltpu.VMEM((depth_cells // steps, girth), f32),
            pltpu.VMEM((layers, girth), f32),
        ],
        compiler_params=pltpu.CompilerParams(vmem_limit_bytes=32 << 20),
        name="polarize",
    )(pile_tile[me], pile_resistance, got, shell_to_depth, shell_to_girth, coating_mask)

    got_back = lax.all_to_all(sent_back, both, 0, 0, tiled=True)

    potential = pl.pallas_call(
        inject_kernel,
        in_specs=[smem, smem, vmem, anywhere],
        out_specs=anywhere,
        out_shape=jax.ShapeDtypeStruct((layers, rows, cols), f32),
        input_output_aliases={3: 0},
        scratch_shapes=[
            pltpu.VMEM((CAP, layers, SUB, LANES), f32),
            pltpu.SemaphoreType.DMA((2, CAP)),
        ],
        name="inject",
    )(table, pile_block, got_back, potential)
    return (potential, current)


def solution(mesh):
    placed = (
        P(None, "gx", "gy"),
        P(None, "gx", "gy"),
        P(None, "gx", "gy"),
        P(),
        P(),
        P(("gx", "gy")),
        P(("gx", "gy"), None, None),
        P(),
        P(),
    )
    return jax.shard_map(
        on_device,
        mesh=mesh,
        in_specs=placed,
        out_specs=(P(None, "gx", "gy"), P(("gx", "gy"), None, None)),
        check_vma=False,
    )
```

```python
import math

import jax
import jax.numpy as jnp
from jax import lax
from jax.experimental import pallas as pl
from jax.experimental.pallas import tpu as pltpu
from jax.sharding import PartitionSpec as P

BLK = 8
CAP = 4
SWEEPS = 4
NEWTON = 3
LANES = 128
SUB = 8
VMEM_LIMIT = 56 << 20
UNROLL = 2

vertical_ratio = 0.25
inject_gain = 0.5
anodic_slope = 1.2
cathodic_slope = 0.8
coated_conductance = 0.05


def turn(x, shift):
    return pltpu.roll(x, shift % LANES, 1)


def lane_ids(rows=SUB):
    return lax.broadcasted_iota(jnp.int32, (rows, LANES), 1)


WIDE = 32
FOLD = 4


def pack_rows(load, keep, send):
    lane = lane_ids()
    bands = []
    for m in range(FOLD):
        packed = turn(load(m), WIDE // 2)
        for g in range(1, LANES // WIDE):
            moved = turn(load(m + FOLD * g), WIDE * g + WIDE // 2)
            packed = jnp.where(lane // WIDE == g, moved, packed)
        keep(m, packed)
        bands.append(packed)
    part = ((lane + WIDE - 12) % WIDE) // BLK
    sent = bands[0]
    for m in range(1, FOLD):
        sent = jnp.where(part == m, turn(bands[m], BLK * m), sent)
    send(sent)


def pack_kernel(tile_ref, me_ref, p_ref, c_ref, s_ref, kept_ref, sent_ref, table_ref):
    rows = p_ref.shape[1]

    @pl.when(pl.program_id(0) == 0)
    def _():
        for j in range(CAP):
            table_ref[j] = -1

        def look(k, count):
            mine = tile_ref[k] == me_ref[0]

            @pl.when(mine & (count < CAP))
            def _():
                table_ref[count] = k

            return count + mine.astype(jnp.int32)

        lax.fori_loop(0, tile_ref.shape[0], look, jnp.int32(0))

    def body(t, carry):
        at = pl.ds(pl.multiple_of(t * SUB, SUB), SUB)
        for i, ref in enumerate((p_ref, c_ref, s_ref)):

            def keep(m, value, i=i):
                kept_ref[i, m, at, :] = value

            def send(value, i=i):
                sent_ref[i, at, :] = value

            pack_rows(lambda l, ref=ref: ref[l, at, :], keep, send)
        return carry

    lax.fori_loop(0, rows // SUB, body, 0)


def pack_edge_kernel(top_ref, bottom_ref, kept_hbm, sent_hbm, kept_ref, sent_ref):
    first = pl.program_id(0) == 0
    for i in range(3):

        def keep(m, value, i=i):
            kept_ref[i, m] = value

        def send(value, i=i):
            sent_ref[i] = value

        pack_rows(
            lambda l, i=i: jnp.where(first, top_ref[i, l], bottom_ref[i, l]), keep, send
        )


def sweep_kernel(
    table_ref,
    block_ref,
    p_hbm,
    c_hbm,
    s_hbm,
    top_hbm,
    bottom_hbm,
    kept_ref,
    left_ref,
    right_ref,
    out_ref,
    sent_ref,
    c_v,
    s_v,
    pa_v,
    pb_v,
    we_v,
    ws_v,
    wu_v,
    inv_v,
    sem,
):
    layers, tile_rows, _ = p_hbm.shape
    tiles = tile_rows // SUB
    first, last = 1, tiles + 2
    lane = lane_ids()
    place = lane % WIDE
    arrays = (pa_v, c_v, s_v)
    copies = []
    own = pl.ds(0, layers)
    for i, (src, dst) in enumerate(zip((p_hbm, c_hbm, s_hbm), arrays)):
        copies.append(
            pltpu.make_async_copy(src, dst.at[own, pl.ds(2 * SUB, tile_rows), :], sem.at[i, 0])
        )
        copies.append(
            pltpu.make_async_copy(top_hbm.at[i], dst.at[own, pl.ds(SUB, SUB), :], sem.at[i, 1])
        )
        copies.append(
            pltpu.make_async_copy(
                bottom_hbm.at[i], dst.at[own, pl.ds(last * SUB, SUB), :], sem.at[i, 2]
            )
        )
    for copy in copies:
        copy.start()
    zero = jnp.zeros((SUB, LANES), jnp.float32)
    for t in (0, last + 1):
        for ref in (c_v, pa_v, pb_v, ws_v):
            for l in range(layers + FOLD):
                ref[l, t * SUB : (t + 1) * SUB, :] = zero

    def at(t, shift=0):
        if shift:
            return pl.ds(t * SUB + shift, SUB)
        return pl.ds(pl.multiple_of(t * SUB, SUB), SUB)

    def join_windows(t, carry):
        src = jnp.where(t == first, tiles, jnp.where(t == last, tiles + 1, t - 2))
        src = pl.ds(pl.multiple_of(src * SUB, SUB), SUB)
        for i, dst in enumerate(arrays):
            left = left_ref[i, src, :]
            right = right_ref[i, src, :]
            for m in range(FOLD):
                kept = kept_ref[i, m, src, :]
                west = turn(left, BLK - BLK * m) if m != 1 else left
                east = turn(right, -BLK * m) if m else right
                inner = turn(kept, BLK)
                value = jnp.where(place < 20, east, west)
                value = jnp.where((place >= 4) & (place < 16), kept, value)
                value = jnp.where((place >= 24) | (place < 4), inner, value)
                dst[layers + m, at(t), :] = value
        return carry

    lax.fori_loop(first, last + 1, join_windows, 0)
    for copy in copies:
        copy.wait()

    def prepare(t, carry):
        def faces(n, here, above):
            we = 0.5 * (here + turn(here, -1))
            ws = 0.5 * (here + c_v[n, at(t, 1), :])
            wn = 0.5 * (here + c_v[n, at(t, -1), :])
            we_v[n, at(t), :] = we
            ws_v[n, at(t), :] = ws
            weight = we + turn(we, 1) + ws + wn
            if above is None:
                return weight, None
            wu = (0.5 * vertical_ratio) * (here + above)
            wu_v[n, at(t), :] = wu
            return weight + wu, wu

        def finish(n, here, weight):
            inside = here > 0.0
            inv_v[n, at(t), :] = jnp.where(inside, 1.0 / jnp.where(inside, weight, 1.0), 0.0)

        here = c_v[0, at(t), :]
        below = None
        for l in range(layers):
            above = c_v[l + 1, at(t), :] if l + 1 < layers else None
            weight, wu = faces(l, here, above)
            finish(l, here, weight if below is None else weight + below)
            here, below = above, wu
        bands = [c_v[layers + m, at(t), :] for m in range(FOLD)]
        weights = []
        for m in range(FOLD - 1):
            weights.append(faces(layers + m, bands[m], bands[m + 1]))
        weight, _ = faces(layers + FOLD - 1, bands[-1], None)
        wu = (0.5 * vertical_ratio) * (bands[-1] + turn(bands[0], -WIDE))
        wu = jnp.where(topmost, 0.0, wu)
        wu_v[layers + FOLD - 1, at(t), :] = wu
        weights.append((weight + wu, wu))
        below = jnp.where(bottommost, 0.0, turn(wu, WIDE))
        for m in range(FOLD):
            finish(layers + m, bands[m], weights[m][0] + below)
            below = weights[m][1]
        return carry

    group = ((lane + LANES - 4) % LANES) // WIDE
    topmost = group == LANES // WIDE - 1
    bottommost = group == 0
    lax.fori_loop(first, last + 1, prepare, 0, unroll=UNROLL)

    def make_sweep(old, store):
        def flat(n, t, here):
            we = we_v[n, at(t), :]
            total = s_v[n, at(t), :] + we * turn(here, -1) + turn(we * here, 1)
            total = total + ws_v[n, at(t), :] * old[n, at(t, 1), :]
            return total + ws_v[n, at(t, -1), :] * old[n, at(t, -1), :]

        def sweep(t, carry):
            values = []
            bands = [old[layers + m, at(t), :] for m in range(FOLD)]
            wus = [wu_v[layers + m, at(t), :] for m in range(FOLD)]
            ups = bands[1:] + [turn(bands[0], -WIDE)]
            downs = [turn(wus[-1] * bands[-1], WIDE)]
            downs += [wus[m] * bands[m] for m in range(FOLD - 1)]
            for m in range(FOLD):
                total = flat(layers + m, t, bands[m]) + wus[m] * ups[m] + downs[m]
                values.append(total * inv_v[layers + m, at(t), :])
            extra = store.windows(t, values)
            below = None
            here = old[0, at(t), :]
            for l in range(layers):
                total = flat(l, t, here)
                if l:
                    total = total + below
                if l + 1 < layers:
                    above = old[l + 1, at(t), :]
                    wu = wu_v[l, at(t), :]
                    total = total + wu * above
                    below, here = wu * here, above
                store.layer(l, t, total * inv_v[l, at(t), :], extra)
            return carry

        return sweep

    class Keep:
        def __init__(self, new):
            self.new = new

        def windows(self, t, values):
            for m in range(FOLD):
                self.new[layers + m, at(t), :] = values[m]

        def layer(self, l, t, value, extra):
            self.new[l, at(t), :] = value

    class Finish:
        def windows(self, t, values):
            return [jnp.where(place < 16, value, turn(value, -BLK)) for value in values]

        def layer(self, l, t, value, extra):
            outer = turn(extra[l % FOLD], LANES - WIDE // 2 - WIDE * (l // FOLD))
            value = jnp.where((lane >= 4) & (lane < LANES - 4), value, outer)
            out_ref[l, pl.ds(pl.multiple_of(t * SUB - 2 * SUB, SUB), SUB), :] = value

    pairs = (pa_v, pb_v)
    for k in range(SWEEPS - 1):
        lax.fori_loop(
            first, last + 1, make_sweep(pairs[k % 2], Keep(pairs[(k + 1) % 2])), 0, unroll=UNROLL
        )
    lax.fori_loop(
        first + 1, last, make_sweep(pairs[(SWEEPS - 1) % 2], Finish()), 0, unroll=UNROLL
    )

    sent_ref[...] = jnp.zeros_like(sent_ref)
    for j in range(CAP):
        k = table_ref[j]

        @pl.when(k >= 0)
        def _():
            block = block_ref[k]
            per_row = LANES // BLK
            rows = pl.ds(pl.multiple_of(block // per_row * BLK, BLK), BLK)
            start = block % per_row * BLK
            packet = zero
            for l in range(layers):
                group = layers - 1 - l
                moved = pltpu.roll(out_ref[l, rows, :], (BLK * group + LANES - start) % LANES, 1)
                packet = jnp.where(lane // BLK == group, moved, packet)
            sent_ref[k] = packet


def polarize_kernel(
    source_ref, resist_ref, got_ref, depth_ref, girth_ref, bare_ref, current_ref, sent_ref, near_v, drive_v, sum_v
):
    layers = depth_ref.shape[1]
    rows, girth = bare_ref.shape[1:]
    step = pl.program_id(0)
    highest = lax.Precision.HIGHEST
    resist = resist_ref[0]
    lane = lane_ids(layers)
    row = lax.broadcasted_iota(jnp.int32, (layers, LANES), 0)

    @pl.when(step == 0)
    def _():
        packet = got_ref[source_ref[0]]
        shell = jnp.zeros((layers, LANES), jnp.float32)
        for x in range(BLK):
            spread = jnp.broadcast_to(packet[x : x + 1, :], (layers, LANES))
            spread = pltpu.roll(spread, 0, 1, stride=BLK, stride_axis=0)
            spread = turn(spread, BLK * (x + 1) - BLK * layers)
            shell = jnp.where(lane // BLK == x, spread, shell)
        near_v[...] = jnp.dot(
            shell[:, : BLK * BLK],
            girth_ref[...],
            precision=highest,
            preferred_element_type=jnp.float32,
        )
        sum_v[...] = jnp.zeros_like(sum_v)

    drive_v[...] = jnp.dot(
        depth_ref[...], near_v[...], precision=highest, preferred_element_type=jnp.float32
    )
    up = math.log2(math.e) / anodic_slope
    down = -math.log2(math.e) / cathodic_slope
    steep = resist / anodic_slope
    steep_down = resist / cathodic_slope
    coated = coated_conductance / (1.0 + coated_conductance * resist)
    chunk = 16

    def body(i, carry):
        at = pl.ds(pl.multiple_of(i * chunk, chunk), chunk)
        driving = drive_v[at, :]
        value = driving
        for n in range(NEWTON):
            anodic = jnp.exp2(value * up)
            cathodic = jnp.exp2(value * down)
            excess = resist * (anodic - cathodic)
            if n:
                excess = excess + (value - driving)
            slope = 1.0 + (steep * anodic + steep_down * cathodic)
            value = value - excess / slope
        bare_current = jnp.exp2(value * up) - jnp.exp2(value * down)
        current_ref[0, at, :] = jnp.where(bare_ref[0, at, :] != 0, bare_current, coated * driving)
        return carry

    lax.fori_loop(0, rows // chunk, body, 0)
    sum_v[...] += lax.dot_general(
        depth_ref[...],
        current_ref[0],
        (((0,), (0,)), ((), ())),
        precision=highest,
        preferred_element_type=jnp.float32,
    )

    @pl.when(step == pl.num_programs(0) - 1)
    def _():
        cells = layers * BLK * BLK
        scale = math.sqrt(cells / (rows * girth * pl.num_programs(0)))
        back = scale * lax.dot_general(
            sum_v[...],
            girth_ref[...],
            (((1,), (1,)), ((), ())),
            precision=highest,
            preferred_element_type=jnp.float32,
        )
        back = jnp.concatenate([back, jnp.zeros_like(back)], axis=1)
        lines = []
        for x in range(BLK):
            spread = turn(back, -BLK * x) if x else back
            spread = pltpu.roll(spread, 0, 1, stride=BLK, stride_axis=0)
            spread = jnp.where(lane // BLK == row, spread, 0.0)
            lines.append(jnp.sum(spread, axis=0, keepdims=True))
        sent_ref[...] = jnp.broadcast_to(jnp.concatenate(lines, axis=0)[None], sent_ref.shape)


def inject_kernel(table_ref, block_ref, got_ref, p_hbm, out_hbm, work_v, sem):
    layers = p_hbm.shape[0]
    per_row = LANES // BLK
    lane = lane_ids()
    piles = [table_ref[j] for j in range(CAP)]
    blocks = [block_ref[jnp.maximum(k, 0)] for k in piles]
    def window(ref, j):
        return ref.at[:, pl.ds(pl.multiple_of(blocks[j] // per_row * BLK, BLK), BLK), :]

    heads = []
    for j in range(CAP):
        head = piles[j] >= 0
        for i in range(j):
            head = head & jnp.logical_not(
                (piles[i] >= 0) & (blocks[i] // per_row == blocks[j] // per_row)
            )
        heads.append(head)
    for j in range(CAP):

        @pl.when(heads[j])
        def _():
            pltpu.make_async_copy(window(p_hbm, j), work_v.at[j], sem.at[0, j]).start()

    for j in range(CAP):

        @pl.when(heads[j])
        def _():
            pltpu.make_async_copy(window(p_hbm, j), work_v.at[j], sem.at[0, j]).wait()
            for i in range(j, CAP):

                @pl.when((piles[i] >= 0) & (blocks[i] // per_row == blocks[j] // per_row))
                def _():
                    start = blocks[i] % per_row * BLK
                    packet = inject_gain * got_ref[jnp.maximum(piles[i], 0)]
                    for l in range(layers):
                        moved = pltpu.roll(packet, (start + LANES - BLK * l) % LANES, 1)
                        inside = (lane >= start) & (lane < start + BLK)
                        work_v[j, l] = work_v[j, l] - jnp.where(inside, moved, 0.0)

            pltpu.make_async_copy(work_v.at[j], window(out_hbm, j), sem.at[1, j]).start()

    for j in range(CAP):

        @pl.when(heads[j])
        def _():
            pltpu.make_async_copy(work_v.at[j], window(out_hbm, j), sem.at[1, j]).wait()


def on_device(
    conductivity,
    source,
    potential_start,
    shell_to_depth,
    shell_to_girth,
    pile_resistance,
    coating_mask,
    pile_tile,
    pile_block,
):
    layers, rows, cols = conductivity.shape
    piles = pile_tile.shape[0]
    depth_cells, girth = coating_mask.shape[1:]
    both = ("gx", "gy")
    me = (lax.axis_index("gx") * lax.axis_size("gy") + lax.axis_index("gy")).astype(jnp.int32)
    me = me.reshape(1)
    smem = pl.BlockSpec(memory_space=pltpu.SMEM)
    vmem = pl.BlockSpec(memory_space=pltpu.VMEM)
    anywhere = pl.BlockSpec(memory_space=pl.ANY)
    f32 = jnp.float32
    three = (potential_start, conductivity, source)

    def pass_on(value, axis, up):
        count = lax.axis_size(axis)
        pairs = [(i, i + 1) for i in range(count - 1)]
        return lax.ppermute(value, axis, pairs if up else [(b, a) for a, b in pairs])

    top = pass_on(jnp.stack([a[:, rows - SUB :, :] for a in three]), "gx", True)
    bottom = pass_on(jnp.stack([a[:, :SUB, :] for a in three]), "gx", False)

    steps = 4
    packed_rows = rows + 2 * SUB
    part = pl.BlockSpec((layers, rows // steps, cols), lambda i: (0, i, 0))
    kept_shape = jax.ShapeDtypeStruct((3, FOLD, packed_rows, cols), f32)
    sent_shape = jax.ShapeDtypeStruct((3, packed_rows, cols), f32)
    kept, packed, table = pl.pallas_call(
        pack_kernel,
        grid=(steps,),
        in_specs=[smem, smem, part, part, part],
        out_specs=[
            pl.BlockSpec((3, FOLD, rows // steps, cols), lambda i: (0, 0, i, 0)),
            pl.BlockSpec((3, rows // steps, cols), lambda i: (0, i, 0)),
            smem,
        ],
        out_shape=[kept_shape, sent_shape, jax.ShapeDtypeStruct((SUB,), jnp.int32)],
        cost_estimate=pl.CostEstimate(
            flops=6 * rows * cols * layers, bytes_accessed=16 * rows * cols * layers, transcendentals=0
        ),
        name="pack_strips",
    )(pile_tile, me, *three)
    whole = pl.BlockSpec((3, layers, SUB, cols), lambda i: (0, 0, 0, 0))
    kept, packed = pl.pallas_call(
        pack_edge_kernel,
        grid=(2,),
        in_specs=[whole, whole, anywhere, anywhere],
        out_specs=[
            pl.BlockSpec((3, FOLD, SUB, cols), lambda i: (0, 0, rows // SUB + i, 0)),
            pl.BlockSpec((3, SUB, cols), lambda i: (0, rows // SUB + i, 0)),
        ],
        out_shape=[kept_shape, sent_shape],
        input_output_aliases={2: 0, 3: 1},
        name="pack_edges",
    )(top, bottom, kept, packed)
    left = pass_on(packed, "gy", True)
    right = pass_on(packed, "gy", False)

    padded = pltpu.VMEM((layers + FOLD, rows + 5 * SUB, cols), f32)
    potential, sent = pl.pallas_call(
        sweep_kernel,
        in_specs=[smem, smem] + [anywhere] * 5 + [vmem] * 3,
        out_specs=[vmem, vmem],
        out_shape=[
            jax.ShapeDtypeStruct((layers, rows, cols), f32),
            jax.ShapeDtypeStruct((piles, SUB, LANES), f32),
        ],
        scratch_shapes=[padded] * 8 + [pltpu.SemaphoreType.DMA((3, 3))],
        compiler_params=pltpu.CompilerParams(vmem_limit_bytes=VMEM_LIMIT),
        name="sweeps",
    )(table, pile_block, *three, top, bottom, kept, left, right)

    got = lax.all_to_all(sent, both, 0, 0, tiled=True)

    steps = 4
    part = pl.BlockSpec((1, depth_cells // steps, girth), lambda i: (0, i, 0))

    def full(*shape):
        return pl.BlockSpec(shape, lambda i: (0,) * len(shape))

    current, sent_back = pl.pallas_call(
        polarize_kernel,
        grid=(steps,),
        in_specs=[
            smem,
            smem,
            full(piles, SUB, LANES),
            pl.BlockSpec((depth_cells // steps, layers), lambda i: (i, 0)),
            full(BLK * BLK, girth),
            part,
        ],
        out_specs=[part, full(piles, SUB, LANES)],
        out_shape=[
            jax.ShapeDtypeStruct((1, depth_cells, girth), f32),
            jax.ShapeDtypeStruct((piles, SUB, LANES), f32),
        ],
        scratch_shapes=[
            pltpu.VMEM((layers, girth), f32),
            pltpu.VMEM((depth_cells // steps, girth), f32),
            pltpu.VMEM((layers, girth), f32),
        ],
        compiler_params=pltpu.CompilerParams(vmem_limit_bytes=32 << 20),
        name="polarize",
    )(pile_tile[me], pile_resistance, got, shell_to_depth, shell_to_girth, coating_mask)

    got_back = lax.all_to_all(sent_back, both, 0, 0, tiled=True)

    potential = pl.pallas_call(
        inject_kernel,
        in_specs=[smem, smem, vmem, anywhere],
        out_specs=anywhere,
        out_shape=jax.ShapeDtypeStruct((layers, rows, cols), f32),
        input_output_aliases={3: 0},
        scratch_shapes=[
            pltpu.VMEM((CAP, layers, SUB, LANES), f32),
            pltpu.SemaphoreType.DMA((2, CAP)),
        ],
        name="inject",
    )(table, pile_block, got_back, potential)
    return (potential, current)


def solution(mesh):
    placed = (
        P(None, "gx", "gy"),
        P(None, "gx", "gy"),
        P(None, "gx", "gy"),
        P(),
        P(),
        P(("gx", "gy")),
        P(("gx", "gy"), None, None),
        P(),
        P(),
    )
    return jax.shard_map(
        on_device,
        mesh=mesh,
        in_specs=placed,
        out_specs=(P(None, "gx", "gy"), P(("gx", "gy"), None, None)),
        check_vma=False,
    )
```

```python
import functools
import math

import jax
import jax.numpy as jnp
from jax import lax
from jax.experimental import pallas as pl
from jax.experimental.pallas import tpu as pltpu
from jax.sharding import PartitionSpec as P

BLK = 8
CAP = 4
SWEEPS = 4
NEWTON = 3
LANES = 128
SUB = 8
VMEM_LIMIT = 56 << 20
UNROLL = 2

vertical_ratio = 0.25
inject_gain = 0.5
anodic_slope = 1.2
cathodic_slope = 0.8
coated_conductance = 0.05


def turn(x, shift):
    return pltpu.roll(x, shift % LANES, 1)


def lane_ids(rows=SUB):
    return lax.broadcasted_iota(jnp.int32, (rows, LANES), 1)


WIDE = 32
FOLD = 4


def pack_rows(load, keep, send):
    lane = lane_ids()
    bands = []
    for m in range(FOLD):
        packed = turn(load(m), WIDE // 2)
        for g in range(1, LANES // WIDE):
            moved = turn(load(m + FOLD * g), WIDE * g + WIDE // 2)
            packed = jnp.where(lane // WIDE == g, moved, packed)
        keep(m, packed)
        bands.append(packed)
    part = ((lane + WIDE - 12) % WIDE) // BLK
    sent = bands[0]
    for m in range(1, FOLD):
        sent = jnp.where(part == m, turn(bands[m], BLK * m), sent)
    send(sent)


def pack_kernel(tile_ref, me_ref, p_ref, c_ref, s_ref, kept_ref, sent_ref, table_ref):
    rows = p_ref.shape[1]

    @pl.when(pl.program_id(0) == 0)
    def _():
        for j in range(CAP):
            table_ref[j] = -1

        def look(k, count):
            mine = tile_ref[k] == me_ref[0]

            @pl.when(mine & (count < CAP))
            def _():
                table_ref[count] = k

            return count + mine.astype(jnp.int32)

        lax.fori_loop(0, tile_ref.shape[0], look, jnp.int32(0))

    def body(t, carry):
        at = pl.ds(pl.multiple_of(t * SUB, SUB), SUB)
        for i, ref in enumerate((p_ref, c_ref, s_ref)):

            def keep(m, value, i=i):
                kept_ref[i, m, at, :] = value

            def send(value, i=i):
                sent_ref[i, at, :] = value

            pack_rows(lambda l, ref=ref: ref[l, at, :], keep, send)
        return carry

    lax.fori_loop(0, rows // SUB, body, 0, unroll=UNROLL)


def pack_edge_kernel(top_ref, bottom_ref, kept_hbm, sent_hbm, kept_ref, sent_ref):
    first = pl.program_id(0) == 0
    for i in range(3):

        def keep(m, value, i=i):
            kept_ref[i, m] = value

        def send(value, i=i):
            sent_ref[i] = value

        pack_rows(
            lambda l, i=i: jnp.where(first, top_ref[i, l], bottom_ref[i, l]), keep, send
        )


NEAR = 16
HALF = LANES // 2


def shells_kernel(
    table_ref,
    block_ref,
    p_hbm,
    c_hbm,
    s_hbm,
    top_hbm,
    bottom_hbm,
    left_hbm,
    right_hbm,
    sent_ref,
    tile_v,
    side_v,
    work_v,
    sem,
):
    layers, rows, _ = p_hbm.shape
    folds = layers // 2
    per_row = LANES // BLK
    lane = lane_ids()
    sources = (p_hbm, c_hbm, s_hbm)
    piles = [table_ref[j] for j in range(CAP)]
    filled = [k >= 0 for k in piles]
    blocks = [block_ref[jnp.maximum(k, 0)] for k in piles]
    row_of = [lax.div(b, per_row) for b in blocks]
    col_of = [lax.rem(b, per_row) for b in blocks]
    border = [
        filled[j] & ((col_of[j] == 0) | (col_of[j] == per_row - 1)) for j in range(CAP)
    ]

    def main_copy(i, j, d):
        where = pl.ds(pl.multiple_of((row_of[j] + d - 1) * SUB, SUB), SUB)
        return pltpu.make_async_copy(
            sources[i].at[:, where, :], tile_v.at[j, i, d], sem.at[j, i, d]
        )

    def edge_copy(i, j, d):
        ref = top_hbm if d == 0 else bottom_hbm
        return pltpu.make_async_copy(ref.at[i], tile_v.at[j, i, d], sem.at[j, i, d])

    def side_copy(ref, j, d):
        tile = row_of[j] + d - 1
        tile = jnp.where(tile < 0, rows // SUB, jnp.where(tile >= rows // SUB, rows // SUB + 1, tile))
        where = pl.ds(pl.multiple_of(tile * SUB, SUB), SUB)
        return pltpu.make_async_copy(ref.at[:, where, :], side_v.at[j, d], sem.at[j, 3, d])

    def each_copy(j, act):
        @pl.when(filled[j])
        def _():
            for d in range(3):
                for i in range(3):
                    if d == 1:
                        act(main_copy(i, j, d))
                        continue
                    outside = row_of[j] == (0 if d == 0 else rows // SUB - 1)

                    @pl.when(outside)
                    def _():
                        act(edge_copy(i, j, d))

                    @pl.when(jnp.logical_not(outside))
                    def _():
                        act(main_copy(i, j, d))

        @pl.when(border[j] & (col_of[j] == 0))
        def _():
            for d in range(3):
                act(side_copy(left_hbm, j, d))

        @pl.when(border[j] & (col_of[j] > 0))
        def _():
            for d in range(3):
                act(side_copy(right_hbm, j, d))

    for j in range(CAP):
        each_copy(j, lambda copy: copy.start())
    sent_ref[...] = jnp.zeros_like(sent_ref)
    pa, c_v, s_v, pb, we_v, ws_v, wu_v, inv_v = (work_v.at[i] for i in range(8))
    zero = jnp.zeros((SUB, LANES), jnp.float32)
    for t in (0, 4):
        for ref in (pa, c_v, pb, ws_v):
            for m in range(folds):
                ref[m, t * SUB : (t + 1) * SUB, :] = zero
    for j in range(CAP):
        each_copy(j, lambda copy: copy.wait())

    slot = (lane % HALF) // NEAR
    upper = lane >= HALF
    shifts = [[(HALF * h + NEAR * j + 4 + LANES - BLK * col_of[j]) % LANES for h in (0, 1)] for j in range(CAP)]
    arrays = (pa, c_v, s_v)

    def gather(d, carry):
        at = pl.ds(pl.multiple_of((d + 1) * SUB, SUB), SUB)
        for i in range(3):
            for m in range(folds):
                value = zero
                for j in range(CAP):
                    low = pltpu.roll(tile_v[j, i, d, m], shifts[j][0], 1)
                    high = pltpu.roll(tile_v[j, i, d, m + folds], shifts[j][1], 1)
                    value = jnp.where(
                        (slot == j) & filled[j], jnp.where(upper, high, low), value
                    )
                arrays[i][m, at, :] = value
        return carry

    lax.fori_loop(0, 3, gather, 0)
    for j in range(CAP):

        @pl.when(border[j])
        def _():
            first = col_of[j] == 0
            begin = jnp.where(first, 0, NEAR - 4)
            back = jnp.where(first, 12, 4)

            def mend(d, carry):
                at = pl.ds(pl.multiple_of((d + 1) * SUB, SUB), SUB)
                for i in range(3):
                    side = side_v[j, d, i]
                    for m in range(folds):
                        value = arrays[i][m, at, :]
                        for h in (0, 1):
                            l = m + folds * h
                            base = HALF * h + NEAR * j
                            known = base - WIDE * (l // FOLD) - BLK * (l % FOLD)
                            moved = pltpu.roll(side, (known + 2 * LANES - back) % LANES, 1)
                            here = (lane >= base + begin) & (lane < base + begin + 4)
                            value = jnp.where(here, moved, value)
                        arrays[i][m, at, :] = value
                return carry

            lax.fori_loop(0, 3, mend, 0)

    def span(t, shift=0):
        return slice(t * SUB + shift, (t + 1) * SUB + shift)

    for t in (1, 2, 3):
        cells = [c_v[m, span(t), :] for m in range(folds)]
        weights, wus = [], []
        for m in range(folds):
            here = cells[m]
            we = 0.5 * (here + turn(here, -1))
            ws = 0.5 * (here + c_v[m, span(t, 1), :])
            wn = 0.5 * (here + c_v[m, span(t, -1), :])
            above = cells[m + 1] if m + 1 < folds else turn(cells[0], HALF)
            wu = (0.5 * vertical_ratio) * (here + above)
            if m + 1 == folds:
                wu = jnp.where(upper, 0.0, wu)
            we_v[m, span(t), :] = we
            ws_v[m, span(t), :] = ws
            wu_v[m, span(t), :] = wu
            weights.append(we + turn(we, 1) + ws + wn + wu)
            wus.append(wu)
        for m in range(folds):
            below = wus[m - 1] if m else turn(wus[-1], HALF)
            inside = cells[m] > 0.0
            weight = jnp.where(inside, weights[m] + below, 1.0)
            inv_v[m, span(t), :] = jnp.where(inside, 1.0 / weight, 0.0)

    def sweep(old, new, t):
        values = [old[m, span(t), :] for m in range(folds)]
        wus = [wu_v[m, span(t), :] for m in range(folds)]
        for m in range(folds):
            here = values[m]
            we = we_v[m, span(t), :]
            total = s_v[m, span(t), :] + we * turn(here, -1) + turn(we * here, 1)
            total = total + ws_v[m, span(t), :] * old[m, span(t, 1), :]
            total = total + ws_v[m, span(t, -1), :] * old[m, span(t, -1), :]
            above = values[m + 1] if m + 1 < folds else turn(values[0], HALF)
            below = wus[m - 1] * values[m - 1] if m else turn(wus[-1] * values[-1], HALF)
            total = total + wus[m] * above + below
            new[m, span(t), :] = total * inv_v[m, span(t), :]

    pairs = (pa, pb)
    for k in range(SWEEPS):
        for t in (1, 2, 3) if k < SWEEPS - 1 else (2,):
            sweep(pairs[k % 2], pairs[(k + 1) % 2], t)
    done = pairs[SWEEPS % 2]
    for j in range(CAP):

        @pl.when(filled[j])
        def _():
            packet = zero
            for l in range(layers):
                group = layers - 1 - l
                begin = HALF * (l // folds) + NEAR * j + 4
                moved = turn(done[l % folds, span(2), :], BLK * group - begin)
                packet = jnp.where(lane // BLK == group, moved, packet)
            sent_ref[piles[j]] = packet


def sweep_kernel(
    half,
    p_hbm,
    c_hbm,
    s_hbm,
    edge_hbm,
    kept_ref,
    kept_edge_ref,
    kept_inner_ref,
    left_ref,
    left_edge_ref,
    left_inner_ref,
    right_ref,
    right_edge_ref,
    right_inner_ref,
    *rest,
):
    out_ref, c_v, s_v, pa_v, pb_v, we_v, ws_v, wu_v, inv_v, sem = rest[-10:]
    layers = p_hbm.shape[0]
    tile_rows = out_ref.shape[1]
    tiles = tile_rows // SUB
    first, last = 1, tiles + 2
    edge = last if half else first
    lane = lane_ids()
    place = lane % WIDE
    arrays = (pa_v, c_v, s_v)
    copies = []
    own = pl.ds(0, layers)
    for i, (src, dst) in enumerate(zip((p_hbm, c_hbm, s_hbm), arrays)):
        begin = half * (tile_rows - SUB)
        into = SUB if half else 2 * SUB
        copies.append(
            pltpu.make_async_copy(
                src.at[:, pl.ds(begin, tile_rows + SUB), :],
                dst.at[own, pl.ds(into, tile_rows + SUB), :],
                sem.at[i, 0],
            )
        )
        copies.append(
            pltpu.make_async_copy(
                edge_hbm.at[i], dst.at[own, pl.ds(edge * SUB, SUB), :], sem.at[i, 1]
            )
        )
    for copy in copies:
        copy.start()
    zero = jnp.zeros((SUB, LANES), jnp.float32)
    for t in (0, last + 1):
        for ref in (c_v, pa_v, pb_v, ws_v):
            for l in range(layers + FOLD):
                ref[l, t * SUB : (t + 1) * SUB, :] = zero

    def at(t, shift=0):
        if shift:
            return pl.ds(t * SUB + shift, SUB)
        return pl.ds(pl.multiple_of(t * SUB, SUB), SUB)

    def join_windows(t, src, kept_rows, left_rows, right_rows):
        for i, dst in enumerate(arrays):
            left = left_rows[i, src, :]
            right = right_rows[i, src, :]
            for m in range(FOLD):
                kept = kept_rows[i, m, src, :]
                west = turn(left, BLK - BLK * m) if m != 1 else left
                east = turn(right, -BLK * m) if m else right
                inner = turn(kept, BLK)
                value = jnp.where(place < 20, east, west)
                value = jnp.where((place >= 4) & (place < 16), kept, value)
                value = jnp.where((place >= 24) | (place < 4), inner, value)
                dst[layers + m, at(t), :] = value

    def join_own(t, carry):
        src = pl.ds(pl.multiple_of(t * SUB - 2 * SUB, SUB), SUB)
        join_windows(t, src, kept_ref, left_ref, right_ref)
        return carry

    lax.fori_loop(first + 1, last, join_own, 0)
    every = slice(None)
    join_windows(edge, every, kept_edge_ref, left_edge_ref, right_edge_ref)
    join_windows(first + last - edge, every, kept_inner_ref, left_inner_ref, right_inner_ref)
    for copy in copies:
        copy.wait()

    def prepare(t, carry):
        def faces(n, here, above):
            we = 0.5 * (here + turn(here, -1))
            ws = 0.5 * (here + c_v[n, at(t, 1), :])
            wn = 0.5 * (here + c_v[n, at(t, -1), :])
            we_v[n, at(t), :] = we
            ws_v[n, at(t), :] = ws
            weight = we + turn(we, 1) + ws + wn
            if above is None:
                return weight, None
            wu = (0.5 * vertical_ratio) * (here + above)
            wu_v[n, at(t), :] = wu
            return weight + wu, wu

        def finish(n, here, weight):
            inside = here > 0.0
            inv_v[n, at(t), :] = jnp.where(inside, 1.0 / jnp.where(inside, weight, 1.0), 0.0)

        here = c_v[0, at(t), :]
        below = None
        for l in range(layers):
            above = c_v[l + 1, at(t), :] if l + 1 < layers else None
            weight, wu = faces(l, here, above)
            finish(l, here, weight if below is None else weight + below)
            here, below = above, wu
        bands = [c_v[layers + m, at(t), :] for m in range(FOLD)]
        weights = []
        for m in range(FOLD - 1):
            weights.append(faces(layers + m, bands[m], bands[m + 1]))
        weight, _ = faces(layers + FOLD - 1, bands[-1], None)
        wu = (0.5 * vertical_ratio) * (bands[-1] + turn(bands[0], -WIDE))
        wu = jnp.where(topmost, 0.0, wu)
        wu_v[layers + FOLD - 1, at(t), :] = wu
        weights.append((weight + wu, wu))
        below = jnp.where(bottommost, 0.0, turn(wu, WIDE))
        for m in range(FOLD):
            finish(layers + m, bands[m], weights[m][0] + below)
            below = weights[m][1]
        return carry

    group = ((lane + LANES - 4) % LANES) // WIDE
    topmost = group == LANES // WIDE - 1
    bottommost = group == 0
    lax.fori_loop(first, last + 1, prepare, 0, unroll=UNROLL)

    def make_sweep(old, store):
        def flat(n, t, here):
            we = we_v[n, at(t), :]
            total = s_v[n, at(t), :] + we * turn(here, -1) + turn(we * here, 1)
            total = total + ws_v[n, at(t), :] * old[n, at(t, 1), :]
            return total + ws_v[n, at(t, -1), :] * old[n, at(t, -1), :]

        def sweep(t, carry):
            values = []
            bands = [old[layers + m, at(t), :] for m in range(FOLD)]
            wus = [wu_v[layers + m, at(t), :] for m in range(FOLD)]
            ups = bands[1:] + [turn(bands[0], -WIDE)]
            downs = [turn(wus[-1] * bands[-1], WIDE)]
            downs += [wus[m] * bands[m] for m in range(FOLD - 1)]
            for m in range(FOLD):
                total = flat(layers + m, t, bands[m]) + wus[m] * ups[m] + downs[m]
                values.append(total * inv_v[layers + m, at(t), :])
            extra = store.windows(t, values)
            below = None
            here = old[0, at(t), :]
            for l in range(layers):
                total = flat(l, t, here)
                if l:
                    total = total + below
                if l + 1 < layers:
                    above = old[l + 1, at(t), :]
                    wu = wu_v[l, at(t), :]
                    total = total + wu * above
                    below, here = wu * here, above
                store.layer(l, t, total * inv_v[l, at(t), :], extra)
            return carry

        return sweep

    class Keep:
        def __init__(self, new):
            self.new = new

        def windows(self, t, values):
            for m in range(FOLD):
                self.new[layers + m, at(t), :] = values[m]

        def layer(self, l, t, value, extra):
            self.new[l, at(t), :] = value

    class Finish:
        def windows(self, t, values):
            return [jnp.where(place < 16, value, turn(value, -BLK)) for value in values]

        def layer(self, l, t, value, extra):
            outer = turn(extra[l % FOLD], LANES - WIDE // 2 - WIDE * (l // FOLD))
            value = jnp.where((lane >= 4) & (lane < LANES - 4), value, outer)
            out_ref[l, pl.ds(pl.multiple_of(t * SUB - 2 * SUB, SUB), SUB), :] = value

    pairs = (pa_v, pb_v)
    for k in range(SWEEPS - 1):
        lax.fori_loop(
            first, last + 1, make_sweep(pairs[k % 2], Keep(pairs[(k + 1) % 2])), 0, unroll=UNROLL
        )
    lax.fori_loop(
        first + 1, last, make_sweep(pairs[(SWEEPS - 1) % 2], Finish()), 0, unroll=UNROLL
    )


def polarize_kernel(
    source_ref, resist_ref, got_ref, depth_ref, girth_ref, bare_ref, current_ref, sent_ref, near_v, drive_v, sum_v
):
    layers = depth_ref.shape[1]
    rows, girth = bare_ref.shape[1:]
    step = pl.program_id(0)
    highest = lax.Precision.HIGHEST
    resist = resist_ref[0]
    lane = lane_ids(layers)
    row = lax.broadcasted_iota(jnp.int32, (layers, LANES), 0)

    @pl.when(step == 0)
    def _():
        packet = got_ref[source_ref[0]]
        shell = jnp.zeros((layers, LANES), jnp.float32)
        for x in range(BLK):
            spread = jnp.broadcast_to(packet[x : x + 1, :], (layers, LANES))
            spread = pltpu.roll(spread, 0, 1, stride=BLK, stride_axis=0)
            spread = turn(spread, BLK * (x + 1) - BLK * layers)
            shell = jnp.where(lane // BLK == x, spread, shell)
        near_v[...] = jnp.dot(
            shell[:, : BLK * BLK],
            girth_ref[...],
            precision=highest,
            preferred_element_type=jnp.float32,
        )
        sum_v[...] = jnp.zeros_like(sum_v)

    drive_v[...] = jnp.dot(
        depth_ref[...], near_v[...], precision=highest, preferred_element_type=jnp.float32
    )
    up = math.log2(math.e) / anodic_slope
    down = -math.log2(math.e) / cathodic_slope
    steep = resist / anodic_slope
    steep_down = resist / cathodic_slope
    coated = coated_conductance / (1.0 + coated_conductance * resist)
    chunk = 16

    def body(i, carry):
        at = pl.ds(pl.multiple_of(i * chunk, chunk), chunk)
        driving = drive_v[at, :]
        value = driving
        for n in range(NEWTON):
            anodic = jnp.exp2(value * up)
            cathodic = jnp.exp2(value * down)
            excess = resist * (anodic - cathodic)
            if n:
                excess = excess + (value - driving)
            slope = 1.0 + (steep * anodic + steep_down * cathodic)
            value = value - excess / slope
        bare_current = jnp.exp2(value * up) - jnp.exp2(value * down)
        current_ref[0, at, :] = jnp.where(bare_ref[0, at, :] != 0, bare_current, coated * driving)
        return carry

    lax.fori_loop(0, rows // chunk, body, 0)
    sum_v[...] += lax.dot_general(
        depth_ref[...],
        current_ref[0],
        (((0,), (0,)), ((), ())),
        precision=highest,
        preferred_element_type=jnp.float32,
    )

    @pl.when(step == pl.num_programs(0) - 1)
    def _():
        cells = layers * BLK * BLK
        scale = math.sqrt(cells / (rows * girth * pl.num_programs(0)))
        back = scale * lax.dot_general(
            sum_v[...],
            girth_ref[...],
            (((1,), (1,)), ((), ())),
            precision=highest,
            preferred_element_type=jnp.float32,
        )
        back = jnp.concatenate([back, jnp.zeros_like(back)], axis=1)
        lines = []
        for x in range(BLK):
            spread = turn(back, -BLK * x) if x else back
            spread = pltpu.roll(spread, 0, 1, stride=BLK, stride_axis=0)
            spread = jnp.where(lane // BLK == row, spread, 0.0)
            lines.append(jnp.sum(spread, axis=0, keepdims=True))
        sent_ref[...] = jnp.broadcast_to(jnp.concatenate(lines, axis=0)[None], sent_ref.shape)


def inject_kernel(table_ref, block_ref, got_ref, p_hbm, out_hbm, work_v, sem):
    layers = p_hbm.shape[0]
    per_row = LANES // BLK
    lane = lane_ids()
    piles = [table_ref[j] for j in range(CAP)]
    blocks = [block_ref[jnp.maximum(k, 0)] for k in piles]
    def window(ref, j):
        return ref.at[:, pl.ds(pl.multiple_of(blocks[j] // per_row * BLK, BLK), BLK), :]

    heads = []
    for j in range(CAP):
        head = piles[j] >= 0
        for i in range(j):
            head = head & jnp.logical_not(
                (piles[i] >= 0) & (blocks[i] // per_row == blocks[j] // per_row)
            )
        heads.append(head)
    for j in range(CAP):

        @pl.when(heads[j])
        def _():
            pltpu.make_async_copy(window(p_hbm, j), work_v.at[j], sem.at[0, j]).start()

    for j in range(CAP):

        @pl.when(heads[j])
        def _():
            pltpu.make_async_copy(window(p_hbm, j), work_v.at[j], sem.at[0, j]).wait()
            for i in range(j, CAP):

                @pl.when((piles[i] >= 0) & (blocks[i] // per_row == blocks[j] // per_row))
                def _():
                    start = blocks[i] % per_row * BLK
                    packet = inject_gain * got_ref[jnp.maximum(piles[i], 0)]
                    for l in range(layers):
                        moved = pltpu.roll(packet, (start + LANES - BLK * l) % LANES, 1)
                        inside = (lane >= start) & (lane < start + BLK)
                        work_v[j, l] = work_v[j, l] - jnp.where(inside, moved, 0.0)

            pltpu.make_async_copy(work_v.at[j], window(out_hbm, j), sem.at[1, j]).start()

    for j in range(CAP):

        @pl.when(heads[j])
        def _():
            pltpu.make_async_copy(work_v.at[j], window(out_hbm, j), sem.at[1, j]).wait()


def on_device(
    conductivity,
    source,
    potential_start,
    shell_to_depth,
    shell_to_girth,
    pile_resistance,
    coating_mask,
    pile_tile,
    pile_block,
):
    layers, rows, cols = conductivity.shape
    piles = pile_tile.shape[0]
    depth_cells, girth = coating_mask.shape[1:]
    both = ("gx", "gy")
    me = (lax.axis_index("gx") * lax.axis_size("gy") + lax.axis_index("gy")).astype(jnp.int32)
    me = me.reshape(1)
    smem = pl.BlockSpec(memory_space=pltpu.SMEM)
    vmem = pl.BlockSpec(memory_space=pltpu.VMEM)
    anywhere = pl.BlockSpec(memory_space=pl.ANY)
    f32 = jnp.float32
    three = (potential_start, conductivity, source)

    def pass_on(value, axis, up):
        count = lax.axis_size(axis)
        pairs = [(i, i + 1) for i in range(count - 1)]
        return lax.ppermute(value, axis, pairs if up else [(b, a) for a, b in pairs])

    top = pass_on(jnp.stack([a[:, rows - SUB :, :] for a in three]), "gx", True)
    bottom = pass_on(jnp.stack([a[:, :SUB, :] for a in three]), "gx", False)

    steps = 4
    packed_rows = rows + 2 * SUB
    part = pl.BlockSpec((layers, rows // steps, cols), lambda i: (0, i, 0))
    kept_shape = jax.ShapeDtypeStruct((3, FOLD, packed_rows, cols), f32)
    sent_shape = jax.ShapeDtypeStruct((3, packed_rows, cols), f32)
    kept, packed, table = pl.pallas_call(
        pack_kernel,
        grid=(steps,),
        in_specs=[smem, smem, part, part, part],
        out_specs=[
            pl.BlockSpec((3, FOLD, rows // steps, cols), lambda i: (0, 0, i, 0)),
            pl.BlockSpec((3, rows // steps, cols), lambda i: (0, i, 0)),
            smem,
        ],
        out_shape=[kept_shape, sent_shape, jax.ShapeDtypeStruct((SUB,), jnp.int32)],
        cost_estimate=pl.CostEstimate(
            flops=6 * rows * cols * layers, bytes_accessed=16 * rows * cols * layers, transcendentals=0
        ),
        name="pack_strips",
    )(pile_tile, me, *three)
    whole = pl.BlockSpec((3, layers, SUB, cols), lambda i: (0, 0, 0, 0))
    kept, packed = pl.pallas_call(
        pack_edge_kernel,
        grid=(2,),
        in_specs=[whole, whole, anywhere, anywhere],
        out_specs=[
            pl.BlockSpec((3, FOLD, SUB, cols), lambda i: (0, 0, rows // SUB + i, 0)),
            pl.BlockSpec((3, SUB, cols), lambda i: (0, rows // SUB + i, 0)),
        ],
        out_shape=[kept_shape, sent_shape],
        input_output_aliases={2: 0, 3: 1},
        name="pack_edges",
    )(top, bottom, kept, packed)
    left = pass_on(packed, "gy", True)
    right = pass_on(packed, "gy", False)

    sent = pl.pallas_call(
        shells_kernel,
        in_specs=[smem, smem] + [anywhere] * 7,
        out_specs=vmem,
        out_shape=jax.ShapeDtypeStruct((piles, SUB, LANES), f32),
        scratch_shapes=[
            pltpu.VMEM((CAP, 3, 3, layers, SUB, LANES), f32),
            pltpu.VMEM((CAP, 3, 3, SUB, LANES), f32),
            pltpu.VMEM((8, layers // 2, 5 * SUB, LANES), f32),
            pltpu.SemaphoreType.DMA((CAP, 4, 3)),
        ],
        compiler_params=pltpu.CompilerParams(vmem_limit_bytes=VMEM_LIMIT),
        name="shells",
    )(table, pile_block, *three, top, bottom, left, right)

    half_rows = rows // 2
    padded = pltpu.VMEM((layers + FOLD, half_rows + 5 * SUB, cols), f32)

    def sweep_half(half, edge, kept, left, right, before=None):
        def parts(*lead):
            zeros = (0,) * len(lead)

            def spec(height, index):
                return pl.BlockSpec(lead + (height, cols), lambda i: zeros + (index, 0))

            inner = half_rows // SUB - half
            return [spec(half_rows, half), spec(SUB, rows // SUB + half), spec(SUB, inner)]

        operands = [*three, edge] + [kept] * 3 + [left] * 3 + [right] * 3
        specs = [anywhere] * 4 + parts(3, FOLD) + parts(3) + parts(3)
        aliases = {}
        if before is not None:
            aliases = {len(operands): 0}
            operands.append(before)
            specs.append(anywhere)
        return pl.pallas_call(
            functools.partial(sweep_kernel, half),
            grid=(1,),
            in_specs=specs,
            out_specs=pl.BlockSpec((layers, half_rows, cols), lambda i: (0, half, 0)),
            out_shape=jax.ShapeDtypeStruct((layers, rows, cols), f32),
            input_output_aliases=aliases,
            scratch_shapes=[padded] * 8 + [pltpu.SemaphoreType.DMA((3, 2))],
            compiler_params=pltpu.CompilerParams(vmem_limit_bytes=VMEM_LIMIT),
            cost_estimate=pl.CostEstimate(
                flops=80 * half_rows * cols * layers,
                bytes_accessed=16 * half_rows * cols * layers,
                transcendentals=0,
            ),
            name="sweeps",
        )(*operands)

    sent, top, left_now, right_now = lax.optimization_barrier((sent, top, left, right))
    got = lax.all_to_all(sent, both, 0, 0, tiled=True)
    potential = sweep_half(0, top, kept, left_now, right_now)

    steps = 4
    part = pl.BlockSpec((1, depth_cells // steps, girth), lambda i: (0, i, 0))

    def full(*shape):
        return pl.BlockSpec(shape, lambda i: (0,) * len(shape))

    current, sent_back = pl.pallas_call(
        polarize_kernel,
        grid=(steps,),
        in_specs=[
            smem,
            smem,
            full(piles, SUB, LANES),
            pl.BlockSpec((depth_cells // steps, layers), lambda i: (i, 0)),
            full(BLK * BLK, girth),
            part,
        ],
        out_specs=[part, full(piles, SUB, LANES)],
        out_shape=[
            jax.ShapeDtypeStruct((1, depth_cells, girth), f32),
            jax.ShapeDtypeStruct((piles, SUB, LANES), f32),
        ],
        scratch_shapes=[
            pltpu.VMEM((layers, girth), f32),
            pltpu.VMEM((depth_cells // steps, girth), f32),
            pltpu.VMEM((layers, girth), f32),
        ],
        compiler_params=pltpu.CompilerParams(vmem_limit_bytes=44 << 20),
        name="polarize",
    )(pile_tile[me], pile_resistance, got, shell_to_depth, shell_to_girth, coating_mask)

    sent_back, bottom, potential = lax.optimization_barrier((sent_back, bottom, potential))
    got_back = lax.all_to_all(sent_back, both, 0, 0, tiled=True)
    potential = sweep_half(1, bottom, kept, left_now, right_now, potential)

    potential = pl.pallas_call(
        inject_kernel,
        in_specs=[smem, smem, vmem, anywhere],
        out_specs=anywhere,
        out_shape=jax.ShapeDtypeStruct((layers, rows, cols), f32),
        input_output_aliases={3: 0},
        scratch_shapes=[
            pltpu.VMEM((CAP, layers, SUB, LANES), f32),
            pltpu.SemaphoreType.DMA((2, CAP)),
        ],
        compiler_params=pltpu.CompilerParams(vmem_limit_bytes=8 << 20),
        name="inject",
    )(table, pile_block, got_back, potential)
    return (potential, current)


def solution(mesh):
    placed = (
        P(None, "gx", "gy"),
        P(None, "gx", "gy"),
        P(None, "gx", "gy"),
        P(),
        P(),
        P(("gx", "gy")),
        P(("gx", "gy"), None, None),
        P(),
        P(),
    )
    return jax.shard_map(
        on_device,
        mesh=mesh,
        in_specs=placed,
        out_specs=(P(None, "gx", "gy"), P(("gx", "gy"), None, None)),
        check_vma=False,
    )
```

```python
import functools
import math

import jax
import jax.numpy as jnp
from jax import lax
from jax.experimental import pallas as pl
from jax.experimental.pallas import tpu as pltpu
from jax.sharding import PartitionSpec as P

BLK = 8
CAP = 4
SWEEPS = 4
NEWTON = 3
LANES = 128
SUB = 8
VMEM_LIMIT = 56 << 20
SHELLS_LIMIT = 52 << 20
UNROLL = 2

vertical_ratio = 0.25
inject_gain = 0.5
anodic_slope = 1.2
cathodic_slope = 0.8
coated_conductance = 0.05


def turn(x, shift):
    return pltpu.roll(x, shift % LANES, 1)


def lane_ids(rows=SUB):
    return lax.broadcasted_iota(jnp.int32, (rows, LANES), 1)


WIDE = 32
FOLD = 4


def pack_rows(load, keep, send):
    lane = lane_ids()
    bands = []
    for m in range(FOLD):
        packed = turn(load(m), WIDE // 2)
        for g in range(1, LANES // WIDE):
            moved = turn(load(m + FOLD * g), WIDE * g + WIDE // 2)
            packed = jnp.where(lane // WIDE == g, moved, packed)
        keep(m, packed)
        bands.append(packed)
    part = ((lane + WIDE - 12) % WIDE) // BLK
    sent = bands[0]
    for m in range(1, FOLD):
        sent = jnp.where(part == m, turn(bands[m], BLK * m), sent)
    send(sent)


def pack_kernel(tile_ref, me_ref, p_ref, c_ref, s_ref, kept_ref, sent_ref, table_ref):
    rows = p_ref.shape[1]

    @pl.when(pl.program_id(0) == 0)
    def _():
        def look(k, count):
            table_ref[jnp.minimum(count, SUB - 1)] = k
            return count + (tile_ref[k] == me_ref[0]).astype(jnp.int32)

        count = lax.fori_loop(0, tile_ref.shape[0], look, jnp.int32(0), unroll=16)
        for j in range(SUB):
            table_ref[j] = jnp.where(j < count, table_ref[j], -1)

    def body(t, carry):
        at = pl.ds(pl.multiple_of(t * SUB, SUB), SUB)
        for i, ref in enumerate((p_ref, c_ref, s_ref)):

            def keep(m, value, i=i):
                kept_ref[i, m, at, :] = value

            def send(value, i=i):
                sent_ref[i, at, :] = value

            pack_rows(lambda l, ref=ref: ref[l, at, :], keep, send)
        return carry

    lax.fori_loop(0, rows // SUB, body, 0, unroll=UNROLL)


def edges_kernel(*refs):
    high_ref, low_ref = refs[6:]
    for i in range(3):
        high_ref[i] = refs[i][...]
        low_ref[i] = refs[3 + i][...]


def pack_edge_kernel(top_ref, bottom_ref, kept_hbm, sent_hbm, kept_ref, sent_ref):
    first = pl.program_id(0) == 0
    for i in range(3):

        def keep(m, value, i=i):
            kept_ref[i, m] = value

        def send(value, i=i):
            sent_ref[i] = value

        pack_rows(
            lambda l, i=i: jnp.where(first, top_ref[i, l], bottom_ref[i, l]), keep, send
        )


NEAR = 16
HALF = LANES // 2


def shells_kernel(
    table_ref,
    block_ref,
    p_hbm,
    c_hbm,
    s_hbm,
    top_hbm,
    bottom_hbm,
    left_hbm,
    right_hbm,
    sent_ref,
    tile_v,
    side_v,
    work_v,
    sem,
):
    layers, rows, _ = p_hbm.shape
    folds = layers // 2
    per_row = LANES // BLK
    lane = lane_ids()
    sources = (p_hbm, c_hbm, s_hbm)
    piles = [table_ref[j] for j in range(CAP)]
    filled = [k >= 0 for k in piles]
    blocks = [block_ref[jnp.maximum(k, 0)] for k in piles]
    row_of = [lax.div(b, per_row) for b in blocks]
    col_of = [lax.rem(b, per_row) for b in blocks]
    border = [
        filled[j] & ((col_of[j] == 0) | (col_of[j] == per_row - 1)) for j in range(CAP)
    ]

    def main_copy(i, j, d):
        where = pl.ds(pl.multiple_of((row_of[j] + d - 1) * SUB, SUB), SUB)
        return pltpu.make_async_copy(
            sources[i].at[:, where, :], tile_v.at[j, i, d], sem.at[j, i, d]
        )

    def edge_copy(i, j, d):
        ref = top_hbm if d == 0 else bottom_hbm
        return pltpu.make_async_copy(ref.at[i], tile_v.at[j, i, d], sem.at[j, i, d])

    def side_copy(ref, j, d):
        tile = row_of[j] + d - 1
        tile = jnp.where(tile < 0, rows // SUB, jnp.where(tile >= rows // SUB, rows // SUB + 1, tile))
        where = pl.ds(pl.multiple_of(tile * SUB, SUB), SUB)
        return pltpu.make_async_copy(ref.at[:, where, :], side_v.at[j, d], sem.at[j, 3, d])

    def each_copy(j, act):
        @pl.when(filled[j])
        def _():
            for d in range(3):
                for i in range(3):
                    if d == 1:
                        act(main_copy(i, j, d))
                        continue
                    outside = row_of[j] == (0 if d == 0 else rows // SUB - 1)

                    @pl.when(outside)
                    def _():
                        act(edge_copy(i, j, d))

                    @pl.when(jnp.logical_not(outside))
                    def _():
                        act(main_copy(i, j, d))

        @pl.when(border[j] & (col_of[j] == 0))
        def _():
            for d in range(3):
                act(side_copy(left_hbm, j, d))

        @pl.when(border[j] & (col_of[j] > 0))
        def _():
            for d in range(3):
                act(side_copy(right_hbm, j, d))

    for j in range(CAP):
        each_copy(j, lambda copy: copy.start())
    sent_ref[...] = jnp.zeros_like(sent_ref)
    pa, c_v, s_v, pb, we_v, ws_v, wu_v, inv_v = (work_v.at[i] for i in range(8))
    zero = jnp.zeros((SUB, LANES), jnp.float32)
    for t in (0, 4):
        for ref in (pa, c_v, pb, ws_v):
            for m in range(folds):
                ref[m, t * SUB : (t + 1) * SUB, :] = zero
    for j in range(CAP):
        each_copy(j, lambda copy: copy.wait())

    slot = (lane % HALF) // NEAR
    upper = lane >= HALF
    shifts = [[(HALF * h + NEAR * j + 4 + LANES - BLK * col_of[j]) % LANES for h in (0, 1)] for j in range(CAP)]
    arrays = (pa, c_v, s_v)

    def gather(d, carry):
        at = pl.ds(pl.multiple_of((d + 1) * SUB, SUB), SUB)
        for i in range(3):
            for m in range(folds):
                value = zero
                for j in range(CAP):
                    low = pltpu.roll(tile_v[j, i, d, m], shifts[j][0], 1)
                    high = pltpu.roll(tile_v[j, i, d, m + folds], shifts[j][1], 1)
                    value = jnp.where(
                        (slot == j) & filled[j], jnp.where(upper, high, low), value
                    )
                arrays[i][m, at, :] = value
        return carry

    lax.fori_loop(0, 3, gather, 0)
    for j in range(CAP):

        @pl.when(border[j])
        def _():
            first = col_of[j] == 0
            begin = jnp.where(first, 0, NEAR - 4)
            back = jnp.where(first, 12, 4)

            def mend(d, carry):
                at = pl.ds(pl.multiple_of((d + 1) * SUB, SUB), SUB)
                for i in range(3):
                    side = side_v[j, d, i]
                    for m in range(folds):
                        value = arrays[i][m, at, :]
                        for h in (0, 1):
                            l = m + folds * h
                            base = HALF * h + NEAR * j
                            known = base - WIDE * (l // FOLD) - BLK * (l % FOLD)
                            moved = pltpu.roll(side, (known + 2 * LANES - back) % LANES, 1)
                            here = (lane >= base + begin) & (lane < base + begin + 4)
                            value = jnp.where(here, moved, value)
                        arrays[i][m, at, :] = value
                return carry

            lax.fori_loop(0, 3, mend, 0)

    def span(t, shift=0):
        return slice(t * SUB + shift, (t + 1) * SUB + shift)

    for t in (1, 2, 3):
        cells = [c_v[m, span(t), :] for m in range(folds)]
        weights, wus = [], []
        for m in range(folds):
            here = cells[m]
            we = 0.5 * (here + turn(here, -1))
            ws = 0.5 * (here + c_v[m, span(t, 1), :])
            wn = 0.5 * (here + c_v[m, span(t, -1), :])
            above = cells[m + 1] if m + 1 < folds else turn(cells[0], HALF)
            wu = (0.5 * vertical_ratio) * (here + above)
            if m + 1 == folds:
                wu = jnp.where(upper, 0.0, wu)
            we_v[m, span(t), :] = we
            ws_v[m, span(t), :] = ws
            wu_v[m, span(t), :] = wu
            weights.append(we + turn(we, 1) + ws + wn + wu)
            wus.append(wu)
        for m in range(folds):
            below = wus[m - 1] if m else turn(wus[-1], HALF)
            inside = cells[m] > 0.0
            weight = jnp.where(inside, weights[m] + below, 1.0)
            inv_v[m, span(t), :] = jnp.where(inside, 1.0 / weight, 0.0)

    def sweep(old, new, t):
        values = [old[m, span(t), :] for m in range(folds)]
        wus = [wu_v[m, span(t), :] for m in range(folds)]
        for m in range(folds):
            here = values[m]
            we = we_v[m, span(t), :]
            total = s_v[m, span(t), :] + we * turn(here, -1) + turn(we * here, 1)
            total = total + ws_v[m, span(t), :] * old[m, span(t, 1), :]
            total = total + ws_v[m, span(t, -1), :] * old[m, span(t, -1), :]
            above = values[m + 1] if m + 1 < folds else turn(values[0], HALF)
            below = wus[m - 1] * values[m - 1] if m else turn(wus[-1] * values[-1], HALF)
            total = total + wus[m] * above + below
            new[m, span(t), :] = total * inv_v[m, span(t), :]

    pairs = (pa, pb)
    for k in range(SWEEPS):
        for t in (1, 2, 3) if k < SWEEPS - 1 else (2,):
            sweep(pairs[k % 2], pairs[(k + 1) % 2], t)
    done = pairs[SWEEPS % 2]
    for j in range(CAP):

        @pl.when(filled[j])
        def _():
            packet = zero
            for l in range(layers):
                group = layers - 1 - l
                begin = HALF * (l // folds) + NEAR * j + 4
                moved = turn(done[l % folds, span(2), :], BLK * group - begin)
                packet = jnp.where(lane // BLK == group, moved, packet)
            sent_ref[piles[j]] = packet


def sweep_kernel(
    half,
    p_hbm,
    c_hbm,
    s_hbm,
    edge_hbm,
    kept_ref,
    kept_edge_ref,
    kept_inner_ref,
    left_ref,
    left_edge_ref,
    left_inner_ref,
    right_ref,
    right_edge_ref,
    right_inner_ref,
    *rest,
):
    out_ref, c_v, s_v, pa_v, pb_v, we_v, ws_v, wu_v, inv_v, sem = rest[-10:]
    layers = p_hbm.shape[0]
    tile_rows = out_ref.shape[1]
    tiles = tile_rows // SUB
    first, last = 1, tiles + 2
    edge = last if half else first
    lane = lane_ids()
    place = lane % WIDE
    arrays = (pa_v, c_v, s_v)
    copies = []
    own = pl.ds(0, layers)
    for i, (src, dst) in enumerate(zip((p_hbm, c_hbm, s_hbm), arrays)):
        begin = half * (tile_rows - SUB)
        into = SUB if half else 2 * SUB
        copies.append(
            pltpu.make_async_copy(
                src.at[:, pl.ds(begin, tile_rows + SUB), :],
                dst.at[own, pl.ds(into, tile_rows + SUB), :],
                sem.at[i, 0],
            )
        )
        copies.append(
            pltpu.make_async_copy(
                edge_hbm.at[i], dst.at[own, pl.ds(edge * SUB, SUB), :], sem.at[i, 1]
            )
        )
    for copy in copies:
        copy.start()
    zero = jnp.zeros((SUB, LANES), jnp.float32)
    for t in (0, last + 1):
        for ref in (c_v, pa_v, pb_v, ws_v):
            for l in range(layers + FOLD):
                ref[l, t * SUB : (t + 1) * SUB, :] = zero

    def at(t, shift=0):
        if shift:
            return pl.ds(t * SUB + shift, SUB)
        return pl.ds(pl.multiple_of(t * SUB, SUB), SUB)

    def join_windows(t, src, kept_rows, left_rows, right_rows):
        for i, dst in enumerate(arrays):
            left = left_rows[i, src, :]
            right = right_rows[i, src, :]
            for m in range(FOLD):
                kept = kept_rows[i, m, src, :]
                west = turn(left, BLK - BLK * m) if m != 1 else left
                east = turn(right, -BLK * m) if m else right
                inner = turn(kept, BLK)
                value = jnp.where(place < 20, east, west)
                value = jnp.where((place >= 4) & (place < 16), kept, value)
                value = jnp.where((place >= 24) | (place < 4), inner, value)
                dst[layers + m, at(t), :] = value

    def join_own(t, carry):
        src = pl.ds(pl.multiple_of(t * SUB - 2 * SUB, SUB), SUB)
        join_windows(t, src, kept_ref, left_ref, right_ref)
        return carry

    lax.fori_loop(first + 1, last, join_own, 0)
    every = slice(None)
    join_windows(edge, every, kept_edge_ref, left_edge_ref, right_edge_ref)
    join_windows(first + last - edge, every, kept_inner_ref, left_inner_ref, right_inner_ref)
    for copy in copies:
        copy.wait()

    def prepare(t, carry):
        def faces(n, here, above):
            we = 0.5 * (here + turn(here, -1))
            ws = 0.5 * (here + c_v[n, at(t, 1), :])
            wn = 0.5 * (here + c_v[n, at(t, -1), :])
            we_v[n, at(t), :] = we
            ws_v[n, at(t), :] = ws
            weight = we + turn(we, 1) + ws + wn
            if above is None:
                return weight, None
            wu = (0.5 * vertical_ratio) * (here + above)
            wu_v[n, at(t), :] = wu
            return weight + wu, wu

        def finish(n, here, weight):
            inside = here > 0.0
            inv_v[n, at(t), :] = jnp.where(inside, 1.0 / jnp.where(inside, weight, 1.0), 0.0)

        here = c_v[0, at(t), :]
        below = None
        for l in range(layers):
            above = c_v[l + 1, at(t), :] if l + 1 < layers else None
            weight, wu = faces(l, here, above)
            finish(l, here, weight if below is None else weight + below)
            here, below = above, wu
        bands = [c_v[layers + m, at(t), :] for m in range(FOLD)]
        weights = []
        for m in range(FOLD - 1):
            weights.append(faces(layers + m, bands[m], bands[m + 1]))
        weight, _ = faces(layers + FOLD - 1, bands[-1], None)
        wu = (0.5 * vertical_ratio) * (bands[-1] + turn(bands[0], -WIDE))
        wu = jnp.where(topmost, 0.0, wu)
        wu_v[layers + FOLD - 1, at(t), :] = wu
        weights.append((weight + wu, wu))
        below = jnp.where(bottommost, 0.0, turn(wu, WIDE))
        for m in range(FOLD):
            finish(layers + m, bands[m], weights[m][0] + below)
            below = weights[m][1]
        return carry

    group = ((lane + LANES - 4) % LANES) // WIDE
    topmost = group == LANES // WIDE - 1
    bottommost = group == 0
    lax.fori_loop(first, last + 1, prepare, 0, unroll=UNROLL)

    def make_sweep(old, store):
        def flat(n, t, here):
            we = we_v[n, at(t), :]
            total = s_v[n, at(t), :] + we * turn(here, -1) + turn(we * here, 1)
            total = total + ws_v[n, at(t), :] * old[n, at(t, 1), :]
            return total + ws_v[n, at(t, -1), :] * old[n, at(t, -1), :]

        def sweep(t, carry):
            values = []
            bands = [old[layers + m, at(t), :] for m in range(FOLD)]
            wus = [wu_v[layers + m, at(t), :] for m in range(FOLD)]
            ups = bands[1:] + [turn(bands[0], -WIDE)]
            downs = [turn(wus[-1] * bands[-1], WIDE)]
            downs += [wus[m] * bands[m] for m in range(FOLD - 1)]
            for m in range(FOLD):
                total = flat(layers + m, t, bands[m]) + wus[m] * ups[m] + downs[m]
                values.append(total * inv_v[layers + m, at(t), :])
            extra = store.windows(t, values)
            below = None
            here = old[0, at(t), :]
            for l in range(layers):
                total = flat(l, t, here)
                if l:
                    total = total + below
                if l + 1 < layers:
                    above = old[l + 1, at(t), :]
                    wu = wu_v[l, at(t), :]
                    total = total + wu * above
                    below, here = wu * here, above
                store.layer(l, t, total * inv_v[l, at(t), :], extra)
            return carry

        return sweep

    class Keep:
        def __init__(self, new):
            self.new = new

        def windows(self, t, values):
            for m in range(FOLD):
                self.new[layers + m, at(t), :] = values[m]

        def layer(self, l, t, value, extra):
            self.new[l, at(t), :] = value

    class Finish:
        def windows(self, t, values):
            return [jnp.where(place < 16, value, turn(value, -BLK)) for value in values]

        def layer(self, l, t, value, extra):
            outer = turn(extra[l % FOLD], LANES - WIDE // 2 - WIDE * (l // FOLD))
            value = jnp.where((lane >= 4) & (lane < LANES - 4), value, outer)
            out_ref[l, pl.ds(pl.multiple_of(t * SUB - 2 * SUB, SUB), SUB), :] = value

    pairs = (pa_v, pb_v)
    for k in range(SWEEPS - 1):
        lax.fori_loop(
            first, last + 1, make_sweep(pairs[k % 2], Keep(pairs[(k + 1) % 2])), 0, unroll=6
        )
    lax.fori_loop(
        first + 1, last, make_sweep(pairs[(SWEEPS - 1) % 2], Finish()), 0, unroll=UNROLL
    )


def polarize_kernel(
    tile_ref, me_ref, resist_ref, got_ref, depth_ref, girth_ref, bare_ref, current_ref, sent_ref, near_v, drive_v, sum_v
):
    layers = depth_ref.shape[1]
    rows, girth = bare_ref.shape[1:]
    step = pl.program_id(0)
    highest = lax.Precision.HIGHEST
    resist = resist_ref[0]
    lane = lane_ids(layers)
    row = lax.broadcasted_iota(jnp.int32, (layers, LANES), 0)

    @pl.when(step == 0)
    def _():
        packet = got_ref[tile_ref[me_ref[0]]]
        shell = jnp.zeros((layers, LANES), jnp.float32)
        for x in range(BLK):
            spread = jnp.broadcast_to(packet[x : x + 1, :], (layers, LANES))
            spread = pltpu.roll(spread, 0, 1, stride=BLK, stride_axis=0)
            spread = turn(spread, BLK * (x + 1) - BLK * layers)
            shell = jnp.where(lane // BLK == x, spread, shell)
        near_v[...] = jnp.dot(
            shell[:, : BLK * BLK],
            girth_ref[...],
            precision=highest,
            preferred_element_type=jnp.float32,
        )
        sum_v[...] = jnp.zeros_like(sum_v)

    drive_v[...] = jnp.dot(
        depth_ref[...], near_v[...], precision=highest, preferred_element_type=jnp.float32
    )
    up = math.log2(math.e) / anodic_slope
    down = -math.log2(math.e) / cathodic_slope
    steep = resist / anodic_slope
    steep_down = resist / cathodic_slope
    coated = coated_conductance / (1.0 + coated_conductance * resist)
    chunk = 64

    def body(i, carry):
        at = pl.ds(pl.multiple_of(i * chunk, chunk), chunk)
        driving = drive_v[at, :]
        value = driving
        for n in range(NEWTON):
            anodic = jnp.exp2(value * up)
            cathodic = jnp.exp2(value * down)
            excess = resist * (anodic - cathodic)
            if n:
                excess = excess + (value - driving)
            slope = 1.0 + (steep * anodic + steep_down * cathodic)
            value = value - excess / slope
        bare_current = jnp.exp2(value * up) - jnp.exp2(value * down)
        current_ref[0, at, :] = jnp.where(bare_ref[0, at, :] != 0, bare_current, coated * driving)
        return carry

    lax.fori_loop(0, rows // chunk, body, 0)
    sum_v[...] += lax.dot_general(
        depth_ref[...],
        current_ref[0],
        (((0,), (0,)), ((), ())),
        precision=lax.Precision.HIGH,
        preferred_element_type=jnp.float32,
    )

    @pl.when(step == pl.num_programs(0) - 1)
    def _():
        cells = layers * BLK * BLK
        scale = math.sqrt(cells / (rows * girth * pl.num_programs(0)))
        back = scale * lax.dot_general(
            sum_v[...],
            girth_ref[...],
            (((1,), (1,)), ((), ())),
            precision=lax.Precision.HIGH,
            preferred_element_type=jnp.float32,
        )
        back = jnp.concatenate([back, jnp.zeros_like(back)], axis=1)
        lines = []
        for x in range(BLK):
            spread = turn(back, -BLK * x) if x else back
            spread = pltpu.roll(spread, 0, 1, stride=BLK, stride_axis=0)
            spread = jnp.where(lane // BLK == row, spread, 0.0)
            lines.append(jnp.sum(spread, axis=0, keepdims=True))
        sent_ref[...] = jnp.broadcast_to(jnp.concatenate(lines, axis=0)[None], sent_ref.shape)


def inject_kernel(table_ref, block_ref, got_ref, p_hbm, out_hbm, work_v, sem):
    layers = p_hbm.shape[0]
    per_row = LANES // BLK
    lane = lane_ids()
    piles = [table_ref[j] for j in range(CAP)]
    blocks = [block_ref[jnp.maximum(k, 0)] for k in piles]
    def window(ref, j):
        return ref.at[:, pl.ds(pl.multiple_of(blocks[j] // per_row * BLK, BLK), BLK), :]

    heads = []
    for j in range(CAP):
        head = piles[j] >= 0
        for i in range(j):
            head = head & jnp.logical_not(
                (piles[i] >= 0) & (blocks[i] // per_row == blocks[j] // per_row)
            )
        heads.append(head)
    for j in range(CAP):

        @pl.when(heads[j])
        def _():
            pltpu.make_async_copy(window(p_hbm, j), work_v.at[j], sem.at[0, j]).start()

    for j in range(CAP):

        @pl.when(heads[j])
        def _():
            pltpu.make_async_copy(window(p_hbm, j), work_v.at[j], sem.at[0, j]).wait()
            for i in range(j, CAP):

                @pl.when((piles[i] >= 0) & (blocks[i] // per_row == blocks[j] // per_row))
                def _():
                    start = blocks[i] % per_row * BLK
                    packet = inject_gain * got_ref[jnp.maximum(piles[i], 0)]
                    for l in range(layers):
                        moved = pltpu.roll(packet, (start + LANES - BLK * l) % LANES, 1)
                        inside = (lane >= start) & (lane < start + BLK)
                        work_v[j, l] = work_v[j, l] - jnp.where(inside, moved, 0.0)

            pltpu.make_async_copy(work_v.at[j], window(out_hbm, j), sem.at[1, j]).start()

    for j in range(CAP):

        @pl.when(heads[j])
        def _():
            pltpu.make_async_copy(work_v.at[j], window(out_hbm, j), sem.at[1, j]).wait()


def on_device(
    conductivity,
    source,
    potential_start,
    shell_to_depth,
    shell_to_girth,
    pile_resistance,
    coating_mask,
    pile_tile,
    pile_block,
):
    layers, rows, cols = conductivity.shape
    piles = pile_tile.shape[0]
    depth_cells, girth = coating_mask.shape[1:]
    both = ("gx", "gy")
    me = (lax.axis_index("gx") * lax.axis_size("gy") + lax.axis_index("gy")).astype(jnp.int32)
    me = me.reshape(1)
    smem = pl.BlockSpec(memory_space=pltpu.SMEM)
    vmem = pl.BlockSpec(memory_space=pltpu.VMEM)
    anywhere = pl.BlockSpec(memory_space=pl.ANY)
    f32 = jnp.float32
    three = (potential_start, conductivity, source)

    def pass_on(value, axis, up):
        count = lax.axis_size(axis)
        pairs = [(i, i + 1) for i in range(count - 1)]
        return lax.ppermute(value, axis, pairs if up else [(b, a) for a, b in pairs])

    edge_shape = jax.ShapeDtypeStruct((3, layers, SUB, cols), f32)
    corner = [
        pl.BlockSpec((layers, SUB, cols), lambda i, r=r: (0, r, 0)) for r in (rows // SUB - 1, 0)
    ]
    high, low = pl.pallas_call(
        edges_kernel,
        grid=(1,),
        in_specs=[corner[0]] * 3 + [corner[1]] * 3,
        out_specs=[pl.BlockSpec((3, layers, SUB, cols), lambda i: (0, 0, 0, 0))] * 2,
        out_shape=[edge_shape] * 2,
        name="edges",
    )(*three, *three)
    top = pass_on(high, "gx", True)
    bottom = pass_on(low, "gx", False)

    steps = 4
    packed_rows = rows + 2 * SUB
    part = pl.BlockSpec((layers, rows // steps, cols), lambda i: (0, i, 0))
    kept_shape = jax.ShapeDtypeStruct((3, FOLD, packed_rows, cols), f32)
    sent_shape = jax.ShapeDtypeStruct((3, packed_rows, cols), f32)
    kept, packed, table = pl.pallas_call(
        pack_kernel,
        grid=(steps,),
        in_specs=[smem, smem, part, part, part],
        out_specs=[
            pl.BlockSpec((3, FOLD, rows // steps, cols), lambda i: (0, 0, i, 0)),
            pl.BlockSpec((3, rows // steps, cols), lambda i: (0, i, 0)),
            smem,
        ],
        out_shape=[kept_shape, sent_shape, jax.ShapeDtypeStruct((SUB,), jnp.int32)],
        cost_estimate=pl.CostEstimate(
            flops=6 * rows * cols * layers, bytes_accessed=16 * rows * cols * layers, transcendentals=0
        ),
        name="pack_strips",
    )(pile_tile, me, *three)
    whole = pl.BlockSpec((3, layers, SUB, cols), lambda i: (0, 0, 0, 0))
    kept, packed = pl.pallas_call(
        pack_edge_kernel,
        grid=(2,),
        in_specs=[whole, whole, anywhere, anywhere],
        out_specs=[
            pl.BlockSpec((3, FOLD, SUB, cols), lambda i: (0, 0, rows // SUB + i, 0)),
            pl.BlockSpec((3, SUB, cols), lambda i: (0, rows // SUB + i, 0)),
        ],
        out_shape=[kept_shape, sent_shape],
        input_output_aliases={2: 0, 3: 1},
        compiler_params=pltpu.CompilerParams(vmem_limit_bytes=53 << 20),
        name="pack_edges",
    )(top, bottom, kept, packed)
    left = pass_on(packed, "gy", True)
    right = pass_on(packed, "gy", False)

    sent = pl.pallas_call(
        shells_kernel,
        in_specs=[smem, smem] + [anywhere] * 7,
        out_specs=vmem,
        out_shape=jax.ShapeDtypeStruct((piles, SUB, LANES), f32),
        scratch_shapes=[
            pltpu.VMEM((CAP, 3, 3, layers, SUB, LANES), f32),
            pltpu.VMEM((CAP, 3, 3, SUB, LANES), f32),
            pltpu.VMEM((8, layers // 2, 5 * SUB, LANES), f32),
            pltpu.SemaphoreType.DMA((CAP, 4, 3)),
        ],
        compiler_params=pltpu.CompilerParams(vmem_limit_bytes=SHELLS_LIMIT),
        name="shells",
    )(table, pile_block, *three, top, bottom, left, right)

    half_rows = rows // 2
    padded = pltpu.VMEM((layers + FOLD, half_rows + 5 * SUB, cols), f32)

    def sweep_half(half, edge, kept, left, right, before=None):
        def parts(*lead):
            zeros = (0,) * len(lead)

            def spec(height, index):
                return pl.BlockSpec(lead + (height, cols), lambda i: zeros + (index, 0))

            inner = half_rows // SUB - half
            return [spec(half_rows, half), spec(SUB, rows // SUB + half), spec(SUB, inner)]

        operands = [*three, edge] + [kept] * 3 + [left] * 3 + [right] * 3
        specs = [anywhere] * 4 + parts(3, FOLD) + parts(3) + parts(3)
        aliases = {}
        if before is not None:
            aliases = {len(operands): 0}
            operands.append(before)
            specs.append(anywhere)
        return pl.pallas_call(
            functools.partial(sweep_kernel, half),
            grid=(1,),
            in_specs=specs,
            out_specs=pl.BlockSpec((layers, half_rows, cols), lambda i: (0, half, 0)),
            out_shape=jax.ShapeDtypeStruct((layers, rows, cols), f32),
            input_output_aliases=aliases,
            scratch_shapes=[padded] * 8 + [pltpu.SemaphoreType.DMA((3, 2))],
            compiler_params=pltpu.CompilerParams(vmem_limit_bytes=VMEM_LIMIT),
            cost_estimate=pl.CostEstimate(
                flops=80 * half_rows * cols * layers,
                bytes_accessed=16 * half_rows * cols * layers,
                transcendentals=0,
            ),
            name="sweeps",
        )(*operands)

    sent, top, left_now, right_now = lax.optimization_barrier((sent, top, left, right))
    got = lax.all_to_all(sent, both, 0, 0, tiled=True)
    potential = sweep_half(0, top, kept, left_now, right_now)

    steps = 4
    part = pl.BlockSpec((1, depth_cells // steps, girth), lambda i: (0, i, 0))

    def full(*shape):
        return pl.BlockSpec(shape, lambda i: (0,) * len(shape))

    current, sent_back = pl.pallas_call(
        polarize_kernel,
        grid=(steps,),
        in_specs=[
            smem,
            smem,
            smem,
            full(piles, SUB, LANES),
            pl.BlockSpec((depth_cells // steps, layers), lambda i: (i, 0)),
            full(BLK * BLK, girth),
            part,
        ],
        out_specs=[part, full(piles, SUB, LANES)],
        out_shape=[
            jax.ShapeDtypeStruct((1, depth_cells, girth), f32),
            jax.ShapeDtypeStruct((piles, SUB, LANES), f32),
        ],
        scratch_shapes=[
            pltpu.VMEM((layers, girth), f32),
            pltpu.VMEM((depth_cells // steps, girth), f32),
            pltpu.VMEM((layers, girth), f32),
        ],
        compiler_params=pltpu.CompilerParams(vmem_limit_bytes=SHELLS_LIMIT),
        name="polarize",
    )(pile_tile, me, pile_resistance, got, shell_to_depth, shell_to_girth, coating_mask)

    sent_back, bottom, potential = lax.optimization_barrier((sent_back, bottom, potential))
    got_back = lax.all_to_all(sent_back, both, 0, 0, tiled=True)
    potential = sweep_half(1, bottom, kept, left_now, right_now, potential)

    potential = pl.pallas_call(
        inject_kernel,
        in_specs=[smem, smem, vmem, anywhere],
        out_specs=anywhere,
        out_shape=jax.ShapeDtypeStruct((layers, rows, cols), f32),
        input_output_aliases={3: 0},
        scratch_shapes=[
            pltpu.VMEM((CAP, layers, SUB, LANES), f32),
            pltpu.SemaphoreType.DMA((2, CAP)),
        ],
        compiler_params=pltpu.CompilerParams(vmem_limit_bytes=8 << 20),
        name="inject",
    )(table, pile_block, got_back, potential)
    return (potential, current)


def solution(mesh):
    placed = (
        P(None, "gx", "gy"),
        P(None, "gx", "gy"),
        P(None, "gx", "gy"),
        P(),
        P(),
        P(("gx", "gy")),
        P(("gx", "gy"), None, None),
        P(),
        P(),
    )
    return jax.shard_map(
        on_device,
        mesh=mesh,
        in_specs=placed,
        out_specs=(P(None, "gx", "gy"), P(("gx", "gy"), None, None)),
        check_vma=False,
    )
```

```python
import functools
import math

import jax
import jax.numpy as jnp
from jax import lax
from jax.experimental import pallas as pl
from jax.experimental.pallas import tpu as pltpu
from jax.sharding import PartitionSpec as P

BLK = 8
CAP = 4
SWEEPS = 4
NEWTON = 3
LANES = 128
SUB = 8
VMEM_LIMIT = 56 << 20
SHELLS_LIMIT = 52 << 20
UNROLL = 2

vertical_ratio = 0.25
inject_gain = 0.5
anodic_slope = 1.2
cathodic_slope = 0.8
coated_conductance = 0.05


def turn(x, shift):
    return pltpu.roll(x, shift % LANES, 1)


def lane_ids(rows=SUB):
    return lax.broadcasted_iota(jnp.int32, (rows, LANES), 1)


WIDE = 32
FOLD = 4


def pack_rows(load, keep, send):
    lane = lane_ids()
    bands = []
    for m in range(FOLD):
        packed = load(m)
        for g in range(1, LANES // WIDE):
            moved = turn(load(m + FOLD * g), WIDE * g)
            packed = jnp.where(((lane + WIDE // 2) % LANES) // WIDE == g, moved, packed)
        keep(m, packed)
        bands.append(packed)
    part = ((lane + 4) % WIDE) // BLK
    sent = bands[0]
    for m in range(1, FOLD):
        sent = jnp.where(part == m, turn(bands[m], BLK * m), sent)
    send(sent)


def table_kernel(tile_ref, me_ref, table_ref):
    def look(k, count):
        table_ref[jnp.minimum(count, SUB - 1)] = k
        return count + (tile_ref[k] == me_ref[0]).astype(jnp.int32)

    count = lax.fori_loop(0, tile_ref.shape[0], look, jnp.int32(0), unroll=16)
    for j in range(SUB):
        table_ref[j] = jnp.where(j < count, table_ref[j], -1)


def pack_kernel(p_ref, c_ref, s_ref, kept_ref, sent_ref):
    rows = p_ref.shape[1]

    def body(t, carry):
        at = pl.ds(pl.multiple_of(t * SUB, SUB), SUB)
        for i, ref in enumerate((p_ref, c_ref, s_ref)):

            def keep(m, value, i=i):
                kept_ref[i, m, at, :] = value

            def send(value, i=i):
                sent_ref[i, at, :] = value

            pack_rows(lambda l, ref=ref: ref[l, at, :], keep, send)
        return carry

    lax.fori_loop(0, rows // SUB, body, 0, unroll=UNROLL)


def edges_kernel(*refs):
    high_ref, low_ref = refs[6:]
    for i in range(3):
        high_ref[i] = refs[i][...]
        low_ref[i] = refs[3 + i][...]


def pack_edge_kernel(top_ref, bottom_ref, kept_hbm, sent_hbm, kept_ref, sent_ref):
    first = pl.program_id(0) == 0
    for i in range(3):

        def keep(m, value, i=i):
            kept_ref[i, m] = value

        def send(value, i=i):
            sent_ref[i] = value

        pack_rows(
            lambda l, i=i: jnp.where(first, top_ref[i, l], bottom_ref[i, l]), keep, send
        )


NEAR = 16
HALF = LANES // 2


def shells_kernel(
    table_ref,
    block_ref,
    p_hbm,
    c_hbm,
    s_hbm,
    top_hbm,
    bottom_hbm,
    left_hbm,
    right_hbm,
    sent_ref,
    tile_v,
    side_v,
    work_v,
    sem,
):
    layers, rows, _ = p_hbm.shape
    folds = layers // 2
    per_row = LANES // BLK
    lane = lane_ids()
    sources = (p_hbm, c_hbm, s_hbm)
    piles = [table_ref[j] for j in range(CAP)]
    filled = [k >= 0 for k in piles]
    blocks = [block_ref[jnp.maximum(k, 0)] for k in piles]
    row_of = [lax.div(b, per_row) for b in blocks]
    col_of = [lax.rem(b, per_row) for b in blocks]
    border = [
        filled[j] & ((col_of[j] == 0) | (col_of[j] == per_row - 1)) for j in range(CAP)
    ]

    def main_copy(i, j, d):
        where = pl.ds(pl.multiple_of((row_of[j] + d - 1) * SUB, SUB), SUB)
        return pltpu.make_async_copy(
            sources[i].at[:, where, :], tile_v.at[j, i, d], sem.at[j, i, d]
        )

    def edge_copy(i, j, d):
        ref = top_hbm if d == 0 else bottom_hbm
        return pltpu.make_async_copy(ref.at[i], tile_v.at[j, i, d], sem.at[j, i, d])

    def side_copy(ref, j, d):
        tile = row_of[j] + d - 1
        tile = jnp.where(tile < 0, rows // SUB, jnp.where(tile >= rows // SUB, rows // SUB + 1, tile))
        where = pl.ds(pl.multiple_of(tile * SUB, SUB), SUB)
        return pltpu.make_async_copy(ref.at[:, where, :], side_v.at[j, d], sem.at[j, 3, d])

    def each_copy(j, act):
        @pl.when(filled[j])
        def _():
            for d in range(3):
                for i in range(3):
                    if d == 1:
                        act(main_copy(i, j, d))
                        continue
                    outside = row_of[j] == (0 if d == 0 else rows // SUB - 1)

                    @pl.when(outside)
                    def _():
                        act(edge_copy(i, j, d))

                    @pl.when(jnp.logical_not(outside))
                    def _():
                        act(main_copy(i, j, d))

        @pl.when(border[j] & (col_of[j] == 0))
        def _():
            for d in range(3):
                act(side_copy(left_hbm, j, d))

        @pl.when(border[j] & (col_of[j] > 0))
        def _():
            for d in range(3):
                act(side_copy(right_hbm, j, d))

    for j in range(CAP):
        each_copy(j, lambda copy: copy.start())
    sent_ref[...] = jnp.zeros_like(sent_ref)
    pa, c_v, s_v, pb, we_v, ws_v, wu_v, inv_v = (work_v.at[i] for i in range(8))
    zero = jnp.zeros((SUB, LANES), jnp.float32)
    for t in (0, 4):
        for ref in (pa, c_v, pb, ws_v):
            for m in range(folds):
                ref[m, t * SUB : (t + 1) * SUB, :] = zero
    for j in range(CAP):
        each_copy(j, lambda copy: copy.wait())

    slot = (lane % HALF) // NEAR
    upper = lane >= HALF
    shifts = [[(HALF * h + NEAR * j + 4 + LANES - BLK * col_of[j]) % LANES for h in (0, 1)] for j in range(CAP)]
    arrays = (pa, c_v, s_v)

    def gather(d, carry):
        at = pl.ds(pl.multiple_of((d + 1) * SUB, SUB), SUB)
        for i in range(3):
            for m in range(folds):
                value = zero
                for j in range(CAP):
                    low = pltpu.roll(tile_v[j, i, d, m], shifts[j][0], 1)
                    high = pltpu.roll(tile_v[j, i, d, m + folds], shifts[j][1], 1)
                    value = jnp.where(
                        (slot == j) & filled[j], jnp.where(upper, high, low), value
                    )
                arrays[i][m, at, :] = value
        return carry

    lax.fori_loop(0, 3, gather, 0)
    for j in range(CAP):

        @pl.when(border[j])
        def _():
            first = col_of[j] == 0
            begin = jnp.where(first, 0, NEAR - 4)
            back = jnp.where(first, 12, 4)

            def mend(d, carry):
                at = pl.ds(pl.multiple_of((d + 1) * SUB, SUB), SUB)
                for i in range(3):
                    side = side_v[j, d, i]
                    for m in range(folds):
                        value = arrays[i][m, at, :]
                        for h in (0, 1):
                            l = m + folds * h
                            base = HALF * h + NEAR * j
                            known = base + WIDE // 2 - WIDE * (l // FOLD) - BLK * (l % FOLD)
                            moved = pltpu.roll(side, (known + 2 * LANES - back) % LANES, 1)
                            here = (lane >= base + begin) & (lane < base + begin + 4)
                            value = jnp.where(here, moved, value)
                        arrays[i][m, at, :] = value
                return carry

            lax.fori_loop(0, 3, mend, 0)

    def span(t, shift=0):
        return slice(t * SUB + shift, (t + 1) * SUB + shift)

    for t in (1, 2, 3):
        cells = [c_v[m, span(t), :] for m in range(folds)]
        weights, wus = [], []
        for m in range(folds):
            here = cells[m]
            we = 0.5 * (here + turn(here, -1))
            ws = 0.5 * (here + c_v[m, span(t, 1), :])
            wn = 0.5 * (here + c_v[m, span(t, -1), :])
            above = cells[m + 1] if m + 1 < folds else turn(cells[0], HALF)
            wu = (0.5 * vertical_ratio) * (here + above)
            if m + 1 == folds:
                wu = jnp.where(upper, 0.0, wu)
            we_v[m, span(t), :] = we
            ws_v[m, span(t), :] = ws
            wu_v[m, span(t), :] = wu
            weights.append(we + turn(we, 1) + ws + wn + wu)
            wus.append(wu)
        for m in range(folds):
            below = wus[m - 1] if m else turn(wus[-1], HALF)
            inside = cells[m] > 0.0
            weight = jnp.where(inside, weights[m] + below, 1.0)
            inv_v[m, span(t), :] = jnp.where(inside, 1.0 / weight, 0.0)

    def sweep(old, new, t):
        values = [old[m, span(t), :] for m in range(folds)]
        wus = [wu_v[m, span(t), :] for m in range(folds)]
        for m in range(folds):
            here = values[m]
            we = we_v[m, span(t), :]
            total = s_v[m, span(t), :] + we * turn(here, -1) + turn(we * here, 1)
            total = total + ws_v[m, span(t), :] * old[m, span(t, 1), :]
            total = total + ws_v[m, span(t, -1), :] * old[m, span(t, -1), :]
            above = values[m + 1] if m + 1 < folds else turn(values[0], HALF)
            below = wus[m - 1] * values[m - 1] if m else turn(wus[-1] * values[-1], HALF)
            total = total + wus[m] * above + below
            new[m, span(t), :] = total * inv_v[m, span(t), :]

    pairs = (pa, pb)
    for k in range(SWEEPS):
        for t in (1, 2, 3) if k < SWEEPS - 1 else (2,):
            sweep(pairs[k % 2], pairs[(k + 1) % 2], t)
    done = pairs[SWEEPS % 2]
    for j in range(CAP):

        @pl.when(filled[j])
        def _():
            packet = zero
            for l in range(layers):
                group = layers - 1 - l
                begin = HALF * (l // folds) + NEAR * j + 4
                moved = turn(done[l % folds, span(2), :], BLK * group - begin)
                packet = jnp.where(lane // BLK == group, moved, packet)
            sent_ref[piles[j]] = packet


def sweep_kernel(
    half,
    p_hbm,
    c_hbm,
    s_hbm,
    edge_hbm,
    kept_ref,
    kept_edge_ref,
    kept_inner_ref,
    left_ref,
    left_edge_ref,
    left_inner_ref,
    right_ref,
    right_edge_ref,
    right_inner_ref,
    *rest,
):
    out_ref, c_v, s_v, pa_v, pb_v, we_v, ws_v, wu_v, inv_v, sem = rest[-10:]
    layers = p_hbm.shape[0]
    tile_rows = out_ref.shape[1]
    tiles = tile_rows // SUB
    first, last = 1, tiles + 2
    edge = last if half else first
    lane = lane_ids()
    place = (lane + WIDE // 2) % WIDE
    arrays = (pa_v, c_v, s_v)
    copies = []
    own = pl.ds(0, layers)
    for i, (src, dst) in enumerate(zip((p_hbm, c_hbm, s_hbm), arrays)):
        begin = half * (tile_rows - SUB)
        into = SUB if half else 2 * SUB
        copies.append(
            pltpu.make_async_copy(
                src.at[:, pl.ds(begin, tile_rows + SUB), :],
                dst.at[own, pl.ds(into, tile_rows + SUB), :],
                sem.at[i, 0],
            )
        )
        copies.append(
            pltpu.make_async_copy(
                edge_hbm.at[i], dst.at[own, pl.ds(edge * SUB, SUB), :], sem.at[i, 1]
            )
        )
    for copy in copies:
        copy.start()
    zero = jnp.zeros((SUB, LANES), jnp.float32)
    for t in (0, last + 1):
        for ref in (c_v, pa_v, pb_v, ws_v):
            for l in range(layers + FOLD):
                ref[l, t * SUB : (t + 1) * SUB, :] = zero

    def at(t, shift=0):
        if shift:
            return pl.ds(t * SUB + shift, SUB)
        return pl.ds(pl.multiple_of(t * SUB, SUB), SUB)

    def join_windows(t, src, kept_rows, left_rows, right_rows):
        for i, dst in enumerate(arrays):
            left = left_rows[i, src, :]
            right = right_rows[i, src, :]
            for m in range(FOLD):
                kept = kept_rows[i, m, src, :]
                west = turn(left, BLK - BLK * m) if m != 1 else left
                east = turn(right, -BLK * m) if m else right
                inner = turn(kept, BLK)
                value = jnp.where(place < 20, east, west)
                value = jnp.where((place >= 4) & (place < 16), kept, value)
                value = jnp.where((place >= 24) | (place < 4), inner, value)
                dst[layers + m, at(t), :] = value

    def join_own(t, carry):
        src = pl.ds(pl.multiple_of(t * SUB - 2 * SUB, SUB), SUB)
        join_windows(t, src, kept_ref, left_ref, right_ref)
        return carry

    lax.fori_loop(first + 1, last, join_own, 0)
    every = slice(None)
    join_windows(edge, every, kept_edge_ref, left_edge_ref, right_edge_ref)
    join_windows(first + last - edge, every, kept_inner_ref, left_inner_ref, right_inner_ref)
    for copy in copies:
        copy.wait()

    def prepare(t, carry):
        def faces(n, here, above):
            we = 0.5 * (here + turn(here, -1))
            ws = 0.5 * (here + c_v[n, at(t, 1), :])
            wn = 0.5 * (here + c_v[n, at(t, -1), :])
            we_v[n, at(t), :] = we
            ws_v[n, at(t), :] = ws
            weight = we + turn(we, 1) + ws + wn
            if above is None:
                return weight, None
            wu = (0.5 * vertical_ratio) * (here + above)
            wu_v[n, at(t), :] = wu
            return weight + wu, wu

        def finish(n, here, weight):
            inside = here > 0.0
            inv_v[n, at(t), :] = jnp.where(inside, 1.0 / jnp.where(inside, weight, 1.0), 0.0)

        here = c_v[0, at(t), :]
        below = None
        for l in range(layers):
            above = c_v[l + 1, at(t), :] if l + 1 < layers else None
            weight, wu = faces(l, here, above)
            finish(l, here, weight if below is None else weight + below)
            here, below = above, wu
        bands = [c_v[layers + m, at(t), :] for m in range(FOLD)]
        weights = []
        for m in range(FOLD - 1):
            weights.append(faces(layers + m, bands[m], bands[m + 1]))
        weight, _ = faces(layers + FOLD - 1, bands[-1], None)
        wu = (0.5 * vertical_ratio) * (bands[-1] + turn(bands[0], -WIDE))
        wu = jnp.where(topmost, 0.0, wu)
        wu_v[layers + FOLD - 1, at(t), :] = wu
        weights.append((weight + wu, wu))
        below = jnp.where(bottommost, 0.0, turn(wu, WIDE))
        for m in range(FOLD):
            finish(layers + m, bands[m], weights[m][0] + below)
            below = weights[m][1]
        return carry

    group = ((lane + WIDE // 2 + LANES - 4) % LANES) // WIDE
    topmost = group == LANES // WIDE - 1
    bottommost = group == 0
    lax.fori_loop(first, last + 1, prepare, 0, unroll=UNROLL)

    def make_sweep(old, store):
        def flat(n, t, here):
            we = we_v[n, at(t), :]
            total = s_v[n, at(t), :] + we * turn(here, -1) + turn(we * here, 1)
            total = total + ws_v[n, at(t), :] * old[n, at(t, 1), :]
            return total + ws_v[n, at(t, -1), :] * old[n, at(t, -1), :]

        def sweep(t, carry):
            values = []
            bands = [old[layers + m, at(t), :] for m in range(FOLD)]
            wus = [wu_v[layers + m, at(t), :] for m in range(FOLD)]
            ups = bands[1:] + [turn(bands[0], -WIDE)]
            downs = [turn(wus[-1] * bands[-1], WIDE)]
            downs += [wus[m] * bands[m] for m in range(FOLD - 1)]
            for m in range(FOLD):
                total = flat(layers + m, t, bands[m]) + wus[m] * ups[m] + downs[m]
                values.append(total * inv_v[layers + m, at(t), :])
            extra = store.windows(t, values)
            below = None
            here = old[0, at(t), :]
            for l in range(layers):
                total = flat(l, t, here)
                if l:
                    total = total + below
                if l + 1 < layers:
                    above = old[l + 1, at(t), :]
                    wu = wu_v[l, at(t), :]
                    total = total + wu * above
                    below, here = wu * here, above
                store.layer(l, t, total * inv_v[l, at(t), :], extra)
            return carry

        return sweep

    class Keep:
        def __init__(self, new):
            self.new = new

        def windows(self, t, values):
            for m in range(FOLD):
                self.new[layers + m, at(t), :] = values[m]

        def layer(self, l, t, value, extra):
            self.new[l, at(t), :] = value

    class Finish:
        def windows(self, t, values):
            return [jnp.where(place < 16, value, turn(value, -BLK)) for value in values]

        def layer(self, l, t, value, extra):
            outer = extra[l % FOLD]
            if l >= FOLD:
                outer = turn(outer, -WIDE * (l // FOLD))
            value = jnp.where((lane >= 4) & (lane < LANES - 4), value, outer)
            out_ref[l, pl.ds(pl.multiple_of(t * SUB - 2 * SUB, SUB), SUB), :] = value

    pairs = (pa_v, pb_v)
    for k in range(SWEEPS - 1):
        lax.fori_loop(
            first, last + 1, make_sweep(pairs[k % 2], Keep(pairs[(k + 1) % 2])), 0, unroll=6
        )
    lax.fori_loop(
        first + 1, last, make_sweep(pairs[(SWEEPS - 1) % 2], Finish()), 0, unroll=UNROLL
    )


def polarize_kernel(
    tile_ref, me_ref, resist_ref, got_ref, depth_ref, girth_ref, bare_ref, current_ref, sent_ref, near_v, drive_v, sum_v
):
    layers = depth_ref.shape[1]
    rows, girth = bare_ref.shape[1:]
    step = pl.program_id(0)
    highest = lax.Precision.HIGHEST
    resist = resist_ref[0]
    lane = lane_ids(layers)
    row = lax.broadcasted_iota(jnp.int32, (layers, LANES), 0)

    @pl.when(step == 0)
    def _():
        packet = got_ref[tile_ref[me_ref[0]]]
        shell = jnp.zeros((layers, LANES), jnp.float32)
        for x in range(BLK):
            spread = jnp.broadcast_to(packet[x : x + 1, :], (layers, LANES))
            spread = pltpu.roll(spread, 0, 1, stride=BLK, stride_axis=0)
            spread = turn(spread, BLK * (x + 1) - BLK * layers)
            shell = jnp.where(lane // BLK == x, spread, shell)
        near_v[...] = jnp.dot(
            shell[:, : BLK * BLK],
            girth_ref[...],
            precision=highest,
            preferred_element_type=jnp.float32,
        )
        sum_v[...] = jnp.zeros_like(sum_v)

    drive_v[...] = jnp.dot(
        depth_ref[...], near_v[...], precision=lax.Precision.HIGH, preferred_element_type=jnp.float32
    )
    up = math.log2(math.e) / anodic_slope
    down = -math.log2(math.e) / cathodic_slope
    steep = resist / anodic_slope
    steep_down = resist / cathodic_slope
    coated = coated_conductance / (1.0 + coated_conductance * resist)
    chunk = 64

    def body(i, carry):
        at = pl.ds(pl.multiple_of(i * chunk, chunk), chunk)
        driving = drive_v[at, :]
        value = driving
        for n in range(NEWTON):
            anodic = jnp.exp2(value * up)
            cathodic = jnp.exp2(value * down)
            excess = resist * (anodic - cathodic)
            if n:
                excess = excess + (value - driving)
            slope = 1.0 + (steep * anodic + steep_down * cathodic)
            value = value - excess / slope
        bare_current = jnp.exp2(value * up) - jnp.exp2(value * down)
        current_ref[0, at, :] = jnp.where(bare_ref[0, at, :] != 0, bare_current, coated * driving)
        return carry

    lax.fori_loop(0, rows // chunk, body, 0)
    sum_v[...] += lax.dot_general(
        depth_ref[...],
        current_ref[0],
        (((0,), (0,)), ((), ())),
        precision=lax.Precision.HIGH,
        preferred_element_type=jnp.float32,
    )

    @pl.when(step == pl.num_programs(0) - 1)
    def _():
        cells = layers * BLK * BLK
        scale = math.sqrt(cells / (rows * girth * pl.num_programs(0)))
        back = scale * lax.dot_general(
            sum_v[...],
            girth_ref[...],
            (((1,), (1,)), ((), ())),
            precision=lax.Precision.HIGH,
            preferred_element_type=jnp.float32,
        )
        back = jnp.concatenate([back, jnp.zeros_like(back)], axis=1)
        lines = []
        for x in range(BLK):
            spread = turn(back, -BLK * x) if x else back
            spread = pltpu.roll(spread, 0, 1, stride=BLK, stride_axis=0)
            spread = jnp.where(lane // BLK == row, spread, 0.0)
            lines.append(jnp.sum(spread, axis=0, keepdims=True))
        sent_ref[...] = jnp.broadcast_to(jnp.concatenate(lines, axis=0)[None], sent_ref.shape)


def inject_kernel(table_ref, block_ref, got_ref, p_hbm, out_hbm, work_v, sem):
    layers = p_hbm.shape[0]
    per_row = LANES // BLK
    lane = lane_ids()
    piles = [table_ref[j] for j in range(CAP)]
    blocks = [block_ref[jnp.maximum(k, 0)] for k in piles]
    def window(ref, j):
        return ref.at[:, pl.ds(pl.multiple_of(blocks[j] // per_row * BLK, BLK), BLK), :]

    heads = []
    for j in range(CAP):
        head = piles[j] >= 0
        for i in range(j):
            head = head & jnp.logical_not(
                (piles[i] >= 0) & (blocks[i] // per_row == blocks[j] // per_row)
            )
        heads.append(head)
    for j in range(CAP):

        @pl.when(heads[j])
        def _():
            pltpu.make_async_copy(window(p_hbm, j), work_v.at[j], sem.at[0, j]).start()

    for j in range(CAP):

        @pl.when(heads[j])
        def _():
            pltpu.make_async_copy(window(p_hbm, j), work_v.at[j], sem.at[0, j]).wait()
            for i in range(j, CAP):

                @pl.when((piles[i] >= 0) & (blocks[i] // per_row == blocks[j] // per_row))
                def _():
                    start = blocks[i] % per_row * BLK
                    packet = inject_gain * got_ref[jnp.maximum(piles[i], 0)]
                    for l in range(layers):
                        moved = pltpu.roll(packet, (start + LANES - BLK * l) % LANES, 1)
                        inside = (lane >= start) & (lane < start + BLK)
                        work_v[j, l] = work_v[j, l] - jnp.where(inside, moved, 0.0)

            pltpu.make_async_copy(work_v.at[j], window(out_hbm, j), sem.at[1, j]).start()

    for j in range(CAP):

        @pl.when(heads[j])
        def _():
            pltpu.make_async_copy(work_v.at[j], window(out_hbm, j), sem.at[1, j]).wait()


def on_device(
    conductivity,
    source,
    potential_start,
    shell_to_depth,
    shell_to_girth,
    pile_resistance,
    coating_mask,
    pile_tile,
    pile_block,
):
    layers, rows, cols = conductivity.shape
    piles = pile_tile.shape[0]
    depth_cells, girth = coating_mask.shape[1:]
    both = ("gx", "gy")
    me = (lax.axis_index("gx") * lax.axis_size("gy") + lax.axis_index("gy")).astype(jnp.int32)
    me = me.reshape(1)
    smem = pl.BlockSpec(memory_space=pltpu.SMEM)
    vmem = pl.BlockSpec(memory_space=pltpu.VMEM)
    anywhere = pl.BlockSpec(memory_space=pl.ANY)
    f32 = jnp.float32
    three = (potential_start, conductivity, source)

    def pass_on(value, axis, up):
        count = lax.axis_size(axis)
        pairs = [(i, i + 1) for i in range(count - 1)]
        return lax.ppermute(value, axis, pairs if up else [(b, a) for a, b in pairs])

    edge_shape = jax.ShapeDtypeStruct((3, layers, SUB, cols), f32)
    corner = [
        pl.BlockSpec((layers, SUB, cols), lambda i, r=r: (0, r, 0)) for r in (rows // SUB - 1, 0)
    ]
    high, low = pl.pallas_call(
        edges_kernel,
        grid=(1,),
        in_specs=[corner[0]] * 3 + [corner[1]] * 3,
        out_specs=[pl.BlockSpec((3, layers, SUB, cols), lambda i: (0, 0, 0, 0))] * 2,
        out_shape=[edge_shape] * 2,
        name="edges",
    )(*three, *three)
    top = pass_on(high, "gx", True)
    bottom = pass_on(low, "gx", False)

    steps = 4
    packed_rows = rows + 2 * SUB
    part = pl.BlockSpec((layers, rows // steps, cols), lambda i: (0, i, 0))
    kept_shape = jax.ShapeDtypeStruct((3, FOLD, packed_rows, cols), f32)
    sent_shape = jax.ShapeDtypeStruct((3, packed_rows, cols), f32)
    kept, packed = pl.pallas_call(
        pack_kernel,
        grid=(steps,),
        in_specs=[part, part, part],
        out_specs=[
            pl.BlockSpec((3, FOLD, rows // steps, cols), lambda i: (0, 0, i, 0)),
            pl.BlockSpec((3, rows // steps, cols), lambda i: (0, i, 0)),
        ],
        out_shape=[kept_shape, sent_shape],
        cost_estimate=pl.CostEstimate(
            flops=6 * rows * cols * layers, bytes_accessed=16 * rows * cols * layers, transcendentals=0
        ),
        name="pack_strips",
    )(*three)
    whole = pl.BlockSpec((3, layers, SUB, cols), lambda i: (0, 0, 0, 0))
    kept, packed = pl.pallas_call(
        pack_edge_kernel,
        grid=(2,),
        in_specs=[whole, whole, anywhere, anywhere],
        out_specs=[
            pl.BlockSpec((3, FOLD, SUB, cols), lambda i: (0, 0, rows // SUB + i, 0)),
            pl.BlockSpec((3, SUB, cols), lambda i: (0, rows // SUB + i, 0)),
        ],
        out_shape=[kept_shape, sent_shape],
        input_output_aliases={2: 0, 3: 1},
        compiler_params=pltpu.CompilerParams(vmem_limit_bytes=53 << 20),
        name="pack_edges",
    )(top, bottom, kept, packed)
    packed, tile_later = lax.optimization_barrier((packed, pile_tile))
    table = pl.pallas_call(
        table_kernel,
        in_specs=[smem, smem],
        out_specs=smem,
        out_shape=jax.ShapeDtypeStruct((SUB,), jnp.int32),
        cost_estimate=pl.CostEstimate(flops=piles, bytes_accessed=8 * piles, transcendentals=0),
        name="table",
    )(tile_later, me)
    left = pass_on(packed, "gy", True)
    right = pass_on(packed, "gy", False)

    sent = pl.pallas_call(
        shells_kernel,
        in_specs=[smem, smem] + [anywhere] * 7,
        out_specs=vmem,
        out_shape=jax.ShapeDtypeStruct((piles, SUB, LANES), f32),
        scratch_shapes=[
            pltpu.VMEM((CAP, 3, 3, layers, SUB, LANES), f32),
            pltpu.VMEM((CAP, 3, 3, SUB, LANES), f32),
            pltpu.VMEM((8, layers // 2, 5 * SUB, LANES), f32),
            pltpu.SemaphoreType.DMA((CAP, 4, 3)),
        ],
        compiler_params=pltpu.CompilerParams(vmem_limit_bytes=SHELLS_LIMIT),
        name="shells",
    )(table, pile_block, *three, top, bottom, left, right)

    half_rows = rows // 2
    padded = pltpu.VMEM((layers + FOLD, half_rows + 5 * SUB, cols), f32)

    def sweep_half(half, edge, kept, left, right, before=None):
        def parts(*lead):
            zeros = (0,) * len(lead)

            def spec(height, index):
                return pl.BlockSpec(lead + (height, cols), lambda i: zeros + (index, 0))

            inner = half_rows // SUB - half
            return [spec(half_rows, half), spec(SUB, rows // SUB + half), spec(SUB, inner)]

        operands = [*three, edge] + [kept] * 3 + [left] * 3 + [right] * 3
        specs = [anywhere] * 4 + parts(3, FOLD) + parts(3) + parts(3)
        aliases = {}
        if before is not None:
            aliases = {len(operands): 0}
            operands.append(before)
            specs.append(anywhere)
        return pl.pallas_call(
            functools.partial(sweep_kernel, half),
            grid=(1,),
            in_specs=specs,
            out_specs=pl.BlockSpec((layers, half_rows, cols), lambda i: (0, half, 0)),
            out_shape=jax.ShapeDtypeStruct((layers, rows, cols), f32),
            input_output_aliases=aliases,
            scratch_shapes=[padded] * 8 + [pltpu.SemaphoreType.DMA((3, 2))],
            compiler_params=pltpu.CompilerParams(vmem_limit_bytes=VMEM_LIMIT),
            cost_estimate=pl.CostEstimate(
                flops=80 * half_rows * cols * layers,
                bytes_accessed=16 * half_rows * cols * layers,
                transcendentals=0,
            ),
            name="sweeps",
        )(*operands)

    sent, top, left_now, right_now = lax.optimization_barrier((sent, top, left, right))
    got = lax.all_to_all(sent, both, 0, 0, tiled=True)
    potential = sweep_half(0, top, kept, left_now, right_now)

    steps = 4
    part = pl.BlockSpec((1, depth_cells // steps, girth), lambda i: (0, i, 0))

    def full(*shape):
        return pl.BlockSpec(shape, lambda i: (0,) * len(shape))

    current, sent_back = pl.pallas_call(
        polarize_kernel,
        grid=(steps,),
        in_specs=[
            smem,
            smem,
            smem,
            full(piles, SUB, LANES),
            pl.BlockSpec((depth_cells // steps, layers), lambda i: (i, 0)),
            full(BLK * BLK, girth),
            part,
        ],
        out_specs=[part, full(piles, SUB, LANES)],
        out_shape=[
            jax.ShapeDtypeStruct((1, depth_cells, girth), f32),
            jax.ShapeDtypeStruct((piles, SUB, LANES), f32),
        ],
        scratch_shapes=[
            pltpu.VMEM((layers, girth), f32),
            pltpu.VMEM((depth_cells // steps, girth), f32),
            pltpu.VMEM((layers, girth), f32),
        ],
        compiler_params=pltpu.CompilerParams(vmem_limit_bytes=SHELLS_LIMIT),
        name="polarize",
    )(pile_tile, me, pile_resistance, got, shell_to_depth, shell_to_girth, coating_mask)

    sent_back, bottom, potential = lax.optimization_barrier((sent_back, bottom, potential))
    got_back = lax.all_to_all(sent_back, both, 0, 0, tiled=True)
    potential = sweep_half(1, bottom, kept, left_now, right_now, potential)

    potential = pl.pallas_call(
        inject_kernel,
        in_specs=[smem, smem, vmem, anywhere],
        out_specs=anywhere,
        out_shape=jax.ShapeDtypeStruct((layers, rows, cols), f32),
        input_output_aliases={3: 0},
        scratch_shapes=[
            pltpu.VMEM((CAP, layers, SUB, LANES), f32),
            pltpu.SemaphoreType.DMA((2, CAP)),
        ],
        compiler_params=pltpu.CompilerParams(vmem_limit_bytes=8 << 20),
        name="inject",
    )(table, pile_block, got_back, potential)
    return (potential, current)


def solution(mesh):
    placed = (
        P(None, "gx", "gy"),
        P(None, "gx", "gy"),
        P(None, "gx", "gy"),
        P(),
        P(),
        P(("gx", "gy")),
        P(("gx", "gy"), None, None),
        P(),
        P(),
    )
    return jax.shard_map(
        on_device,
        mesh=mesh,
        in_specs=placed,
        out_specs=(P(None, "gx", "gy"), P(("gx", "gy"), None, None)),
        check_vma=False,
    )
```

```python
import functools
import math

import jax
import jax.numpy as jnp
from jax import lax
from jax.experimental import pallas as pl
from jax.experimental.pallas import tpu as pltpu
from jax.sharding import PartitionSpec as P

BLK = 8
CAP = 4
SWEEPS = 4
NEWTON = 3
LANES = 128
SUB = 8
VMEM_LIMIT = 56 << 20
SHELLS_LIMIT = 52 << 20
UNROLL = 2

vertical_ratio = 0.25
inject_gain = 0.5
anodic_slope = 1.2
cathodic_slope = 0.8
coated_conductance = 0.05


def turn(x, shift):
    return pltpu.roll(x, shift % LANES, 1)


def lane_ids(rows=SUB):
    return lax.broadcasted_iota(jnp.int32, (rows, LANES), 1)


WIDE = 32
FOLD = 4


def pack_rows(load, keep):
    lane = lane_ids()
    bands = []
    for m in range(FOLD):
        packed = load(m)
        for g in range(1, LANES // WIDE):
            moved = turn(load(m + FOLD * g), WIDE * g)
            packed = jnp.where(((lane + WIDE // 2) % LANES) // WIDE == g, moved, packed)
        keep(m, packed)
        bands.append(packed)
    part = ((lane + 4) % WIDE) // BLK
    sent = bands[0]
    for m in range(1, FOLD):
        sent = jnp.where(part == m, turn(bands[m], BLK * m), sent)
    return sent


def pack_pair(load, keep, right_ref, left_ref, at):
    rightward = lane_ids() // FOLD % 2 == (WIDE - 12 - WIDE // 2) // FOLD % 2
    sides = [
        [pack_rows(functools.partial(load, odd, i), functools.partial(keep, odd, i)) for i in range(3)]
        for odd in range(2)
    ]
    pairs = [(sides[0][0], sides[0][1]), (sides[1][0], sides[1][1]), (sides[0][2], sides[1][2])]
    for plane, (one, two) in enumerate(pairs):
        right_ref[plane, at, :] = jnp.where(rightward, one, turn(two, FOLD))
        left_ref[plane, at, :] = jnp.where(rightward, turn(two, -FOLD), one)


def table_kernel(tile_ref, me_ref, table_ref):
    def look(k, count):
        table_ref[jnp.minimum(count, SUB - 1)] = k
        return count + (tile_ref[k] == me_ref[0]).astype(jnp.int32)

    count = lax.fori_loop(0, tile_ref.shape[0], look, jnp.int32(0), unroll=16)
    for j in range(SUB):
        table_ref[j] = jnp.where(j < count, table_ref[j], -1)


def pack_kernel(p_ref, c_ref, s_ref, kept_ref, right_ref, left_ref):
    refs = (p_ref, c_ref, s_ref)

    def body(u, carry):
        def rows(odd):
            return pl.ds(pl.multiple_of(u * 2 * SUB, SUB) + odd * SUB, SUB)

        def load(odd, i, l):
            return refs[i][l, rows(odd), :]

        def keep(odd, i, m, value):
            kept_ref[i, m, rows(odd), :] = value

        pack_pair(load, keep, right_ref, left_ref, pl.ds(pl.multiple_of(u * SUB, SUB), SUB))
        return carry

    lax.fori_loop(0, p_ref.shape[1] // (2 * SUB), body, 0)


def edges_kernel(*refs):
    high_ref, low_ref = refs[6:]
    for i in range(3):
        high_ref[i] = refs[i][...]
        low_ref[i] = refs[3 + i][...]


def pack_edge_kernel(
    top_ref, bottom_ref, kept_hbm, right_hbm, left_hbm, kept_ref, right_ref, left_ref
):
    refs = (top_ref, bottom_ref)

    def load(odd, i, l):
        return refs[odd][i, l]

    def keep(odd, i, m, value):
        kept_ref[i, m, odd * SUB : (odd + 1) * SUB, :] = value

    pack_pair(load, keep, right_ref, left_ref, slice(None))


NEAR = 16
HALF = LANES // 2


def shells_kernel(
    table_ref,
    block_ref,
    p_hbm,
    c_hbm,
    s_hbm,
    top_hbm,
    bottom_hbm,
    left_hbm,
    right_hbm,
    sent_ref,
    tile_v,
    side_v,
    work_v,
    sem,
):
    layers, rows, _ = p_hbm.shape
    folds = layers // 2
    per_row = LANES // BLK
    lane = lane_ids()
    sources = (p_hbm, c_hbm, s_hbm)
    piles = [table_ref[j] for j in range(CAP)]
    filled = [k >= 0 for k in piles]
    blocks = [block_ref[jnp.maximum(k, 0)] for k in piles]
    row_of = [lax.div(b, per_row) for b in blocks]
    col_of = [lax.rem(b, per_row) for b in blocks]
    border = [
        filled[j] & ((col_of[j] == 0) | (col_of[j] == per_row - 1)) for j in range(CAP)
    ]

    def main_copy(i, j, d):
        where = pl.ds(pl.multiple_of((row_of[j] + d - 1) * SUB, SUB), SUB)
        return pltpu.make_async_copy(
            sources[i].at[:, where, :], tile_v.at[j, i, d], sem.at[j, i, d]
        )

    def edge_copy(i, j, d):
        ref = top_hbm if d == 0 else bottom_hbm
        return pltpu.make_async_copy(ref.at[i], tile_v.at[j, i, d], sem.at[j, i, d])

    def packed_tile(j, d):
        tile = row_of[j] + d - 1
        above = jnp.where(tile >= rows // SUB, rows // SUB + 1, tile)
        return jnp.where(tile < 0, rows // SUB, above)

    def side_copy(ref, j, d):
        where = pl.ds(pl.multiple_of(lax.div(packed_tile(j, d), 2) * SUB, SUB), SUB)
        return pltpu.make_async_copy(ref.at[:, where, :], side_v.at[j, d], sem.at[j, 3, d])

    def each_copy(j, act):
        @pl.when(filled[j])
        def _():
            for d in range(3):
                for i in range(3):
                    if d == 1:
                        act(main_copy(i, j, d))
                        continue
                    outside = row_of[j] == (0 if d == 0 else rows // SUB - 1)

                    @pl.when(outside)
                    def _():
                        act(edge_copy(i, j, d))

                    @pl.when(jnp.logical_not(outside))
                    def _():
                        act(main_copy(i, j, d))

        @pl.when(border[j] & (col_of[j] == 0))
        def _():
            for d in range(3):
                act(side_copy(left_hbm, j, d))

        @pl.when(border[j] & (col_of[j] > 0))
        def _():
            for d in range(3):
                act(side_copy(right_hbm, j, d))

    for j in range(CAP):
        each_copy(j, lambda copy: copy.start())
    sent_ref[...] = jnp.zeros_like(sent_ref)
    pa, c_v, s_v, pb, we_v, ws_v, wu_v, inv_v = (work_v.at[i] for i in range(8))
    zero = jnp.zeros((SUB, LANES), jnp.float32)
    for t in (0, 4):
        for ref in (pa, c_v, pb, ws_v):
            for m in range(folds):
                ref[m, t * SUB : (t + 1) * SUB, :] = zero
    for j in range(CAP):
        each_copy(j, lambda copy: copy.wait())

    slot = (lane % HALF) // NEAR
    upper = lane >= HALF
    shifts = [[(HALF * h + NEAR * j + 4 + LANES - BLK * col_of[j]) % LANES for h in (0, 1)] for j in range(CAP)]
    arrays = (pa, c_v, s_v)

    def gather(d, carry):
        at = pl.ds(pl.multiple_of((d + 1) * SUB, SUB), SUB)
        for i in range(3):
            for m in range(folds):
                value = zero
                for j in range(CAP):
                    low = pltpu.roll(tile_v[j, i, d, m], shifts[j][0], 1)
                    high = pltpu.roll(tile_v[j, i, d, m + folds], shifts[j][1], 1)
                    value = jnp.where(
                        (slot == j) & filled[j], jnp.where(upper, high, low), value
                    )
                arrays[i][m, at, :] = value
        return carry

    lax.fori_loop(0, 3, gather, 0)
    for j in range(CAP):

        @pl.when(border[j])
        def _():
            first = col_of[j] == 0
            begin = jnp.where(first, 0, NEAR - 4)
            back = jnp.where(first, 12, 4)

            def mend(d, carry):
                at = pl.ds(pl.multiple_of((d + 1) * SUB, SUB), SUB)
                odd = lax.rem(packed_tile(j, d), 2)
                apart = jnp.where(first, -FOLD, FOLD)
                for i in range(3):
                    side = side_v[j, d, 2 if i == 2 else odd]
                    skip = (0, apart, apart * odd)[i]
                    for m in range(folds):
                        value = arrays[i][m, at, :]
                        for h in (0, 1):
                            l = m + folds * h
                            base = HALF * h + NEAR * j
                            known = base + WIDE // 2 - WIDE * (l // FOLD) - BLK * (l % FOLD)
                            moved = pltpu.roll(side, (known + 2 * LANES - back + skip) % LANES, 1)
                            here = (lane >= base + begin) & (lane < base + begin + 4)
                            value = jnp.where(here, moved, value)
                        arrays[i][m, at, :] = value
                return carry

            lax.fori_loop(0, 3, mend, 0)

    def span(t, shift=0):
        return slice(t * SUB + shift, (t + 1) * SUB + shift)

    for t in (1, 2, 3):
        cells = [c_v[m, span(t), :] for m in range(folds)]
        weights, wus = [], []
        for m in range(folds):
            here = cells[m]
            we = 0.5 * (here + turn(here, -1))
            ws = 0.5 * (here + c_v[m, span(t, 1), :])
            wn = 0.5 * (here + c_v[m, span(t, -1), :])
            above = cells[m + 1] if m + 1 < folds else turn(cells[0], HALF)
            wu = (0.5 * vertical_ratio) * (here + above)
            if m + 1 == folds:
                wu = jnp.where(upper, 0.0, wu)
            we_v[m, span(t), :] = we
            ws_v[m, span(t), :] = ws
            wu_v[m, span(t), :] = wu
            weights.append(we + turn(we, 1) + ws + wn + wu)
            wus.append(wu)
        for m in range(folds):
            below = wus[m - 1] if m else turn(wus[-1], HALF)
            inside = cells[m] > 0.0
            weight = jnp.where(inside, weights[m] + below, 1.0)
            inv_v[m, span(t), :] = jnp.where(inside, 1.0 / weight, 0.0)

    def sweep(old, new, t):
        values = [old[m, span(t), :] for m in range(folds)]
        wus = [wu_v[m, span(t), :] for m in range(folds)]
        for m in range(folds):
            here = values[m]
            we = we_v[m, span(t), :]
            total = s_v[m, span(t), :] + we * turn(here, -1) + turn(we * here, 1)
            total = total + ws_v[m, span(t), :] * old[m, span(t, 1), :]
            total = total + ws_v[m, span(t, -1), :] * old[m, span(t, -1), :]
            above = values[m + 1] if m + 1 < folds else turn(values[0], HALF)
            below = wus[m - 1] * values[m - 1] if m else turn(wus[-1] * values[-1], HALF)
            total = total + wus[m] * above + below
            new[m, span(t), :] = total * inv_v[m, span(t), :]

    pairs = (pa, pb)
    for k in range(SWEEPS):
        for t in (1, 2, 3) if k < SWEEPS - 1 else (2,):
            sweep(pairs[k % 2], pairs[(k + 1) % 2], t)
    done = pairs[SWEEPS % 2]
    for j in range(CAP):

        @pl.when(filled[j])
        def _():
            packet = zero
            for l in range(layers):
                group = layers - 1 - l
                begin = HALF * (l // folds) + NEAR * j + 4
                moved = turn(done[l % folds, span(2), :], BLK * group - begin)
                packet = jnp.where(lane // BLK == group, moved, packet)
            sent_ref[piles[j]] = packet


def sweep_kernel(
    half,
    p_hbm,
    c_hbm,
    s_hbm,
    edge_hbm,
    kept_ref,
    kept_edge_ref,
    kept_inner_ref,
    left_ref,
    left_edge_ref,
    left_inner_ref,
    right_ref,
    right_edge_ref,
    right_inner_ref,
    *rest,
):
    out_ref, c_v, s_v, pa_v, pb_v, we_v, ws_v, wu_v, inv_v, sem = rest[-10:]
    layers = p_hbm.shape[0]
    tile_rows = out_ref.shape[1]
    tiles = tile_rows // SUB
    first, last = 1, tiles + 2
    edge = last if half else first
    lane = lane_ids()
    place = (lane + WIDE // 2) % WIDE
    arrays = (pa_v, c_v, s_v)
    copies = []
    own = pl.ds(0, layers)
    for i, (src, dst) in enumerate(zip((p_hbm, c_hbm, s_hbm), arrays)):
        begin = half * (tile_rows - SUB)
        into = SUB if half else 2 * SUB
        copies.append(
            pltpu.make_async_copy(
                src.at[:, pl.ds(begin, tile_rows + SUB), :],
                dst.at[own, pl.ds(into, tile_rows + SUB), :],
                sem.at[i, 0],
            )
        )
        copies.append(
            pltpu.make_async_copy(
                edge_hbm.at[i], dst.at[own, pl.ds(edge * SUB, SUB), :], sem.at[i, 1]
            )
        )
    for copy in copies:
        copy.start()
    zero = jnp.zeros((SUB, LANES), jnp.float32)
    for t in (0, last + 1):
        for ref in (c_v, pa_v, pb_v, ws_v):
            for l in range(layers + FOLD):
                ref[l, t * SUB : (t + 1) * SUB, :] = zero

    def at(t, shift=0):
        if shift:
            return pl.ds(t * SUB + shift, SUB)
        return pl.ds(pl.multiple_of(t * SUB, SUB), SUB)

    def join_windows(t, odd, src, at_u, kept_rows, left_rows, right_rows):
        for i, dst in enumerate(arrays):
            left = left_rows[2 if i == 2 else odd, at_u, :]
            right = right_rows[2 if i == 2 else odd, at_u, :]
            apart = (0, FOLD, FOLD * odd)[i]
            for m in range(FOLD):
                kept = kept_rows[i, m, src, :]
                west = turn(left, BLK - BLK * m - apart) if m != 1 or apart else left
                east = turn(right, apart - BLK * m) if m or apart else right
                inner = turn(kept, BLK)
                value = jnp.where(place < 20, east, west)
                value = jnp.where((place >= 4) & (place < 16), kept, value)
                value = jnp.where((place >= 24) | (place < 4), inner, value)
                dst[layers + m, at(t), :] = value

    def join_own(u, carry):
        at_u = pl.ds(pl.multiple_of(u * SUB, SUB), SUB)
        for odd in range(2):
            src = pl.ds(pl.multiple_of(u * 2 * SUB, SUB) + odd * SUB, SUB)
            join_windows(2 * u + odd + 2, odd, src, at_u, kept_ref, left_ref, right_ref)
        return carry

    lax.fori_loop(0, tiles // 2, join_own, 0)
    every = slice(None)
    join_windows(edge, half, every, every, kept_edge_ref, left_edge_ref, right_edge_ref)
    join_windows(
        first + last - edge, half, every, every, kept_inner_ref, left_inner_ref, right_inner_ref
    )
    for copy in copies:
        copy.wait()

    def prepare(t, carry):
        def faces(n, here, above):
            we = 0.5 * (here + turn(here, -1))
            ws = 0.5 * (here + c_v[n, at(t, 1), :])
            wn = 0.5 * (here + c_v[n, at(t, -1), :])
            we_v[n, at(t), :] = we
            ws_v[n, at(t), :] = ws
            weight = we + turn(we, 1) + ws + wn
            if above is None:
                return weight, None
            wu = (0.5 * vertical_ratio) * (here + above)
            wu_v[n, at(t), :] = wu
            return weight + wu, wu

        def finish(n, here, weight):
            inside = here > 0.0
            inv_v[n, at(t), :] = jnp.where(inside, 1.0 / jnp.where(inside, weight, 1.0), 0.0)

        here = c_v[0, at(t), :]
        below = None
        for l in range(layers):
            above = c_v[l + 1, at(t), :] if l + 1 < layers else None
            weight, wu = faces(l, here, above)
            finish(l, here, weight if below is None else weight + below)
            here, below = above, wu
        bands = [c_v[layers + m, at(t), :] for m in range(FOLD)]
        weights = []
        for m in range(FOLD - 1):
            weights.append(faces(layers + m, bands[m], bands[m + 1]))
        weight, _ = faces(layers + FOLD - 1, bands[-1], None)
        wu = (0.5 * vertical_ratio) * (bands[-1] + turn(bands[0], -WIDE))
        wu = jnp.where(topmost, 0.0, wu)
        wu_v[layers + FOLD - 1, at(t), :] = wu
        weights.append((weight + wu, wu))
        below = jnp.where(bottommost, 0.0, turn(wu, WIDE))
        for m in range(FOLD):
            finish(layers + m, bands[m], weights[m][0] + below)
            below = weights[m][1]
        return carry

    group = ((lane + WIDE // 2 + LANES - 4) % LANES) // WIDE
    topmost = group == LANES // WIDE - 1
    bottommost = group == 0
    lax.fori_loop(first, last + 1, prepare, 0, unroll=UNROLL)

    def make_sweep(old, store):
        def flat(n, t, here):
            we = we_v[n, at(t), :]
            total = s_v[n, at(t), :] + we * turn(here, -1) + turn(we * here, 1)
            total = total + ws_v[n, at(t), :] * old[n, at(t, 1), :]
            return total + ws_v[n, at(t, -1), :] * old[n, at(t, -1), :]

        def sweep(t, carry):
            values = []
            bands = [old[layers + m, at(t), :] for m in range(FOLD)]
            wus = [wu_v[layers + m, at(t), :] for m in range(FOLD)]
            ups = bands[1:] + [turn(bands[0], -WIDE)]
            downs = [turn(wus[-1] * bands[-1], WIDE)]
            downs += [wus[m] * bands[m] for m in range(FOLD - 1)]
            for m in range(FOLD):
                total = flat(layers + m, t, bands[m]) + wus[m] * ups[m] + downs[m]
                values.append(total * inv_v[layers + m, at(t), :])
            extra = store.windows(t, values)
            below = None
            here = old[0, at(t), :]
            for l in range(layers):
                total = flat(l, t, here)
                if l:
                    total = total + below
                if l + 1 < layers:
                    above = old[l + 1, at(t), :]
                    wu = wu_v[l, at(t), :]
                    total = total + wu * above
                    below, here = wu * here, above
                store.layer(l, t, total * inv_v[l, at(t), :], extra)
            return carry

        return sweep

    class Keep:
        def __init__(self, new):
            self.new = new

        def windows(self, t, values):
            for m in range(FOLD):
                self.new[layers + m, at(t), :] = values[m]

        def layer(self, l, t, value, extra):
            self.new[l, at(t), :] = value

    class Finish:
        def windows(self, t, values):
            return [jnp.where(place < 16, value, turn(value, -BLK)) for value in values]

        def layer(self, l, t, value, extra):
            outer = extra[l % FOLD]
            if l >= FOLD:
                outer = turn(outer, -WIDE * (l // FOLD))
            value = jnp.where((lane >= 4) & (lane < LANES - 4), value, outer)
            out_ref[l, pl.ds(pl.multiple_of(t * SUB - 2 * SUB, SUB), SUB), :] = value

    pairs = (pa_v, pb_v)
    for k in range(SWEEPS - 1):
        lax.fori_loop(
            first, last + 1, make_sweep(pairs[k % 2], Keep(pairs[(k + 1) % 2])), 0, unroll=6
        )
    lax.fori_loop(
        first + 1, last, make_sweep(pairs[(SWEEPS - 1) % 2], Finish()), 0, unroll=UNROLL
    )


def polarize_kernel(
    tile_ref, me_ref, resist_ref, got_ref, depth_ref, girth_ref, bare_ref, current_ref, sent_ref, near_v, drive_v, sum_v
):
    layers = depth_ref.shape[1]
    rows, girth = bare_ref.shape[1:]
    step = pl.program_id(0)
    highest = lax.Precision.HIGHEST
    resist = resist_ref[0]
    lane = lane_ids(layers)
    row = lax.broadcasted_iota(jnp.int32, (layers, LANES), 0)

    @pl.when(step == 0)
    def _():
        packet = got_ref[tile_ref[me_ref[0]]]
        shell = jnp.zeros((layers, LANES), jnp.float32)
        for x in range(BLK):
            spread = jnp.broadcast_to(packet[x : x + 1, :], (layers, LANES))
            spread = pltpu.roll(spread, 0, 1, stride=BLK, stride_axis=0)
            spread = turn(spread, BLK * (x + 1) - BLK * layers)
            shell = jnp.where(lane // BLK == x, spread, shell)
        near_v[...] = jnp.dot(
            shell[:, : BLK * BLK],
            girth_ref[...],
            precision=highest,
            preferred_element_type=jnp.float32,
        )
        sum_v[...] = jnp.zeros_like(sum_v)

    drive_v[...] = jnp.dot(
        depth_ref[...], near_v[...], precision=lax.Precision.HIGH, preferred_element_type=jnp.float32
    )
    up = math.log2(math.e) / anodic_slope
    down = -math.log2(math.e) / cathodic_slope
    steep = resist / anodic_slope
    steep_down = resist / cathodic_slope
    coated = coated_conductance / (1.0 + coated_conductance * resist)
    chunk = 64

    def body(i, carry):
        at = pl.ds(pl.multiple_of(i * chunk, chunk), chunk)
        driving = drive_v[at, :]
        value = driving
        for n in range(NEWTON):
            anodic = jnp.exp2(value * up)
            cathodic = jnp.exp2(value * down)
            excess = resist * (anodic - cathodic)
            if n:
                excess = excess + (value - driving)
            slope = 1.0 + (steep * anodic + steep_down * cathodic)
            value = value - excess / slope
        bare_current = jnp.exp2(value * up) - jnp.exp2(value * down)
        current_ref[0, at, :] = jnp.where(bare_ref[0, at, :] != 0, bare_current, coated * driving)
        return carry

    lax.fori_loop(0, rows // chunk, body, 0)
    sum_v[...] += lax.dot_general(
        depth_ref[...],
        current_ref[0],
        (((0,), (0,)), ((), ())),
        precision=lax.Precision.HIGH,
        preferred_element_type=jnp.float32,
    )

    @pl.when(step == pl.num_programs(0) - 1)
    def _():
        cells = layers * BLK * BLK
        scale = math.sqrt(cells / (rows * girth * pl.num_programs(0)))
        back = scale * lax.dot_general(
            sum_v[...],
            girth_ref[...],
            (((1,), (1,)), ((), ())),
            precision=lax.Precision.HIGH,
            preferred_element_type=jnp.float32,
        )
        back = jnp.concatenate([back, jnp.zeros_like(back)], axis=1)
        lines = []
        for x in range(BLK):
            spread = turn(back, -BLK * x) if x else back
            spread = pltpu.roll(spread, 0, 1, stride=BLK, stride_axis=0)
            spread = jnp.where(lane // BLK == row, spread, 0.0)
            lines.append(jnp.sum(spread, axis=0, keepdims=True))
        sent_ref[...] = jnp.broadcast_to(jnp.concatenate(lines, axis=0)[None], sent_ref.shape)


def inject_kernel(table_ref, block_ref, got_ref, p_hbm, out_hbm, work_v, sem):
    layers = p_hbm.shape[0]
    per_row = LANES // BLK
    lane = lane_ids()
    piles = [table_ref[j] for j in range(CAP)]
    blocks = [block_ref[jnp.maximum(k, 0)] for k in piles]
    def window(ref, j):
        return ref.at[:, pl.ds(pl.multiple_of(blocks[j] // per_row * BLK, BLK), BLK), :]

    heads = []
    for j in range(CAP):
        head = piles[j] >= 0
        for i in range(j):
            head = head & jnp.logical_not(
                (piles[i] >= 0) & (blocks[i] // per_row == blocks[j] // per_row)
            )
        heads.append(head)
    for j in range(CAP):

        @pl.when(heads[j])
        def _():
            pltpu.make_async_copy(window(p_hbm, j), work_v.at[j], sem.at[0, j]).start()

    for j in range(CAP):

        @pl.when(heads[j])
        def _():
            pltpu.make_async_copy(window(p_hbm, j), work_v.at[j], sem.at[0, j]).wait()
            for i in range(j, CAP):

                @pl.when((piles[i] >= 0) & (blocks[i] // per_row == blocks[j] // per_row))
                def _():
                    start = blocks[i] % per_row * BLK
                    packet = inject_gain * got_ref[jnp.maximum(piles[i], 0)]
                    for l in range(layers):
                        moved = pltpu.roll(packet, (start + LANES - BLK * l) % LANES, 1)
                        inside = (lane >= start) & (lane < start + BLK)
                        work_v[j, l] = work_v[j, l] - jnp.where(inside, moved, 0.0)

            pltpu.make_async_copy(work_v.at[j], window(out_hbm, j), sem.at[1, j]).start()

    for j in range(CAP):

        @pl.when(heads[j])
        def _():
            pltpu.make_async_copy(work_v.at[j], window(out_hbm, j), sem.at[1, j]).wait()


def on_device(
    conductivity,
    source,
    potential_start,
    shell_to_depth,
    shell_to_girth,
    pile_resistance,
    coating_mask,
    pile_tile,
    pile_block,
):
    layers, rows, cols = conductivity.shape
    piles = pile_tile.shape[0]
    depth_cells, girth = coating_mask.shape[1:]
    both = ("gx", "gy")
    me = (lax.axis_index("gx") * lax.axis_size("gy") + lax.axis_index("gy")).astype(jnp.int32)
    me = me.reshape(1)
    smem = pl.BlockSpec(memory_space=pltpu.SMEM)
    vmem = pl.BlockSpec(memory_space=pltpu.VMEM)
    anywhere = pl.BlockSpec(memory_space=pl.ANY)
    f32 = jnp.float32
    three = (potential_start, conductivity, source)

    def pass_on(value, axis, up):
        count = lax.axis_size(axis)
        pairs = [(i, i + 1) for i in range(count - 1)]
        return lax.ppermute(value, axis, pairs if up else [(b, a) for a, b in pairs])

    edge_shape = jax.ShapeDtypeStruct((3, layers, SUB, cols), f32)
    corner = [
        pl.BlockSpec((layers, SUB, cols), lambda i, r=r: (0, r, 0)) for r in (rows // SUB - 1, 0)
    ]
    high, low = pl.pallas_call(
        edges_kernel,
        grid=(1,),
        in_specs=[corner[0]] * 3 + [corner[1]] * 3,
        out_specs=[pl.BlockSpec((3, layers, SUB, cols), lambda i: (0, 0, 0, 0))] * 2,
        out_shape=[edge_shape] * 2,
        name="edges",
    )(*three, *three)
    top = pass_on(high, "gx", True)
    bottom = pass_on(low, "gx", False)

    steps = 4
    packed_rows = rows + 2 * SUB
    part = pl.BlockSpec((layers, rows // steps, cols), lambda i: (0, i, 0))
    kept_shape = jax.ShapeDtypeStruct((3, FOLD, packed_rows, cols), f32)
    sent_shape = jax.ShapeDtypeStruct((3, packed_rows // 2, cols), f32)
    message = pl.BlockSpec((3, rows // steps // 2, cols), lambda i: (0, i, 0))
    kept, rightward, leftward = pl.pallas_call(
        pack_kernel,
        grid=(steps,),
        in_specs=[part, part, part],
        out_specs=[
            pl.BlockSpec((3, FOLD, rows // steps, cols), lambda i: (0, 0, i, 0)),
            message,
            message,
        ],
        out_shape=[kept_shape, sent_shape, sent_shape],
        cost_estimate=pl.CostEstimate(
            flops=6 * rows * cols * layers, bytes_accessed=16 * rows * cols * layers, transcendentals=0
        ),
        name="pack_strips",
    )(*three)
    whole = pl.BlockSpec((3, layers, SUB, cols), lambda i: (0, 0, 0, 0))
    message = pl.BlockSpec((3, SUB, cols), lambda i: (0, rows // SUB // 2, 0))
    kept, rightward, leftward = pl.pallas_call(
        pack_edge_kernel,
        grid=(1,),
        in_specs=[whole, whole, anywhere, anywhere, anywhere],
        out_specs=[
            pl.BlockSpec((3, FOLD, 2 * SUB, cols), lambda i: (0, 0, rows // SUB // 2, 0)),
            message,
            message,
        ],
        out_shape=[kept_shape, sent_shape, sent_shape],
        input_output_aliases={2: 0, 3: 1, 4: 2},
        compiler_params=pltpu.CompilerParams(vmem_limit_bytes=53 << 20),
        name="pack_edges",
    )(top, bottom, kept, rightward, leftward)
    rightward, tile_later = lax.optimization_barrier((rightward, pile_tile))
    table = pl.pallas_call(
        table_kernel,
        in_specs=[smem, smem],
        out_specs=smem,
        out_shape=jax.ShapeDtypeStruct((SUB,), jnp.int32),
        cost_estimate=pl.CostEstimate(flops=piles, bytes_accessed=8 * piles, transcendentals=0),
        name="table",
    )(tile_later, me)
    left = pass_on(rightward, "gy", True)
    right = pass_on(leftward, "gy", False)

    sent = pl.pallas_call(
        shells_kernel,
        in_specs=[smem, smem] + [anywhere] * 7,
        out_specs=vmem,
        out_shape=jax.ShapeDtypeStruct((piles, SUB, LANES), f32),
        scratch_shapes=[
            pltpu.VMEM((CAP, 3, 3, layers, SUB, LANES), f32),
            pltpu.VMEM((CAP, 3, 3, SUB, LANES), f32),
            pltpu.VMEM((8, layers // 2, 5 * SUB, LANES), f32),
            pltpu.SemaphoreType.DMA((CAP, 4, 3)),
        ],
        compiler_params=pltpu.CompilerParams(vmem_limit_bytes=SHELLS_LIMIT),
        name="shells",
    )(table, pile_block, *three, top, bottom, left, right)

    half_rows = rows // 2
    padded = pltpu.VMEM((layers + FOLD, half_rows + 5 * SUB, cols), f32)

    def sweep_half(half, edge, kept, left, right, before=None):
        def parts(lead, height, *blocks):
            zeros = (0,) * len(lead)

            def spec(height, index):
                return pl.BlockSpec(lead + (height, cols), lambda i: zeros + (index, 0))

            return [spec(height, half), spec(SUB, blocks[0]), spec(SUB, blocks[1])]

        tiles = rows // SUB
        kept_parts = parts((3, FOLD), half_rows, tiles + half, tiles // 2 - half)
        sent_parts = parts((3,), half_rows // 2, tiles // 2, tiles // 4 - half)
        operands = [*three, edge] + [kept] * 3 + [left] * 3 + [right] * 3
        specs = [anywhere] * 4 + kept_parts + sent_parts + sent_parts
        aliases = {}
        if before is not None:
            aliases = {len(operands): 0}
            operands.append(before)
            specs.append(anywhere)
        return pl.pallas_call(
            functools.partial(sweep_kernel, half),
            grid=(1,),
            in_specs=specs,
            out_specs=pl.BlockSpec((layers, half_rows, cols), lambda i: (0, half, 0)),
            out_shape=jax.ShapeDtypeStruct((layers, rows, cols), f32),
            input_output_aliases=aliases,
            scratch_shapes=[padded] * 8 + [pltpu.SemaphoreType.DMA((3, 2))],
            compiler_params=pltpu.CompilerParams(vmem_limit_bytes=VMEM_LIMIT),
            cost_estimate=pl.CostEstimate(
                flops=80 * half_rows * cols * layers,
                bytes_accessed=16 * half_rows * cols * layers,
                transcendentals=0,
            ),
            name="sweeps",
        )(*operands)

    sent, top, left_now, right_now = lax.optimization_barrier((sent, top, left, right))
    got = lax.all_to_all(sent, both, 0, 0, tiled=True)
    potential = sweep_half(0, top, kept, left_now, right_now)

    steps = 4
    part = pl.BlockSpec((1, depth_cells // steps, girth), lambda i: (0, i, 0))

    def full(*shape):
        return pl.BlockSpec(shape, lambda i: (0,) * len(shape))

    current, sent_back = pl.pallas_call(
        polarize_kernel,
        grid=(steps,),
        in_specs=[
            smem,
            smem,
            smem,
            full(piles, SUB, LANES),
            pl.BlockSpec((depth_cells // steps, layers), lambda i: (i, 0)),
            full(BLK * BLK, girth),
            part,
        ],
        out_specs=[part, full(piles, SUB, LANES)],
        out_shape=[
            jax.ShapeDtypeStruct((1, depth_cells, girth), f32),
            jax.ShapeDtypeStruct((piles, SUB, LANES), f32),
        ],
        scratch_shapes=[
            pltpu.VMEM((layers, girth), f32),
            pltpu.VMEM((depth_cells // steps, girth), f32),
            pltpu.VMEM((layers, girth), f32),
        ],
        compiler_params=pltpu.CompilerParams(vmem_limit_bytes=SHELLS_LIMIT),
        name="polarize",
    )(pile_tile, me, pile_resistance, got, shell_to_depth, shell_to_girth, coating_mask)

    sent_back, bottom, potential = lax.optimization_barrier((sent_back, bottom, potential))
    got_back = lax.all_to_all(sent_back, both, 0, 0, tiled=True)
    potential = sweep_half(1, bottom, kept, left_now, right_now, potential)

    potential = pl.pallas_call(
        inject_kernel,
        in_specs=[smem, smem, vmem, anywhere],
        out_specs=anywhere,
        out_shape=jax.ShapeDtypeStruct((layers, rows, cols), f32),
        input_output_aliases={3: 0},
        scratch_shapes=[
            pltpu.VMEM((CAP, layers, SUB, LANES), f32),
            pltpu.SemaphoreType.DMA((2, CAP)),
        ],
        compiler_params=pltpu.CompilerParams(vmem_limit_bytes=8 << 20),
        name="inject",
    )(table, pile_block, got_back, potential)
    return (potential, current)


def solution(mesh):
    placed = (
        P(None, "gx", "gy"),
        P(None, "gx", "gy"),
        P(None, "gx", "gy"),
        P(),
        P(),
        P(("gx", "gy")),
        P(("gx", "gy"), None, None),
        P(),
        P(),
    )
    return jax.shard_map(
        on_device,
        mesh=mesh,
        in_specs=placed,
        out_specs=(P(None, "gx", "gy"), P(("gx", "gy"), None, None)),
        check_vma=False,
    )
```

```python
import functools
import math

import jax
import jax.numpy as jnp
from jax import lax
from jax.experimental import pallas as pl
from jax.experimental.pallas import tpu as pltpu
from jax.sharding import PartitionSpec as P

BLK = 8
CAP = 4
SWEEPS = 4
NEWTON = 3
LANES = 128
SUB = 8
VMEM_LIMIT = 56 << 20
SHELLS_LIMIT = 52 << 20
UNROLL = 2

vertical_ratio = 0.25
inject_gain = 0.5
anodic_slope = 1.2
cathodic_slope = 0.8
coated_conductance = 0.05


def turn(x, shift):
    return pltpu.roll(x, shift % LANES, 1)


def lane_ids(rows=SUB):
    return lax.broadcasted_iota(jnp.int32, (rows, LANES), 1)


WIDE = 32
FOLD = 4


def pack_rows(load, keep):
    lane = lane_ids()
    bands = []
    for m in range(FOLD):
        packed = load(m)
        for g in range(1, LANES // WIDE):
            moved = turn(load(m + FOLD * g), WIDE * g)
            packed = jnp.where(((lane + WIDE // 2) % LANES) // WIDE == g, moved, packed)
        keep(m, packed)
        bands.append(packed)
    part = ((lane + 4) % WIDE) // BLK
    sent = bands[0]
    for m in range(1, FOLD):
        sent = jnp.where(part == m, turn(bands[m], BLK * m), sent)
    return sent


def pack_pair(load, keep, right_ref, left_ref, at):
    rightward = lane_ids() // FOLD % 2 == (WIDE - 12 - WIDE // 2) // FOLD % 2
    sides = [
        [pack_rows(functools.partial(load, odd, i), functools.partial(keep, odd, i)) for i in range(3)]
        for odd in range(2)
    ]
    pairs = [(sides[0][0], sides[0][1]), (sides[1][0], sides[1][1]), (sides[0][2], sides[1][2])]
    for plane, (one, two) in enumerate(pairs):
        right_ref[plane, at, :] = jnp.where(rightward, one, turn(two, FOLD))
        left_ref[plane, at, :] = jnp.where(rightward, turn(two, -FOLD), one)


def table_kernel(tile_ref, me_ref, table_ref):
    def look(k, count):
        table_ref[jnp.minimum(count, SUB - 1)] = k
        return count + (tile_ref[k] == me_ref[0]).astype(jnp.int32)

    count = lax.fori_loop(0, tile_ref.shape[0], look, jnp.int32(0), unroll=16)
    for j in range(SUB):
        table_ref[j] = jnp.where(j < count, table_ref[j], -1)


def pack_kernel(p_ref, c_ref, s_ref, kept_ref, right_ref, left_ref):
    refs = (p_ref, c_ref, s_ref)

    def body(u, carry):
        def rows(odd):
            return pl.ds(pl.multiple_of(u * 2 * SUB, SUB) + odd * SUB, SUB)

        def load(odd, i, l):
            return refs[i][l, rows(odd), :]

        def keep(odd, i, m, value):
            kept_ref[i, m, rows(odd), :] = value

        pack_pair(load, keep, right_ref, left_ref, pl.ds(pl.multiple_of(u * SUB, SUB), SUB))
        return carry

    lax.fori_loop(0, p_ref.shape[1] // (2 * SUB), body, 0)


def edges_kernel(*refs):
    high_ref, low_ref = refs[6:]
    for i in range(3):
        high_ref[i] = refs[i][...]
        low_ref[i] = refs[3 + i][...]


def pack_edge_kernel(
    top_ref, bottom_ref, kept_hbm, right_hbm, left_hbm, kept_ref, right_ref, left_ref
):
    refs = (top_ref, bottom_ref)

    def load(odd, i, l):
        return refs[odd][i, l]

    def keep(odd, i, m, value):
        kept_ref[i, m, odd * SUB : (odd + 1) * SUB, :] = value

    pack_pair(load, keep, right_ref, left_ref, slice(None))


NEAR = 16
HALF = LANES // 2


def shells_kernel(
    table_ref,
    block_ref,
    p_hbm,
    c_hbm,
    s_hbm,
    top_hbm,
    bottom_hbm,
    left_hbm,
    right_hbm,
    sent_ref,
    tile_v,
    side_v,
    work_v,
    sem,
):
    layers, rows, _ = p_hbm.shape
    folds = layers // 2
    per_row = LANES // BLK
    lane = lane_ids()
    sources = (p_hbm, c_hbm, s_hbm)
    piles = [table_ref[j] for j in range(CAP)]
    filled = [k >= 0 for k in piles]
    blocks = [block_ref[jnp.maximum(k, 0)] for k in piles]
    row_of = [lax.div(b, per_row) for b in blocks]
    col_of = [lax.rem(b, per_row) for b in blocks]
    border = [
        filled[j] & ((col_of[j] == 0) | (col_of[j] == per_row - 1)) for j in range(CAP)
    ]

    def main_copy(i, j, d):
        where = pl.ds(pl.multiple_of((row_of[j] + d - 1) * SUB, SUB), SUB)
        return pltpu.make_async_copy(
            sources[i].at[:, where, :], tile_v.at[j, i, d], sem.at[j, i, d]
        )

    def edge_copy(i, j, d):
        ref = top_hbm if d == 0 else bottom_hbm
        return pltpu.make_async_copy(ref.at[i], tile_v.at[j, i, d], sem.at[j, i, d])

    def packed_tile(j, d):
        tile = row_of[j] + d - 1
        above = jnp.where(tile >= rows // SUB, rows // SUB + 1, tile)
        return jnp.where(tile < 0, rows // SUB, above)

    def side_copy(ref, j, d):
        where = pl.ds(pl.multiple_of(lax.div(packed_tile(j, d), 2) * SUB, SUB), SUB)
        return pltpu.make_async_copy(ref.at[:, where, :], side_v.at[j, d], sem.at[j, 3, d])

    def each_copy(j, act):
        @pl.when(filled[j])
        def _():
            for d in range(3):
                for i in range(3):
                    if d == 1:
                        act(main_copy(i, j, d))
                        continue
                    outside = row_of[j] == (0 if d == 0 else rows // SUB - 1)

                    @pl.when(outside)
                    def _():
                        act(edge_copy(i, j, d))

                    @pl.when(jnp.logical_not(outside))
                    def _():
                        act(main_copy(i, j, d))

        @pl.when(border[j] & (col_of[j] == 0))
        def _():
            for d in range(3):
                act(side_copy(left_hbm, j, d))

        @pl.when(border[j] & (col_of[j] > 0))
        def _():
            for d in range(3):
                act(side_copy(right_hbm, j, d))

    for j in range(CAP):
        each_copy(j, lambda copy: copy.start())
    sent_ref[...] = jnp.zeros_like(sent_ref)
    pa, c_v, s_v, pb, we_v, ws_v, wu_v, inv_v = (work_v.at[i] for i in range(8))
    zero = jnp.zeros((SUB, LANES), jnp.float32)
    for t in (0, 4):
        for ref in (pa, c_v, pb, ws_v):
            for m in range(folds):
                ref[m, t * SUB : (t + 1) * SUB, :] = zero
    for j in range(CAP):
        each_copy(j, lambda copy: copy.wait())

    slot = (lane % HALF) // NEAR
    upper = lane >= HALF
    shifts = [[(HALF * h + NEAR * j + 4 + LANES - BLK * col_of[j]) % LANES for h in (0, 1)] for j in range(CAP)]
    arrays = (pa, c_v, s_v)

    def gather(d, carry):
        at = pl.ds(pl.multiple_of((d + 1) * SUB, SUB), SUB)
        for i in range(3):
            for m in range(folds):
                value = zero
                for j in range(CAP):
                    low = pltpu.roll(tile_v[j, i, d, m], shifts[j][0], 1)
                    high = pltpu.roll(tile_v[j, i, d, m + folds], shifts[j][1], 1)
                    value = jnp.where(
                        (slot == j) & filled[j], jnp.where(upper, high, low), value
                    )
                arrays[i][m, at, :] = value
        return carry

    lax.fori_loop(0, 3, gather, 0)
    for j in range(CAP):

        @pl.when(border[j])
        def _():
            first = col_of[j] == 0
            begin = jnp.where(first, 0, NEAR - 4)
            back = jnp.where(first, 12, 4)

            def mend(d, carry):
                at = pl.ds(pl.multiple_of((d + 1) * SUB, SUB), SUB)
                odd = lax.rem(packed_tile(j, d), 2)
                apart = jnp.where(first, -FOLD, FOLD)
                for i in range(3):
                    side = side_v[j, d, 2 if i == 2 else odd]
                    skip = (0, apart, apart * odd)[i]
                    for m in range(folds):
                        value = arrays[i][m, at, :]
                        for h in (0, 1):
                            l = m + folds * h
                            base = HALF * h + NEAR * j
                            known = base + WIDE // 2 - WIDE * (l // FOLD) - BLK * (l % FOLD)
                            moved = pltpu.roll(side, (known + 2 * LANES - back + skip) % LANES, 1)
                            here = (lane >= base + begin) & (lane < base + begin + 4)
                            value = jnp.where(here, moved, value)
                        arrays[i][m, at, :] = value
                return carry

            lax.fori_loop(0, 3, mend, 0)

    def span(t, shift=0):
        return slice(t * SUB + shift, (t + 1) * SUB + shift)

    for t in (1, 2, 3):
        cells = [c_v[m, span(t), :] for m in range(folds)]
        weights, wus = [], []
        for m in range(folds):
            here = cells[m]
            we = 0.5 * (here + turn(here, -1))
            ws = 0.5 * (here + c_v[m, span(t, 1), :])
            wn = 0.5 * (here + c_v[m, span(t, -1), :])
            above = cells[m + 1] if m + 1 < folds else turn(cells[0], HALF)
            wu = (0.5 * vertical_ratio) * (here + above)
            if m + 1 == folds:
                wu = jnp.where(upper, 0.0, wu)
            we_v[m, span(t), :] = we
            ws_v[m, span(t), :] = ws
            wu_v[m, span(t), :] = wu
            weights.append(we + turn(we, 1) + ws + wn + wu)
            wus.append(wu)
        for m in range(folds):
            below = wus[m - 1] if m else turn(wus[-1], HALF)
            inside = cells[m] > 0.0
            weight = jnp.where(inside, weights[m] + below, 1.0)
            inv_v[m, span(t), :] = jnp.where(inside, 1.0 / weight, 0.0)

    def sweep(old, new, t):
        values = [old[m, span(t), :] for m in range(folds)]
        wus = [wu_v[m, span(t), :] for m in range(folds)]
        for m in range(folds):
            here = values[m]
            we = we_v[m, span(t), :]
            total = s_v[m, span(t), :] + we * turn(here, -1) + turn(we * here, 1)
            total = total + ws_v[m, span(t), :] * old[m, span(t, 1), :]
            total = total + ws_v[m, span(t, -1), :] * old[m, span(t, -1), :]
            above = values[m + 1] if m + 1 < folds else turn(values[0], HALF)
            below = wus[m - 1] * values[m - 1] if m else turn(wus[-1] * values[-1], HALF)
            total = total + wus[m] * above + below
            new[m, span(t), :] = total * inv_v[m, span(t), :]

    pairs = (pa, pb)
    for k in range(SWEEPS):
        for t in (1, 2, 3) if k < SWEEPS - 1 else (2,):
            sweep(pairs[k % 2], pairs[(k + 1) % 2], t)
    done = pairs[SWEEPS % 2]
    for j in range(CAP):

        @pl.when(filled[j])
        def _():
            packet = zero
            for l in range(layers):
                group = layers - 1 - l
                begin = HALF * (l // folds) + NEAR * j + 4
                moved = turn(done[l % folds, span(2), :], BLK * group - begin)
                packet = jnp.where(lane // BLK == group, moved, packet)
            sent_ref[piles[j]] = packet


def sweep_kernel(
    half,
    p_hbm,
    c_hbm,
    s_hbm,
    edge_hbm,
    kept_ref,
    kept_edge_ref,
    kept_inner_ref,
    left_ref,
    left_edge_ref,
    left_inner_ref,
    right_ref,
    right_edge_ref,
    right_inner_ref,
    *rest,
):
    out_ref, c_v, s_v, pa_v, pb_v, we_v, ws_v, wu_v, inv_v, sem = rest[-10:]
    layers = p_hbm.shape[0]
    tile_rows = out_ref.shape[1]
    tiles = tile_rows // SUB
    first, last = 1, tiles + 2
    edge = last if half else first
    lane = lane_ids()
    place = (lane + WIDE // 2) % WIDE
    arrays = (pa_v, c_v, s_v)
    copies = []
    own = pl.ds(0, layers)
    for i in (1, 0, 2):
        src, dst = (p_hbm, c_hbm, s_hbm)[i], arrays[i]
        begin = half * (tile_rows - SUB)
        into = SUB if half else 2 * SUB
        copies.append(
            pltpu.make_async_copy(
                src.at[:, pl.ds(begin, tile_rows + SUB), :],
                dst.at[own, pl.ds(into, tile_rows + SUB), :],
                sem.at[i, 0],
            )
        )
        copies.append(
            pltpu.make_async_copy(
                edge_hbm.at[i], dst.at[own, pl.ds(edge * SUB, SUB), :], sem.at[i, 1]
            )
        )
    for copy in copies:
        copy.start()
    zero = jnp.zeros((SUB, LANES), jnp.float32)
    for t in (0, last + 1):
        for ref in (c_v, pa_v, pb_v, ws_v):
            for l in range(layers + FOLD):
                ref[l, t * SUB : (t + 1) * SUB, :] = zero

    def at(t, shift=0):
        if shift:
            return pl.ds(t * SUB + shift, SUB)
        return pl.ds(pl.multiple_of(t * SUB, SUB), SUB)

    def join_windows(t, odd, src, at_u, kept_rows, left_rows, right_rows):
        for i, dst in enumerate(arrays):
            left = left_rows[2 if i == 2 else odd, at_u, :]
            right = right_rows[2 if i == 2 else odd, at_u, :]
            apart = (0, FOLD, FOLD * odd)[i]
            for m in range(FOLD):
                kept = kept_rows[i, m, src, :]
                still = i == 0
                west = left if still and m == 1 else turn(left, LANES + BLK - BLK * m - apart)
                east = right if still and m == 0 else turn(right, LANES + apart - BLK * m)
                inner = turn(kept, BLK)
                value = jnp.where(place < 20, east, west)
                value = jnp.where((place >= 4) & (place < 16), kept, value)
                value = jnp.where((place >= 24) | (place < 4), inner, value)
                dst[layers + m, at(t), :] = value

    def join_own(n, carry):
        at_u = pl.ds(pl.multiple_of(lax.div(n, 2) * SUB, SUB), SUB)
        src = pl.ds(pl.multiple_of(n * SUB, SUB), SUB)
        join_windows(n + 2, lax.rem(n, 2), src, at_u, kept_ref, left_ref, right_ref)
        return carry

    lax.fori_loop(0, tiles, join_own, 0)
    every = slice(None)
    join_windows(edge, half, every, every, kept_edge_ref, left_edge_ref, right_edge_ref)
    join_windows(
        first + last - edge, half, every, every, kept_inner_ref, left_inner_ref, right_inner_ref
    )
    for copy in copies[:2]:
        copy.wait()

    def prepare(t, carry):
        def faces(n, here, above):
            we = 0.5 * (here + turn(here, -1))
            ws = 0.5 * (here + c_v[n, at(t, 1), :])
            wn = 0.5 * (here + c_v[n, at(t, -1), :])
            we_v[n, at(t), :] = we
            ws_v[n, at(t), :] = ws
            weight = we + turn(we, 1) + ws + wn
            if above is None:
                return weight, None
            wu = (0.5 * vertical_ratio) * (here + above)
            wu_v[n, at(t), :] = wu
            return weight + wu, wu

        def finish(n, here, weight):
            inside = here > 0.0
            inv_v[n, at(t), :] = jnp.where(inside, 1.0 / jnp.where(inside, weight, 1.0), 0.0)

        here = c_v[0, at(t), :]
        below = None
        for l in range(layers):
            above = c_v[l + 1, at(t), :] if l + 1 < layers else None
            weight, wu = faces(l, here, above)
            finish(l, here, weight if below is None else weight + below)
            here, below = above, wu
        bands = [c_v[layers + m, at(t), :] for m in range(FOLD)]
        weights = []
        for m in range(FOLD - 1):
            weights.append(faces(layers + m, bands[m], bands[m + 1]))
        weight, _ = faces(layers + FOLD - 1, bands[-1], None)
        wu = (0.5 * vertical_ratio) * (bands[-1] + turn(bands[0], -WIDE))
        wu = jnp.where(topmost, 0.0, wu)
        wu_v[layers + FOLD - 1, at(t), :] = wu
        weights.append((weight + wu, wu))
        below = jnp.where(bottommost, 0.0, turn(wu, WIDE))
        for m in range(FOLD):
            finish(layers + m, bands[m], weights[m][0] + below)
            below = weights[m][1]
        return carry

    group = ((lane + WIDE // 2 + LANES - 4) % LANES) // WIDE
    topmost = group == LANES // WIDE - 1
    bottommost = group == 0
    lax.fori_loop(first, last + 1, prepare, 0, unroll=UNROLL)
    for copy in copies[2:]:
        copy.wait()

    def make_sweep(old, store):
        def flat(n, t, here):
            we = we_v[n, at(t), :]
            total = s_v[n, at(t), :] + we * turn(here, -1) + turn(we * here, 1)
            total = total + ws_v[n, at(t), :] * old[n, at(t, 1), :]
            return total + ws_v[n, at(t, -1), :] * old[n, at(t, -1), :]

        def sweep(t, carry):
            values = []
            bands = [old[layers + m, at(t), :] for m in range(FOLD)]
            wus = [wu_v[layers + m, at(t), :] for m in range(FOLD)]
            ups = bands[1:] + [turn(bands[0], -WIDE)]
            downs = [turn(wus[-1] * bands[-1], WIDE)]
            downs += [wus[m] * bands[m] for m in range(FOLD - 1)]
            for m in range(FOLD):
                total = flat(layers + m, t, bands[m]) + wus[m] * ups[m] + downs[m]
                values.append(total * inv_v[layers + m, at(t), :])
            extra = store.windows(t, values)
            below = None
            here = old[0, at(t), :]
            for l in range(layers):
                total = flat(l, t, here)
                if l:
                    total = total + below
                if l + 1 < layers:
                    above = old[l + 1, at(t), :]
                    wu = wu_v[l, at(t), :]
                    total = total + wu * above
                    below, here = wu * here, above
                store.layer(l, t, total * inv_v[l, at(t), :], extra)
            return carry

        return sweep

    class Keep:
        def __init__(self, new):
            self.new = new

        def windows(self, t, values):
            for m in range(FOLD):
                self.new[layers + m, at(t), :] = values[m]

        def layer(self, l, t, value, extra):
            self.new[l, at(t), :] = value

    class Finish:
        def windows(self, t, values):
            return [jnp.where(place < 16, value, turn(value, -BLK)) for value in values]

        def layer(self, l, t, value, extra):
            outer = extra[l % FOLD]
            if l >= FOLD:
                outer = turn(outer, -WIDE * (l // FOLD))
            value = jnp.where((lane >= 4) & (lane < LANES - 4), value, outer)
            out_ref[l, pl.ds(pl.multiple_of(t * SUB - 2 * SUB, SUB), SUB), :] = value

    pairs = (pa_v, pb_v)
    for k in range(SWEEPS - 1):
        lax.fori_loop(
            first, last + 1, make_sweep(pairs[k % 2], Keep(pairs[(k + 1) % 2])), 0, unroll=6
        )
    lax.fori_loop(
        first + 1, last, make_sweep(pairs[(SWEEPS - 1) % 2], Finish()), 0, unroll=UNROLL
    )


def polarize_kernel(
    tile_ref, me_ref, resist_ref, got_ref, depth_ref, girth_ref, bare_ref, current_ref, sent_ref, near_v, drive_v, sum_v
):
    layers = depth_ref.shape[0]
    rows, girth = bare_ref.shape[1:]
    step = pl.program_id(0)
    highest = lax.Precision.HIGHEST
    resist = resist_ref[0]
    lane = lane_ids(layers)
    row = lax.broadcasted_iota(jnp.int32, (layers, LANES), 0)

    @pl.when(step == 0)
    def _():
        packet = got_ref[tile_ref[me_ref[0]]]
        shell = jnp.zeros((layers, LANES), jnp.float32)
        for x in range(BLK):
            spread = jnp.broadcast_to(packet[x : x + 1, :], (layers, LANES))
            spread = pltpu.roll(spread, 0, 1, stride=BLK, stride_axis=0)
            spread = turn(spread, BLK * (x + 1) - BLK * layers)
            shell = jnp.where(lane // BLK == x, spread, shell)
        near_v[...] = jnp.dot(
            shell[:, : BLK * BLK],
            girth_ref[...],
            precision=highest,
            preferred_element_type=jnp.float32,
        )
        sum_v[...] = jnp.zeros_like(sum_v)

    drive_v[...] = lax.dot_general(
        depth_ref[...],
        near_v[...],
        (((0,), (0,)), ((), ())),
        precision=lax.Precision.HIGH,
        preferred_element_type=jnp.float32,
    )
    up = math.log2(math.e) / anodic_slope
    down = -math.log2(math.e) / cathodic_slope
    steep = resist / anodic_slope
    steep_down = resist / cathodic_slope
    coated = coated_conductance / (1.0 + coated_conductance * resist)
    chunk = 128

    def body(i, carry):
        at = pl.ds(pl.multiple_of(i * chunk, chunk), chunk)
        driving = drive_v[at, :]
        value = driving
        for n in range(NEWTON):
            anodic = jnp.exp2(value * up)
            cathodic = jnp.exp2(value * down)
            excess = resist * (anodic - cathodic)
            if n:
                excess = excess + (value - driving)
            slope = 1.0 + (steep * anodic + steep_down * cathodic)
            value = value - excess / slope
        bare_current = jnp.exp2(value * up) - jnp.exp2(value * down)
        current_ref[0, at, :] = jnp.where(bare_ref[0, at, :] != 0, bare_current, coated * driving)
        return carry

    lax.fori_loop(0, rows // chunk, body, 0)
    sum_v[...] += lax.dot_general(
        depth_ref[...],
        current_ref[0],
        (((1,), (0,)), ((), ())),
        precision=lax.Precision.HIGH,
        preferred_element_type=jnp.float32,
    )

    @pl.when(step == pl.num_programs(0) - 1)
    def _():
        cells = layers * BLK * BLK
        scale = math.sqrt(cells / (rows * girth * pl.num_programs(0)))
        back = scale * lax.dot_general(
            sum_v[...],
            girth_ref[...],
            (((1,), (1,)), ((), ())),
            precision=lax.Precision.HIGH,
            preferred_element_type=jnp.float32,
        )
        back = jnp.concatenate([back, jnp.zeros_like(back)], axis=1)
        lines = []
        for x in range(BLK):
            spread = turn(back, -BLK * x) if x else back
            spread = pltpu.roll(spread, 0, 1, stride=BLK, stride_axis=0)
            spread = jnp.where(lane // BLK == row, spread, 0.0)
            lines.append(jnp.sum(spread, axis=0, keepdims=True))
        sent_ref[...] = jnp.broadcast_to(jnp.concatenate(lines, axis=0)[None], sent_ref.shape)


def inject_kernel(table_ref, block_ref, got_ref, p_hbm, out_hbm, work_v, sem):
    layers = p_hbm.shape[0]
    per_row = LANES // BLK
    lane = lane_ids()
    piles = [table_ref[j] for j in range(CAP)]
    blocks = [block_ref[jnp.maximum(k, 0)] for k in piles]
    def window(ref, j):
        return ref.at[:, pl.ds(pl.multiple_of(blocks[j] // per_row * BLK, BLK), BLK), :]

    heads = []
    for j in range(CAP):
        head = piles[j] >= 0
        for i in range(j):
            head = head & jnp.logical_not(
                (piles[i] >= 0) & (blocks[i] // per_row == blocks[j] // per_row)
            )
        heads.append(head)
    for j in range(CAP):

        @pl.when(heads[j])
        def _():
            pltpu.make_async_copy(window(p_hbm, j), work_v.at[j], sem.at[0, j]).start()

    for j in range(CAP):

        @pl.when(heads[j])
        def _():
            pltpu.make_async_copy(window(p_hbm, j), work_v.at[j], sem.at[0, j]).wait()
            for i in range(j, CAP):

                @pl.when((piles[i] >= 0) & (blocks[i] // per_row == blocks[j] // per_row))
                def _():
                    start = blocks[i] % per_row * BLK
                    packet = inject_gain * got_ref[jnp.maximum(piles[i], 0)]
                    for l in range(layers):
                        moved = pltpu.roll(packet, (start + LANES - BLK * l) % LANES, 1)
                        inside = (lane >= start) & (lane < start + BLK)
                        work_v[j, l] = work_v[j, l] - jnp.where(inside, moved, 0.0)

            pltpu.make_async_copy(work_v.at[j], window(out_hbm, j), sem.at[1, j]).start()

    for j in range(CAP):

        @pl.when(heads[j])
        def _():
            pltpu.make_async_copy(work_v.at[j], window(out_hbm, j), sem.at[1, j]).wait()


def on_device(
    conductivity,
    source,
    potential_start,
    shell_to_depth,
    shell_to_girth,
    pile_resistance,
    coating_mask,
    pile_tile,
    pile_block,
):
    layers, rows, cols = conductivity.shape
    piles = pile_tile.shape[0]
    depth_cells, girth = coating_mask.shape[1:]
    both = ("gx", "gy")
    me = (lax.axis_index("gx") * lax.axis_size("gy") + lax.axis_index("gy")).astype(jnp.int32)
    me = me.reshape(1)
    smem = pl.BlockSpec(memory_space=pltpu.SMEM)
    vmem = pl.BlockSpec(memory_space=pltpu.VMEM)
    anywhere = pl.BlockSpec(memory_space=pl.ANY)
    f32 = jnp.float32
    three = (potential_start, conductivity, source)

    def pass_on(value, axis, up):
        count = lax.axis_size(axis)
        pairs = [(i, i + 1) for i in range(count - 1)]
        return lax.ppermute(value, axis, pairs if up else [(b, a) for a, b in pairs])

    edge_shape = jax.ShapeDtypeStruct((3, layers, SUB, cols), f32)
    corner = [
        pl.BlockSpec((layers, SUB, cols), lambda i, r=r: (0, r, 0)) for r in (rows // SUB - 1, 0)
    ]
    high, low = pl.pallas_call(
        edges_kernel,
        grid=(1,),
        in_specs=[corner[0]] * 3 + [corner[1]] * 3,
        out_specs=[pl.BlockSpec((3, layers, SUB, cols), lambda i: (0, 0, 0, 0))] * 2,
        out_shape=[edge_shape] * 2,
        name="edges",
    )(*three, *three)
    top = pass_on(high, "gx", True)
    bottom = pass_on(low, "gx", False)

    steps = 4
    packed_rows = rows + 2 * SUB
    part = pl.BlockSpec((layers, rows // steps, cols), lambda i: (0, i, 0))
    kept_shape = jax.ShapeDtypeStruct((3, FOLD, packed_rows, cols), f32)
    sent_shape = jax.ShapeDtypeStruct((3, packed_rows // 2, cols), f32)
    message = pl.BlockSpec((3, rows // steps // 2, cols), lambda i: (0, i, 0))
    kept, rightward, leftward = pl.pallas_call(
        pack_kernel,
        grid=(steps,),
        in_specs=[part, part, part],
        out_specs=[
            pl.BlockSpec((3, FOLD, rows // steps, cols), lambda i: (0, 0, i, 0)),
            message,
            message,
        ],
        out_shape=[kept_shape, sent_shape, sent_shape],
        cost_estimate=pl.CostEstimate(
            flops=6 * rows * cols * layers, bytes_accessed=16 * rows * cols * layers, transcendentals=0
        ),
        name="pack_strips",
    )(*three)
    whole = pl.BlockSpec((3, layers, SUB, cols), lambda i: (0, 0, 0, 0))
    message = pl.BlockSpec((3, SUB, cols), lambda i: (0, rows // SUB // 2, 0))
    kept, rightward, leftward = pl.pallas_call(
        pack_edge_kernel,
        grid=(1,),
        in_specs=[whole, whole, anywhere, anywhere, anywhere],
        out_specs=[
            pl.BlockSpec((3, FOLD, 2 * SUB, cols), lambda i: (0, 0, rows // SUB // 2, 0)),
            message,
            message,
        ],
        out_shape=[kept_shape, sent_shape, sent_shape],
        input_output_aliases={2: 0, 3: 1, 4: 2},
        compiler_params=pltpu.CompilerParams(vmem_limit_bytes=53 << 20),
        name="pack_edges",
    )(top, bottom, kept, rightward, leftward)
    rightward, tile_later = lax.optimization_barrier((rightward, pile_tile))
    table = pl.pallas_call(
        table_kernel,
        in_specs=[smem, smem],
        out_specs=smem,
        out_shape=jax.ShapeDtypeStruct((SUB,), jnp.int32),
        cost_estimate=pl.CostEstimate(flops=piles, bytes_accessed=8 * piles, transcendentals=0),
        name="table",
    )(tile_later, me)
    left = pass_on(rightward, "gy", True)
    right = pass_on(leftward, "gy", False)

    sent = pl.pallas_call(
        shells_kernel,
        in_specs=[smem, smem] + [anywhere] * 7,
        out_specs=vmem,
        out_shape=jax.ShapeDtypeStruct((piles, SUB, LANES), f32),
        scratch_shapes=[
            pltpu.VMEM((CAP, 3, 3, layers, SUB, LANES), f32),
            pltpu.VMEM((CAP, 3, 3, SUB, LANES), f32),
            pltpu.VMEM((8, layers // 2, 5 * SUB, LANES), f32),
            pltpu.SemaphoreType.DMA((CAP, 4, 3)),
        ],
        compiler_params=pltpu.CompilerParams(vmem_limit_bytes=SHELLS_LIMIT),
        name="shells",
    )(table, pile_block, *three, top, bottom, left, right)

    half_rows = rows // 2
    padded = pltpu.VMEM((layers + FOLD, half_rows + 5 * SUB, cols), f32)

    def sweep_half(half, edge, kept, left, right, before=None):
        def parts(lead, height, *blocks):
            zeros = (0,) * len(lead)

            def spec(height, index):
                return pl.BlockSpec(lead + (height, cols), lambda i: zeros + (index, 0))

            return [spec(height, half), spec(SUB, blocks[0]), spec(SUB, blocks[1])]

        tiles = rows // SUB
        kept_parts = parts((3, FOLD), half_rows, tiles + half, tiles // 2 - half)
        sent_parts = parts((3,), half_rows // 2, tiles // 2, tiles // 4 - half)
        operands = [*three, edge] + [kept] * 3 + [left] * 3 + [right] * 3
        specs = [anywhere] * 4 + kept_parts + sent_parts + sent_parts
        aliases = {}
        if before is not None:
            aliases = {len(operands): 0}
            operands.append(before)
            specs.append(anywhere)
        return pl.pallas_call(
            functools.partial(sweep_kernel, half),
            grid=(1,),
            in_specs=specs,
            out_specs=pl.BlockSpec((layers, half_rows, cols), lambda i: (0, half, 0)),
            out_shape=jax.ShapeDtypeStruct((layers, rows, cols), f32),
            input_output_aliases=aliases,
            scratch_shapes=[padded] * 8 + [pltpu.SemaphoreType.DMA((3, 2))],
            compiler_params=pltpu.CompilerParams(vmem_limit_bytes=VMEM_LIMIT),
            cost_estimate=pl.CostEstimate(
                flops=80 * half_rows * cols * layers,
                bytes_accessed=16 * half_rows * cols * layers,
                transcendentals=0,
            ),
            name="sweeps",
        )(*operands)

    sent, top, left_now, right_now = lax.optimization_barrier((sent, top, left, right))
    got = lax.all_to_all(sent, both, 0, 0, tiled=True)
    potential = sweep_half(0, top, kept, left_now, right_now)

    steps = 4
    part = pl.BlockSpec((1, depth_cells // steps, girth), lambda i: (0, i, 0))

    def full(*shape):
        return pl.BlockSpec(shape, lambda i: (0,) * len(shape))

    current, sent_back = pl.pallas_call(
        polarize_kernel,
        grid=(steps,),
        in_specs=[
            smem,
            smem,
            smem,
            full(piles, SUB, LANES),
            pl.BlockSpec((layers, depth_cells // steps), lambda i: (0, i)),
            full(BLK * BLK, girth),
            part,
        ],
        out_specs=[part, full(piles, SUB, LANES)],
        out_shape=[
            jax.ShapeDtypeStruct((1, depth_cells, girth), f32),
            jax.ShapeDtypeStruct((piles, SUB, LANES), f32),
        ],
        scratch_shapes=[
            pltpu.VMEM((layers, girth), f32),
            pltpu.VMEM((depth_cells // steps, girth), f32),
            pltpu.VMEM((layers, girth), f32),
        ],
        compiler_params=pltpu.CompilerParams(vmem_limit_bytes=SHELLS_LIMIT),
        name="polarize",
    )(pile_tile, me, pile_resistance, got, shell_to_depth.T, shell_to_girth, coating_mask)

    sent_back, bottom, potential = lax.optimization_barrier((sent_back, bottom, potential))
    got_back = lax.all_to_all(sent_back, both, 0, 0, tiled=True)
    potential = sweep_half(1, bottom, kept, left_now, right_now, potential)

    potential = pl.pallas_call(
        inject_kernel,
        in_specs=[smem, smem, vmem, anywhere],
        out_specs=anywhere,
        out_shape=jax.ShapeDtypeStruct((layers, rows, cols), f32),
        input_output_aliases={3: 0},
        scratch_shapes=[
            pltpu.VMEM((CAP, layers, SUB, LANES), f32),
            pltpu.SemaphoreType.DMA((2, CAP)),
        ],
        compiler_params=pltpu.CompilerParams(vmem_limit_bytes=8 << 20),
        name="inject",
    )(table, pile_block, got_back, potential)
    return (potential, current)


def solution(mesh):
    placed = (
        P(None, "gx", "gy"),
        P(None, "gx", "gy"),
        P(None, "gx", "gy"),
        P(),
        P(),
        P(("gx", "gy")),
        P(("gx", "gy"), None, None),
        P(),
        P(),
    )
    return jax.shard_map(
        on_device,
        mesh=mesh,
        in_specs=placed,
        out_specs=(P(None, "gx", "gy"), P(("gx", "gy"), None, None)),
        check_vma=False,
    )
```

```python
import functools
import math

import jax
import jax.numpy as jnp
from jax import lax
from jax.experimental import pallas as pl
from jax.experimental.pallas import tpu as pltpu
from jax.sharding import PartitionSpec as P

BLK = 8
CAP = 4
SWEEPS = 4
NEWTON = 3
LANES = 128
SUB = 8
VMEM_LIMIT = 56 << 20
SHELLS_LIMIT = 52 << 20
UNROLL = 2

vertical_ratio = 0.25
inject_gain = 0.5
anodic_slope = 1.2
cathodic_slope = 0.8
coated_conductance = 0.05


def turn(x, shift):
    return pltpu.roll(x, shift % LANES, 1)


def lane_ids(rows=SUB):
    return lax.broadcasted_iota(jnp.int32, (rows, LANES), 1)


WIDE = 32
FOLD = 4


def pack_rows(load, keep):
    lane = lane_ids()
    bands = []
    for m in range(FOLD):
        packed = load(m)
        for g in range(1, LANES // WIDE):
            moved = turn(load(m + FOLD * g), WIDE * g)
            packed = jnp.where(((lane + WIDE // 2) % LANES) // WIDE == g, moved, packed)
        keep(m, packed)
        bands.append(packed)
    part = ((lane + 4) % WIDE) // BLK
    sent = bands[0]
    for m in range(1, FOLD):
        sent = jnp.where(part == m, turn(bands[m], BLK * m), sent)
    return sent


def pack_pair(load, keep, right_ref, left_ref, at):
    rightward = lane_ids() // FOLD % 2 == (WIDE - 12 - WIDE // 2) // FOLD % 2
    sides = [
        [pack_rows(functools.partial(load, odd, i), functools.partial(keep, odd, i)) for i in range(3)]
        for odd in range(2)
    ]
    pairs = [(sides[0][0], sides[0][1]), (sides[1][0], sides[1][1]), (sides[0][2], sides[1][2])]
    for plane, (one, two) in enumerate(pairs):
        right_ref[plane, at, :] = jnp.where(rightward, one, turn(two, FOLD))
        left_ref[plane, at, :] = jnp.where(rightward, turn(two, -FOLD), one)


def table_kernel(tile_ref, me_ref, table_ref):
    def look(k, count):
        table_ref[jnp.minimum(count, SUB - 1)] = k
        return count + (tile_ref[k] == me_ref[0]).astype(jnp.int32)

    count = lax.fori_loop(0, tile_ref.shape[0], look, jnp.int32(0), unroll=16)
    for j in range(SUB):
        table_ref[j] = jnp.where(j < count, table_ref[j], -1)


def pack_kernel(p_ref, c_ref, s_ref, kept_ref, right_ref, left_ref):
    refs = (p_ref, c_ref, s_ref)

    def body(u, carry):
        def rows(odd):
            return pl.ds(pl.multiple_of(u * 2 * SUB, SUB) + odd * SUB, SUB)

        def load(odd, i, l):
            return refs[i][l, rows(odd), :]

        def keep(odd, i, m, value):
            kept_ref[i, m, rows(odd), :] = value

        pack_pair(load, keep, right_ref, left_ref, pl.ds(pl.multiple_of(u * SUB, SUB), SUB))
        return carry

    lax.fori_loop(0, p_ref.shape[1] // (2 * SUB), body, 0)


def edges_kernel(*refs):
    high_ref, low_ref = refs[6:]
    for i in range(3):
        high_ref[i] = refs[i][...]
        low_ref[i] = refs[3 + i][...]


def pack_edge_kernel(
    top_ref, bottom_ref, kept_hbm, right_hbm, left_hbm, kept_ref, right_ref, left_ref
):
    refs = (top_ref, bottom_ref)

    def load(odd, i, l):
        return refs[odd][i, l]

    def keep(odd, i, m, value):
        kept_ref[i, m, odd * SUB : (odd + 1) * SUB, :] = value

    pack_pair(load, keep, right_ref, left_ref, slice(None))


NEAR = 16
HALF = LANES // 2


def slots_of(table_ref, block_ref):
    per_row = LANES // BLK
    piles = [table_ref[j] for j in range(CAP)]
    filled = [k >= 0 for k in piles]
    blocks = [block_ref[jnp.maximum(k, 0)] for k in piles]
    row_of = [lax.div(b, per_row) for b in blocks]
    col_of = [lax.rem(b, per_row) for b in blocks]
    return piles, filled, row_of, col_of


def near_kernel(
    table_ref, block_ref, p_hbm, c_hbm, s_hbm, top_hbm, bottom_hbm, near_ref, tile_v, sem
):
    layers, rows, _ = p_hbm.shape
    folds = layers // 2
    lane = lane_ids()
    sources = (p_hbm, c_hbm, s_hbm)
    _, filled, row_of, col_of = slots_of(table_ref, block_ref)

    def main_copy(i, j, d):
        where = pl.ds(pl.multiple_of((row_of[j] + d - 1) * SUB, SUB), SUB)
        return pltpu.make_async_copy(
            sources[i].at[:, where, :], tile_v.at[j, i, d], sem.at[j, i, d]
        )

    def edge_copy(i, j, d):
        ref = top_hbm if d == 0 else bottom_hbm
        return pltpu.make_async_copy(ref.at[i], tile_v.at[j, i, d], sem.at[j, i, d])

    def each_copy(j, act):
        @pl.when(filled[j])
        def _():
            for d in range(3):
                for i in range(3):
                    if d == 1:
                        act(main_copy(i, j, d))
                        continue
                    outside = row_of[j] == (0 if d == 0 else rows // SUB - 1)

                    @pl.when(outside)
                    def _():
                        act(edge_copy(i, j, d))

                    @pl.when(jnp.logical_not(outside))
                    def _():
                        act(main_copy(i, j, d))

    for j in range(CAP):
        each_copy(j, lambda copy: copy.start())
    for j in range(CAP):
        each_copy(j, lambda copy: copy.wait())
    slot = (lane % HALF) // NEAR
    upper = lane >= HALF
    shifts = [[(HALF * h + NEAR * j + 4 + LANES - BLK * col_of[j]) % LANES for h in (0, 1)] for j in range(CAP)]
    zero = jnp.zeros((SUB, LANES), jnp.float32)

    def gather(d, carry):
        at = pl.ds(pl.multiple_of(d * SUB, SUB), SUB)
        for i in range(3):
            for m in range(folds):
                value = zero
                for j in range(CAP):
                    low = pltpu.roll(tile_v[j, i, d, m], shifts[j][0], 1)
                    high = pltpu.roll(tile_v[j, i, d, m + folds], shifts[j][1], 1)
                    value = jnp.where(
                        (slot == j) & filled[j], jnp.where(upper, high, low), value
                    )
                near_ref[i, m, at, :] = value
        return carry

    lax.fori_loop(0, 3, gather, 0)


def shells_kernel(
    table_ref, block_ref, near_ref, left_hbm, right_hbm, sent_ref, side_v, work_v, sem
):
    folds = near_ref.shape[1]
    layers = 2 * folds
    rows = (left_hbm.shape[1] - SUB) * 2
    per_row = LANES // BLK
    lane = lane_ids()
    piles, filled, row_of, col_of = slots_of(table_ref, block_ref)
    border = [
        filled[j] & ((col_of[j] == 0) | (col_of[j] == per_row - 1)) for j in range(CAP)
    ]

    def packed_tile(j, d):
        tile = row_of[j] + d - 1
        above = jnp.where(tile >= rows // SUB, rows // SUB + 1, tile)
        return jnp.where(tile < 0, rows // SUB, above)

    def side_copy(ref, j, d):
        where = pl.ds(pl.multiple_of(lax.div(packed_tile(j, d), 2) * SUB, SUB), SUB)
        return pltpu.make_async_copy(ref.at[:, where, :], side_v.at[j, d], sem.at[j, d])

    def each_copy(j, act):
        @pl.when(border[j] & (col_of[j] == 0))
        def _():
            for d in range(3):
                act(side_copy(left_hbm, j, d))

        @pl.when(border[j] & (col_of[j] > 0))
        def _():
            for d in range(3):
                act(side_copy(right_hbm, j, d))

    for j in range(CAP):
        each_copy(j, lambda copy: copy.start())
    sent_ref[...] = jnp.zeros_like(sent_ref)
    pa, c_v, s_v, pb, we_v, ws_v, wu_v, inv_v = (work_v.at[i] for i in range(8))
    zero = jnp.zeros((SUB, LANES), jnp.float32)
    for t in (0, 4):
        for ref in (pa, c_v, pb, ws_v):
            for m in range(folds):
                ref[m, t * SUB : (t + 1) * SUB, :] = zero
    arrays = (pa, c_v, s_v)
    for i in range(3):
        arrays[i][:, SUB : 4 * SUB, :] = near_ref[i]
    upper = lane >= HALF
    for j in range(CAP):
        each_copy(j, lambda copy: copy.wait())
    for j in range(CAP):

        @pl.when(border[j])
        def _():
            first = col_of[j] == 0
            begin = jnp.where(first, 0, NEAR - 4)
            back = jnp.where(first, 12, 4)

            def mend(d, carry):
                at = pl.ds(pl.multiple_of((d + 1) * SUB, SUB), SUB)
                odd = lax.rem(packed_tile(j, d), 2)
                apart = jnp.where(first, -FOLD, FOLD)
                for i in range(3):
                    side = side_v[j, d, 2 if i == 2 else odd]
                    skip = (0, apart, apart * odd)[i]
                    for m in range(folds):
                        value = arrays[i][m, at, :]
                        for h in (0, 1):
                            l = m + folds * h
                            base = HALF * h + NEAR * j
                            known = base + WIDE // 2 - WIDE * (l // FOLD) - BLK * (l % FOLD)
                            moved = pltpu.roll(side, (known + 2 * LANES - back + skip) % LANES, 1)
                            here = (lane >= base + begin) & (lane < base + begin + 4)
                            value = jnp.where(here, moved, value)
                        arrays[i][m, at, :] = value
                return carry

            lax.fori_loop(0, 3, mend, 0)

    def span(t, shift=0):
        return slice(t * SUB + shift, (t + 1) * SUB + shift)

    for t in (1, 2, 3):
        cells = [c_v[m, span(t), :] for m in range(folds)]
        weights, wus = [], []
        for m in range(folds):
            here = cells[m]
            we = 0.5 * (here + turn(here, -1))
            ws = 0.5 * (here + c_v[m, span(t, 1), :])
            wn = 0.5 * (here + c_v[m, span(t, -1), :])
            above = cells[m + 1] if m + 1 < folds else turn(cells[0], HALF)
            wu = (0.5 * vertical_ratio) * (here + above)
            if m + 1 == folds:
                wu = jnp.where(upper, 0.0, wu)
            we_v[m, span(t), :] = we
            ws_v[m, span(t), :] = ws
            wu_v[m, span(t), :] = wu
            weights.append(we + turn(we, 1) + ws + wn + wu)
            wus.append(wu)
        for m in range(folds):
            below = wus[m - 1] if m else turn(wus[-1], HALF)
            inside = cells[m] > 0.0
            weight = jnp.where(inside, weights[m] + below, 1.0)
            inv_v[m, span(t), :] = jnp.where(inside, 1.0 / weight, 0.0)

    def sweep(old, new, t):
        values = [old[m, span(t), :] for m in range(folds)]
        wus = [wu_v[m, span(t), :] for m in range(folds)]
        for m in range(folds):
            here = values[m]
            we = we_v[m, span(t), :]
            total = s_v[m, span(t), :] + we * turn(here, -1) + turn(we * here, 1)
            total = total + ws_v[m, span(t), :] * old[m, span(t, 1), :]
            total = total + ws_v[m, span(t, -1), :] * old[m, span(t, -1), :]
            above = values[m + 1] if m + 1 < folds else turn(values[0], HALF)
            below = wus[m - 1] * values[m - 1] if m else turn(wus[-1] * values[-1], HALF)
            total = total + wus[m] * above + below
            new[m, span(t), :] = total * inv_v[m, span(t), :]

    pairs = (pa, pb)
    for k in range(SWEEPS):
        for t in (1, 2, 3) if k < SWEEPS - 1 else (2,):
            sweep(pairs[k % 2], pairs[(k + 1) % 2], t)
    done = pairs[SWEEPS % 2]
    for j in range(CAP):

        @pl.when(filled[j])
        def _():
            packet = zero
            for l in range(layers):
                group = layers - 1 - l
                begin = HALF * (l // folds) + NEAR * j + 4
                moved = turn(done[l % folds, span(2), :], BLK * group - begin)
                packet = jnp.where(lane // BLK == group, moved, packet)
            sent_ref[piles[j]] = packet


def sweep_kernel(
    half,
    p_hbm,
    c_hbm,
    s_hbm,
    edge_hbm,
    kept_ref,
    kept_edge_ref,
    kept_inner_ref,
    left_ref,
    left_edge_ref,
    left_inner_ref,
    right_ref,
    right_edge_ref,
    right_inner_ref,
    *rest,
):
    out_ref, c_v, s_v, pa_v, pb_v, we_v, ws_v, wu_v, inv_v, sem = rest[-10:]
    layers = p_hbm.shape[0]
    tile_rows = out_ref.shape[1]
    tiles = tile_rows // SUB
    first, last = 1, tiles + 2
    edge = last if half else first
    lane = lane_ids()
    place = (lane + WIDE // 2) % WIDE
    arrays = (pa_v, c_v, s_v)
    copies = []
    own = pl.ds(0, layers)
    for i in (1, 0, 2):
        src, dst = (p_hbm, c_hbm, s_hbm)[i], arrays[i]
        begin = half * (tile_rows - SUB)
        into = SUB if half else 2 * SUB
        copies.append(
            pltpu.make_async_copy(
                src.at[:, pl.ds(begin, tile_rows + SUB), :],
                dst.at[own, pl.ds(into, tile_rows + SUB), :],
                sem.at[i, 0],
            )
        )
        copies.append(
            pltpu.make_async_copy(
                edge_hbm.at[i], dst.at[own, pl.ds(edge * SUB, SUB), :], sem.at[i, 1]
            )
        )
    for copy in copies:
        copy.start()
    zero = jnp.zeros((SUB, LANES), jnp.float32)
    for t in (0, last + 1):
        for ref in (c_v, pa_v, pb_v, ws_v):
            for l in range(layers + FOLD):
                ref[l, t * SUB : (t + 1) * SUB, :] = zero

    def at(t, shift=0):
        if shift:
            return pl.ds(t * SUB + shift, SUB)
        return pl.ds(pl.multiple_of(t * SUB, SUB), SUB)

    def join_windows(t, odd, src, at_u, kept_rows, left_rows, right_rows):
        for i, dst in enumerate(arrays):
            left = left_rows[2 if i == 2 else odd, at_u, :]
            right = right_rows[2 if i == 2 else odd, at_u, :]
            apart = (0, FOLD, FOLD * odd)[i]
            for m in range(FOLD):
                kept = kept_rows[i, m, src, :]
                still = i == 0
                west = left if still and m == 1 else turn(left, LANES + BLK - BLK * m - apart)
                east = right if still and m == 0 else turn(right, LANES + apart - BLK * m)
                inner = turn(kept, BLK)
                value = jnp.where(place < 20, east, west)
                value = jnp.where((place >= 4) & (place < 16), kept, value)
                value = jnp.where((place >= 24) | (place < 4), inner, value)
                dst[layers + m, at(t), :] = value

    def join_own(n, carry):
        at_u = pl.ds(pl.multiple_of(lax.div(n, 2) * SUB, SUB), SUB)
        src = pl.ds(pl.multiple_of(n * SUB, SUB), SUB)
        join_windows(n + 2, lax.rem(n, 2), src, at_u, kept_ref, left_ref, right_ref)
        return carry

    lax.fori_loop(0, tiles, join_own, 0)
    every = slice(None)
    join_windows(edge, half, every, every, kept_edge_ref, left_edge_ref, right_edge_ref)
    join_windows(
        first + last - edge, half, every, every, kept_inner_ref, left_inner_ref, right_inner_ref
    )
    for copy in copies[:2]:
        copy.wait()

    def prepare(t, carry):
        def faces(n, here, above):
            we = 0.5 * (here + turn(here, -1))
            ws = 0.5 * (here + c_v[n, at(t, 1), :])
            wn = 0.5 * (here + c_v[n, at(t, -1), :])
            we_v[n, at(t), :] = we
            ws_v[n, at(t), :] = ws
            weight = we + turn(we, 1) + ws + wn
            if above is None:
                return weight, None
            wu = (0.5 * vertical_ratio) * (here + above)
            wu_v[n, at(t), :] = wu
            return weight + wu, wu

        def finish(n, here, weight):
            inside = here > 0.0
            inv_v[n, at(t), :] = jnp.where(inside, 1.0 / jnp.where(inside, weight, 1.0), 0.0)

        here = c_v[0, at(t), :]
        below = None
        for l in range(layers):
            above = c_v[l + 1, at(t), :] if l + 1 < layers else None
            weight, wu = faces(l, here, above)
            finish(l, here, weight if below is None else weight + below)
            here, below = above, wu
        bands = [c_v[layers + m, at(t), :] for m in range(FOLD)]
        weights = []
        for m in range(FOLD - 1):
            weights.append(faces(layers + m, bands[m], bands[m + 1]))
        weight, _ = faces(layers + FOLD - 1, bands[-1], None)
        wu = (0.5 * vertical_ratio) * (bands[-1] + turn(bands[0], -WIDE))
        wu = jnp.where(topmost, 0.0, wu)
        wu_v[layers + FOLD - 1, at(t), :] = wu
        weights.append((weight + wu, wu))
        below = jnp.where(bottommost, 0.0, turn(wu, WIDE))
        for m in range(FOLD):
            finish(layers + m, bands[m], weights[m][0] + below)
            below = weights[m][1]
        return carry

    group = ((lane + WIDE // 2 + LANES - 4) % LANES) // WIDE
    topmost = group == LANES // WIDE - 1
    bottommost = group == 0
    lax.fori_loop(first, last + 1, prepare, 0, unroll=UNROLL)
    for copy in copies[2:]:
        copy.wait()

    def make_sweep(old, store):
        def flat(n, t, here):
            we = we_v[n, at(t), :]
            total = s_v[n, at(t), :] + we * turn(here, -1) + turn(we * here, 1)
            total = total + ws_v[n, at(t), :] * old[n, at(t, 1), :]
            return total + ws_v[n, at(t, -1), :] * old[n, at(t, -1), :]

        def sweep(t, carry):
            values = []
            bands = [old[layers + m, at(t), :] for m in range(FOLD)]
            wus = [wu_v[layers + m, at(t), :] for m in range(FOLD)]
            ups = bands[1:] + [turn(bands[0], -WIDE)]
            downs = [turn(wus[-1] * bands[-1], WIDE)]
            downs += [wus[m] * bands[m] for m in range(FOLD - 1)]
            for m in range(FOLD):
                total = flat(layers + m, t, bands[m]) + wus[m] * ups[m] + downs[m]
                values.append(total * inv_v[layers + m, at(t), :])
            extra = store.windows(t, values)
            below = None
            here = old[0, at(t), :]
            for l in range(layers):
                total = flat(l, t, here)
                if l:
                    total = total + below
                if l + 1 < layers:
                    above = old[l + 1, at(t), :]
                    wu = wu_v[l, at(t), :]
                    total = total + wu * above
                    below, here = wu * here, above
                store.layer(l, t, total * inv_v[l, at(t), :], extra)
            return carry

        return sweep

    class Keep:
        def __init__(self, new):
            self.new = new

        def windows(self, t, values):
            for m in range(FOLD):
                self.new[layers + m, at(t), :] = values[m]

        def layer(self, l, t, value, extra):
            self.new[l, at(t), :] = value

    class Finish:
        def windows(self, t, values):
            return [jnp.where(place < 16, value, turn(value, -BLK)) for value in values]

        def layer(self, l, t, value, extra):
            outer = extra[l % FOLD]
            if l >= FOLD:
                outer = turn(outer, -WIDE * (l // FOLD))
            value = jnp.where((lane >= 4) & (lane < LANES - 4), value, outer)
            out_ref[l, pl.ds(pl.multiple_of(t * SUB - 2 * SUB, SUB), SUB), :] = value

    pairs = (pa_v, pb_v)
    for k in range(SWEEPS - 1):
        lax.fori_loop(
            first, last + 1, make_sweep(pairs[k % 2], Keep(pairs[(k + 1) % 2])), 0, unroll=6
        )
    lax.fori_loop(
        first + 1, last, make_sweep(pairs[(SWEEPS - 1) % 2], Finish()), 0, unroll=UNROLL
    )


def polarize_kernel(
    tile_ref, me_ref, resist_ref, got_ref, depth_ref, girth_ref, bare_ref, current_ref, sent_ref, near_v, drive_v, sum_v
):
    layers = depth_ref.shape[0]
    rows, girth = bare_ref.shape[1:]
    step = pl.program_id(0)
    highest = lax.Precision.HIGHEST
    resist = resist_ref[0]
    lane = lane_ids(layers)
    row = lax.broadcasted_iota(jnp.int32, (layers, LANES), 0)

    @pl.when(step == 0)
    def _():
        packet = got_ref[tile_ref[me_ref[0]]]
        shell = jnp.zeros((layers, LANES), jnp.float32)
        for x in range(BLK):
            spread = jnp.broadcast_to(packet[x : x + 1, :], (layers, LANES))
            spread = pltpu.roll(spread, 0, 1, stride=BLK, stride_axis=0)
            spread = turn(spread, BLK * (x + 1) - BLK * layers)
            shell = jnp.where(lane // BLK == x, spread, shell)
        near_v[...] = jnp.dot(
            shell[:, : BLK * BLK],
            girth_ref[...],
            precision=highest,
            preferred_element_type=jnp.float32,
        )
        sum_v[...] = jnp.zeros_like(sum_v)

    drive_v[...] = lax.dot_general(
        depth_ref[...],
        near_v[...],
        (((0,), (0,)), ((), ())),
        precision=lax.Precision.HIGH,
        preferred_element_type=jnp.float32,
    )
    up = math.log2(math.e) / anodic_slope
    down = -math.log2(math.e) / cathodic_slope
    steep = resist / anodic_slope
    steep_down = resist / cathodic_slope
    coated = coated_conductance / (1.0 + coated_conductance * resist)
    chunk = 128

    def body(i, carry):
        at = pl.ds(pl.multiple_of(i * chunk, chunk), chunk)
        driving = drive_v[at, :]
        value = driving
        for n in range(NEWTON):
            anodic = jnp.exp2(value * up)
            cathodic = jnp.exp2(value * down)
            excess = resist * (anodic - cathodic)
            if n:
                excess = excess + (value - driving)
            slope = 1.0 + (steep * anodic + steep_down * cathodic)
            value = value - excess / slope
        bare_current = jnp.exp2(value * up) - jnp.exp2(value * down)
        current_ref[0, at, :] = jnp.where(bare_ref[0, at, :] != 0, bare_current, coated * driving)
        return carry

    lax.fori_loop(0, rows // chunk, body, 0)
    sum_v[...] += lax.dot_general(
        depth_ref[...],
        current_ref[0],
        (((1,), (0,)), ((), ())),
        precision=lax.Precision.HIGH,
        preferred_element_type=jnp.float32,
    )

    @pl.when(step == pl.num_programs(0) - 1)
    def _():
        cells = layers * BLK * BLK
        scale = math.sqrt(cells / (rows * girth * pl.num_programs(0)))
        back = scale * lax.dot_general(
            sum_v[...],
            girth_ref[...],
            (((1,), (1,)), ((), ())),
            precision=lax.Precision.HIGH,
            preferred_element_type=jnp.float32,
        )
        back = jnp.concatenate([back, jnp.zeros_like(back)], axis=1)
        lines = []
        for x in range(BLK):
            spread = turn(back, -BLK * x) if x else back
            spread = pltpu.roll(spread, 0, 1, stride=BLK, stride_axis=0)
            spread = jnp.where(lane // BLK == row, spread, 0.0)
            lines.append(jnp.sum(spread, axis=0, keepdims=True))
        sent_ref[...] = jnp.broadcast_to(jnp.concatenate(lines, axis=0)[None], sent_ref.shape)


def inject_kernel(table_ref, block_ref, got_ref, p_hbm, out_hbm, work_v, sem):
    layers = p_hbm.shape[0]
    per_row = LANES // BLK
    lane = lane_ids()
    piles = [table_ref[j] for j in range(CAP)]
    blocks = [block_ref[jnp.maximum(k, 0)] for k in piles]
    def window(ref, j):
        return ref.at[:, pl.ds(pl.multiple_of(blocks[j] // per_row * BLK, BLK), BLK), :]

    heads = []
    for j in range(CAP):
        head = piles[j] >= 0
        for i in range(j):
            head = head & jnp.logical_not(
                (piles[i] >= 0) & (blocks[i] // per_row == blocks[j] // per_row)
            )
        heads.append(head)
    for j in range(CAP):

        @pl.when(heads[j])
        def _():
            pltpu.make_async_copy(window(p_hbm, j), work_v.at[j], sem.at[0, j]).start()

    for j in range(CAP):

        @pl.when(heads[j])
        def _():
            pltpu.make_async_copy(window(p_hbm, j), work_v.at[j], sem.at[0, j]).wait()
            for i in range(j, CAP):

                @pl.when((piles[i] >= 0) & (blocks[i] // per_row == blocks[j] // per_row))
                def _():
                    start = blocks[i] % per_row * BLK
                    packet = inject_gain * got_ref[jnp.maximum(piles[i], 0)]
                    for l in range(layers):
                        moved = pltpu.roll(packet, (start + LANES - BLK * l) % LANES, 1)
                        inside = (lane >= start) & (lane < start + BLK)
                        work_v[j, l] = work_v[j, l] - jnp.where(inside, moved, 0.0)

            pltpu.make_async_copy(work_v.at[j], window(out_hbm, j), sem.at[1, j]).start()

    for j in range(CAP):

        @pl.when(heads[j])
        def _():
            pltpu.make_async_copy(work_v.at[j], window(out_hbm, j), sem.at[1, j]).wait()


def on_device(
    conductivity,
    source,
    potential_start,
    shell_to_depth,
    shell_to_girth,
    pile_resistance,
    coating_mask,
    pile_tile,
    pile_block,
):
    layers, rows, cols = conductivity.shape
    piles = pile_tile.shape[0]
    depth_cells, girth = coating_mask.shape[1:]
    both = ("gx", "gy")
    me = (lax.axis_index("gx") * lax.axis_size("gy") + lax.axis_index("gy")).astype(jnp.int32)
    me = me.reshape(1)
    smem = pl.BlockSpec(memory_space=pltpu.SMEM)
    vmem = pl.BlockSpec(memory_space=pltpu.VMEM)
    anywhere = pl.BlockSpec(memory_space=pl.ANY)
    f32 = jnp.float32
    three = (potential_start, conductivity, source)

    def pass_on(value, axis, up):
        count = lax.axis_size(axis)
        pairs = [(i, i + 1) for i in range(count - 1)]
        return lax.ppermute(value, axis, pairs if up else [(b, a) for a, b in pairs])

    edge_shape = jax.ShapeDtypeStruct((3, layers, SUB, cols), f32)
    corner = [
        pl.BlockSpec((layers, SUB, cols), lambda i, r=r: (0, r, 0)) for r in (rows // SUB - 1, 0)
    ]
    high, low = pl.pallas_call(
        edges_kernel,
        grid=(1,),
        in_specs=[corner[0]] * 3 + [corner[1]] * 3,
        out_specs=[pl.BlockSpec((3, layers, SUB, cols), lambda i: (0, 0, 0, 0))] * 2,
        out_shape=[edge_shape] * 2,
        name="edges",
    )(*three, *three)
    top = pass_on(high, "gx", True)
    bottom = pass_on(low, "gx", False)

    steps = 4
    packed_rows = rows + 2 * SUB
    part = pl.BlockSpec((layers, rows // steps, cols), lambda i: (0, i, 0))
    kept_shape = jax.ShapeDtypeStruct((3, FOLD, packed_rows, cols), f32)
    sent_shape = jax.ShapeDtypeStruct((3, packed_rows // 2, cols), f32)
    message = pl.BlockSpec((3, rows // steps // 2, cols), lambda i: (0, i, 0))
    kept, rightward, leftward = pl.pallas_call(
        pack_kernel,
        grid=(steps,),
        in_specs=[part, part, part],
        out_specs=[
            pl.BlockSpec((3, FOLD, rows // steps, cols), lambda i: (0, 0, i, 0)),
            message,
            message,
        ],
        out_shape=[kept_shape, sent_shape, sent_shape],
        cost_estimate=pl.CostEstimate(
            flops=6 * rows * cols * layers, bytes_accessed=16 * rows * cols * layers, transcendentals=0
        ),
        name="pack_strips",
    )(*three)
    whole = pl.BlockSpec((3, layers, SUB, cols), lambda i: (0, 0, 0, 0))
    message = pl.BlockSpec((3, SUB, cols), lambda i: (0, rows // SUB // 2, 0))
    kept, rightward, leftward = pl.pallas_call(
        pack_edge_kernel,
        grid=(1,),
        in_specs=[whole, whole, anywhere, anywhere, anywhere],
        out_specs=[
            pl.BlockSpec((3, FOLD, 2 * SUB, cols), lambda i: (0, 0, rows // SUB // 2, 0)),
            message,
            message,
        ],
        out_shape=[kept_shape, sent_shape, sent_shape],
        input_output_aliases={2: 0, 3: 1, 4: 2},
        compiler_params=pltpu.CompilerParams(vmem_limit_bytes=53 << 20),
        name="pack_edges",
    )(top, bottom, kept, rightward, leftward)
    rightward, tile_later = lax.optimization_barrier((rightward, pile_tile))
    table = pl.pallas_call(
        table_kernel,
        in_specs=[smem, smem],
        out_specs=smem,
        out_shape=jax.ShapeDtypeStruct((SUB,), jnp.int32),
        cost_estimate=pl.CostEstimate(flops=piles, bytes_accessed=8 * piles, transcendentals=0),
        name="table",
    )(tile_later, me)
    near = pl.pallas_call(
        near_kernel,
        in_specs=[smem, smem] + [anywhere] * 5,
        out_specs=vmem,
        out_shape=jax.ShapeDtypeStruct((3, layers // 2, 3 * SUB, LANES), f32),
        scratch_shapes=[
            pltpu.VMEM((CAP, 3, 3, layers, SUB, LANES), f32),
            pltpu.SemaphoreType.DMA((CAP, 3, 3)),
        ],
        compiler_params=pltpu.CompilerParams(vmem_limit_bytes=SHELLS_LIMIT),
        cost_estimate=pl.CostEstimate(
            flops=40 * 24 * cols * layers, bytes_accessed=150 * 24 * cols * layers, transcendentals=0
        ),
        name="near",
    )(table, pile_block, *three, top, bottom)
    left = pass_on(rightward, "gy", True)
    right = pass_on(leftward, "gy", False)

    sent = pl.pallas_call(
        shells_kernel,
        in_specs=[smem, smem, vmem, anywhere, anywhere],
        out_specs=vmem,
        out_shape=jax.ShapeDtypeStruct((piles, SUB, LANES), f32),
        scratch_shapes=[
            pltpu.VMEM((CAP, 3, 3, SUB, LANES), f32),
            pltpu.VMEM((8, layers // 2, 5 * SUB, LANES), f32),
            pltpu.SemaphoreType.DMA((CAP, 3)),
        ],
        compiler_params=pltpu.CompilerParams(vmem_limit_bytes=SHELLS_LIMIT),
        name="shells",
    )(table, pile_block, near, left, right)

    half_rows = rows // 2
    padded = pltpu.VMEM((layers + FOLD, half_rows + 5 * SUB, cols), f32)

    def sweep_half(half, edge, kept, left, right, before=None):
        def parts(lead, height, *blocks):
            zeros = (0,) * len(lead)

            def spec(height, index):
                return pl.BlockSpec(lead + (height, cols), lambda i: zeros + (index, 0))

            return [spec(height, half), spec(SUB, blocks[0]), spec(SUB, blocks[1])]

        tiles = rows // SUB
        kept_parts = parts((3, FOLD), half_rows, tiles + half, tiles // 2 - half)
        sent_parts = parts((3,), half_rows // 2, tiles // 2, tiles // 4 - half)
        operands = [*three, edge] + [kept] * 3 + [left] * 3 + [right] * 3
        specs = [anywhere] * 4 + kept_parts + sent_parts + sent_parts
        aliases = {}
        if before is not None:
            aliases = {len(operands): 0}
            operands.append(before)
            specs.append(anywhere)
        return pl.pallas_call(
            functools.partial(sweep_kernel, half),
            grid=(1,),
            in_specs=specs,
            out_specs=pl.BlockSpec((layers, half_rows, cols), lambda i: (0, half, 0)),
            out_shape=jax.ShapeDtypeStruct((layers, rows, cols), f32),
            input_output_aliases=aliases,
            scratch_shapes=[padded] * 8 + [pltpu.SemaphoreType.DMA((3, 2))],
            compiler_params=pltpu.CompilerParams(vmem_limit_bytes=VMEM_LIMIT),
            cost_estimate=pl.CostEstimate(
                flops=80 * half_rows * cols * layers,
                bytes_accessed=16 * half_rows * cols * layers,
                transcendentals=0,
            ),
            name="sweeps",
        )(*operands)

    sent, top, left_now, right_now = lax.optimization_barrier((sent, top, left, right))
    got = lax.all_to_all(sent, both, 0, 0, tiled=True)
    potential = sweep_half(0, top, kept, left_now, right_now)

    steps = 4
    part = pl.BlockSpec((1, depth_cells // steps, girth), lambda i: (0, i, 0))

    def full(*shape):
        return pl.BlockSpec(shape, lambda i: (0,) * len(shape))

    current, sent_back = pl.pallas_call(
        polarize_kernel,
        grid=(steps,),
        in_specs=[
            smem,
            smem,
            smem,
            full(piles, SUB, LANES),
            pl.BlockSpec((layers, depth_cells // steps), lambda i: (0, i)),
            full(BLK * BLK, girth),
            part,
        ],
        out_specs=[part, full(piles, SUB, LANES)],
        out_shape=[
            jax.ShapeDtypeStruct((1, depth_cells, girth), f32),
            jax.ShapeDtypeStruct((piles, SUB, LANES), f32),
        ],
        scratch_shapes=[
            pltpu.VMEM((layers, girth), f32),
            pltpu.VMEM((depth_cells // steps, girth), f32),
            pltpu.VMEM((layers, girth), f32),
        ],
        compiler_params=pltpu.CompilerParams(vmem_limit_bytes=SHELLS_LIMIT),
        name="polarize",
    )(pile_tile, me, pile_resistance, got, shell_to_depth.T, shell_to_girth, coating_mask)

    sent_back, bottom, potential = lax.optimization_barrier((sent_back, bottom, potential))
    got_back = lax.all_to_all(sent_back, both, 0, 0, tiled=True)
    potential = sweep_half(1, bottom, kept, left_now, right_now, potential)

    potential = pl.pallas_call(
        inject_kernel,
        in_specs=[smem, smem, vmem, anywhere],
        out_specs=anywhere,
        out_shape=jax.ShapeDtypeStruct((layers, rows, cols), f32),
        input_output_aliases={3: 0},
        scratch_shapes=[
            pltpu.VMEM((CAP, layers, SUB, LANES), f32),
            pltpu.SemaphoreType.DMA((2, CAP)),
        ],
        compiler_params=pltpu.CompilerParams(vmem_limit_bytes=8 << 20),
        name="inject",
    )(table, pile_block, got_back, potential)
    return (potential, current)


def solution(mesh):
    placed = (
        P(None, "gx", "gy"),
        P(None, "gx", "gy"),
        P(None, "gx", "gy"),
        P(),
        P(),
        P(("gx", "gy")),
        P(("gx", "gy"), None, None),
        P(),
        P(),
    )
    return jax.shard_map(
        on_device,
        mesh=mesh,
        in_specs=placed,
        out_specs=(P(None, "gx", "gy"), P(("gx", "gy"), None, None)),
        check_vma=False,
    )
```

```python
import functools
import math

import jax
import jax.numpy as jnp
from jax import lax
from jax.experimental import pallas as pl
from jax.experimental.pallas import tpu as pltpu
from jax.sharding import PartitionSpec as P

BLK = 8
CAP = 4
SWEEPS = 4
NEWTON = 3
LANES = 128
SUB = 8
VMEM_LIMIT = 56 << 20
SHELLS_LIMIT = 52 << 20
UNROLL = 2

vertical_ratio = 0.25
inject_gain = 0.5
anodic_slope = 1.2
cathodic_slope = 0.8
coated_conductance = 0.05


def turn(x, shift):
    return pltpu.roll(x, shift % LANES, 1)


def lane_ids(rows=SUB):
    return lax.broadcasted_iota(jnp.int32, (rows, LANES), 1)


WIDE = 32
FOLD = 4


def pack_rows(load, keep):
    lane = lane_ids()
    bands = []
    for m in range(FOLD):
        packed = load(m)
        for g in range(1, LANES // WIDE):
            moved = turn(load(m + FOLD * g), WIDE * g)
            packed = jnp.where(((lane + WIDE // 2) % LANES) // WIDE == g, moved, packed)
        keep(m, packed)
        bands.append(packed)
    part = ((lane + 4) % WIDE) // BLK
    sent = bands[0]
    for m in range(1, FOLD):
        sent = jnp.where(part == m, turn(bands[m], BLK * m), sent)
    return sent


def pack_pair(load, keep, right_ref, left_ref, at):
    rightward = lane_ids() // FOLD % 2 == (WIDE - 12 - WIDE // 2) // FOLD % 2
    sides = [
        [pack_rows(functools.partial(load, odd, i), functools.partial(keep, odd, i)) for i in range(3)]
        for odd in range(2)
    ]
    pairs = [(sides[0][0], sides[0][1]), (sides[1][0], sides[1][1]), (sides[0][2], sides[1][2])]
    for plane, (one, two) in enumerate(pairs):
        right_ref[plane, at, :] = jnp.where(rightward, one, turn(two, FOLD))
        left_ref[plane, at, :] = jnp.where(rightward, turn(two, -FOLD), one)


def table_kernel(tile_ref, me_ref, table_ref):
    def look(k, count):
        table_ref[jnp.minimum(count, SUB - 1)] = k
        return count + (tile_ref[k] == me_ref[0]).astype(jnp.int32)

    count = lax.fori_loop(0, tile_ref.shape[0], look, jnp.int32(0), unroll=16)
    for j in range(SUB):
        table_ref[j] = jnp.where(j < count, table_ref[j], -1)


def pack_kernel(p_ref, c_ref, s_ref, kept_ref, right_ref, left_ref):
    refs = (p_ref, c_ref, s_ref)

    def body(u, carry):
        def rows(odd):
            return pl.ds(pl.multiple_of(u * 2 * SUB, SUB) + odd * SUB, SUB)

        def load(odd, i, l):
            return refs[i][l, rows(odd), :]

        def keep(odd, i, m, value):
            kept_ref[i, m, rows(odd), :] = value

        pack_pair(load, keep, right_ref, left_ref, pl.ds(pl.multiple_of(u * SUB, SUB), SUB))
        return carry

    lax.fori_loop(0, p_ref.shape[1] // (2 * SUB), body, 0)


def edges_kernel(*refs):
    high_ref, low_ref = refs[6:]
    for i in range(3):
        high_ref[i] = refs[i][...]
        low_ref[i] = refs[3 + i][...]


def pack_edge_kernel(
    top_ref, bottom_ref, kept_hbm, right_hbm, left_hbm, kept_ref, right_ref, left_ref
):
    refs = (top_ref, bottom_ref)

    def load(odd, i, l):
        return refs[odd][i, l]

    def keep(odd, i, m, value):
        kept_ref[i, m, odd * SUB : (odd + 1) * SUB, :] = value

    pack_pair(load, keep, right_ref, left_ref, slice(None))


NEAR = 16
HALF = LANES // 2


def slots_of(table_ref, block_ref):
    per_row = LANES // BLK
    piles = [table_ref[j] for j in range(CAP)]
    filled = [k >= 0 for k in piles]
    blocks = [block_ref[jnp.maximum(k, 0)] for k in piles]
    row_of = [lax.div(b, per_row) for b in blocks]
    col_of = [lax.rem(b, per_row) for b in blocks]
    return piles, filled, row_of, col_of


def near_kernel(
    table_ref, block_ref, p_hbm, c_hbm, s_hbm, top_hbm, bottom_hbm, near_ref, tile_v, sem
):
    layers, rows, _ = p_hbm.shape
    folds = layers // 2
    lane = lane_ids()
    sources = (p_hbm, c_hbm, s_hbm)
    _, filled, row_of, col_of = slots_of(table_ref, block_ref)

    def main_copy(i, j, d):
        where = pl.ds(pl.multiple_of((row_of[j] + d - 1) * SUB, SUB), SUB)
        return pltpu.make_async_copy(
            sources[i].at[:, where, :], tile_v.at[j, i, d], sem.at[j, i, d]
        )

    def edge_copy(i, j, d):
        ref = top_hbm if d == 0 else bottom_hbm
        return pltpu.make_async_copy(ref.at[i], tile_v.at[j, i, d], sem.at[j, i, d])

    def each_copy(j, act):
        @pl.when(filled[j])
        def _():
            for d in range(3):
                for i in range(3):
                    if d == 1:
                        act(main_copy(i, j, d))
                        continue
                    outside = row_of[j] == (0 if d == 0 else rows // SUB - 1)

                    @pl.when(outside)
                    def _():
                        act(edge_copy(i, j, d))

                    @pl.when(jnp.logical_not(outside))
                    def _():
                        act(main_copy(i, j, d))

    for j in range(CAP):
        each_copy(j, lambda copy: copy.start())
    for j in range(CAP):
        each_copy(j, lambda copy: copy.wait())
    slot = (lane % HALF) // NEAR
    upper = lane >= HALF
    shifts = [[(HALF * h + NEAR * j + 4 + LANES - BLK * col_of[j]) % LANES for h in (0, 1)] for j in range(CAP)]
    zero = jnp.zeros((SUB, LANES), jnp.float32)

    def gather(d, carry):
        at = pl.ds(pl.multiple_of(d * SUB, SUB), SUB)
        for i in range(3):
            for m in range(folds):
                value = zero
                for j in range(CAP):
                    low = pltpu.roll(tile_v[j, i, d, m], shifts[j][0], 1)
                    high = pltpu.roll(tile_v[j, i, d, m + folds], shifts[j][1], 1)
                    value = jnp.where(
                        (slot == j) & filled[j], jnp.where(upper, high, low), value
                    )
                near_ref[i, m, at, :] = value
        return carry

    lax.fori_loop(0, 3, gather, 0)


def shells_kernel(
    table_ref, block_ref, near_ref, left_hbm, right_hbm, sent_ref, side_v, work_v, sem
):
    folds = near_ref.shape[1]
    layers = 2 * folds
    rows = (left_hbm.shape[1] - SUB) * 2
    per_row = LANES // BLK
    lane = lane_ids()
    piles, filled, row_of, col_of = slots_of(table_ref, block_ref)
    border = [
        filled[j] & ((col_of[j] == 0) | (col_of[j] == per_row - 1)) for j in range(CAP)
    ]

    def packed_tile(j, d):
        tile = row_of[j] + d - 1
        above = jnp.where(tile >= rows // SUB, rows // SUB + 1, tile)
        return jnp.where(tile < 0, rows // SUB, above)

    def side_copy(ref, j, d):
        where = pl.ds(pl.multiple_of(lax.div(packed_tile(j, d), 2) * SUB, SUB), SUB)
        return pltpu.make_async_copy(ref.at[:, where, :], side_v.at[j, d], sem.at[j, d])

    def each_copy(j, act):
        @pl.when(border[j] & (col_of[j] == 0))
        def _():
            for d in range(3):
                act(side_copy(left_hbm, j, d))

        @pl.when(border[j] & (col_of[j] > 0))
        def _():
            for d in range(3):
                act(side_copy(right_hbm, j, d))

    for j in range(CAP):
        each_copy(j, lambda copy: copy.start())
    sent_ref[...] = jnp.zeros_like(sent_ref)
    pa, c_v, s_v, pb, we_v, ws_v, wu_v, inv_v = (work_v.at[i] for i in range(8))
    zero = jnp.zeros((SUB, LANES), jnp.float32)
    for t in (0, 4):
        for ref in (pa, c_v, pb, ws_v):
            for m in range(folds):
                ref[m, t * SUB : (t + 1) * SUB, :] = zero
    arrays = (pa, c_v, s_v)
    for i in range(3):
        arrays[i][:, SUB : 4 * SUB, :] = near_ref[i]
    upper = lane >= HALF
    for j in range(CAP):
        each_copy(j, lambda copy: copy.wait())
    for j in range(CAP):

        @pl.when(border[j])
        def _():
            first = col_of[j] == 0
            begin = jnp.where(first, 0, NEAR - 4)
            back = jnp.where(first, 12, 4)

            def mend(d, carry):
                at = pl.ds(pl.multiple_of((d + 1) * SUB, SUB), SUB)
                odd = lax.rem(packed_tile(j, d), 2)
                apart = jnp.where(first, -FOLD, FOLD)
                for i in range(3):
                    side = side_v[j, d, 2 if i == 2 else odd]
                    skip = (0, apart, apart * odd)[i]
                    for m in range(folds):
                        value = arrays[i][m, at, :]
                        for h in (0, 1):
                            l = m + folds * h
                            base = HALF * h + NEAR * j
                            known = base + WIDE // 2 - WIDE * (l // FOLD) - BLK * (l % FOLD)
                            moved = pltpu.roll(side, (known + 2 * LANES - back + skip) % LANES, 1)
                            here = (lane >= base + begin) & (lane < base + begin + 4)
                            value = jnp.where(here, moved, value)
                        arrays[i][m, at, :] = value
                return carry

            lax.fori_loop(0, 3, mend, 0)

    def span(t, shift=0):
        return slice(t * SUB + shift, (t + 1) * SUB + shift)

    for t in (1, 2, 3):
        cells = [c_v[m, span(t), :] for m in range(folds)]
        weights, wus = [], []
        for m in range(folds):
            here = cells[m]
            we = 0.5 * (here + turn(here, -1))
            ws = 0.5 * (here + c_v[m, span(t, 1), :])
            wn = 0.5 * (here + c_v[m, span(t, -1), :])
            above = cells[m + 1] if m + 1 < folds else turn(cells[0], HALF)
            wu = (0.5 * vertical_ratio) * (here + above)
            if m + 1 == folds:
                wu = jnp.where(upper, 0.0, wu)
            we_v[m, span(t), :] = we
            ws_v[m, span(t), :] = ws
            wu_v[m, span(t), :] = wu
            weights.append(we + turn(we, 1) + ws + wn + wu)
            wus.append(wu)
        for m in range(folds):
            below = wus[m - 1] if m else turn(wus[-1], HALF)
            inside = cells[m] > 0.0
            weight = jnp.where(inside, weights[m] + below, 1.0)
            inv_v[m, span(t), :] = jnp.where(inside, 1.0 / weight, 0.0)

    def sweep(old, new, t):
        values = [old[m, span(t), :] for m in range(folds)]
        wus = [wu_v[m, span(t), :] for m in range(folds)]
        for m in range(folds):
            here = values[m]
            we = we_v[m, span(t), :]
            total = s_v[m, span(t), :] + we * turn(here, -1) + turn(we * here, 1)
            total = total + ws_v[m, span(t), :] * old[m, span(t, 1), :]
            total = total + ws_v[m, span(t, -1), :] * old[m, span(t, -1), :]
            above = values[m + 1] if m + 1 < folds else turn(values[0], HALF)
            below = wus[m - 1] * values[m - 1] if m else turn(wus[-1] * values[-1], HALF)
            total = total + wus[m] * above + below
            new[m, span(t), :] = total * inv_v[m, span(t), :]

    pairs = (pa, pb)
    for k in range(SWEEPS):
        for t in (1, 2, 3) if k < SWEEPS - 1 else (2,):
            sweep(pairs[k % 2], pairs[(k + 1) % 2], t)
    done = pairs[SWEEPS % 2]
    for j in range(CAP):

        @pl.when(filled[j])
        def _():
            packet = zero
            for l in range(layers):
                group = layers - 1 - l
                begin = HALF * (l // folds) + NEAR * j + 4
                moved = turn(done[l % folds, span(2), :], BLK * group - begin)
                packet = jnp.where(lane // BLK == group, moved, packet)
            sent_ref[piles[j]] = packet


def sweep_kernel(
    half,
    p_hbm,
    c_hbm,
    s_hbm,
    edge_hbm,
    kept_ref,
    kept_edge_ref,
    kept_inner_ref,
    left_ref,
    left_edge_ref,
    left_inner_ref,
    right_ref,
    right_edge_ref,
    right_inner_ref,
    *rest,
):
    out_ref, c_v, s_v, pa_v, pb_v, we_v, ws_v, wu_v, inv_v, sem = rest[-10:]
    layers = p_hbm.shape[0]
    tile_rows = out_ref.shape[1]
    tiles = tile_rows // SUB
    first, last = 1, tiles + 2
    edge = last if half else first
    lane = lane_ids()
    place = (lane + WIDE // 2) % WIDE
    arrays = (pa_v, c_v, s_v)
    copies = []
    own = pl.ds(0, layers)
    for i in (1, 0, 2):
        src, dst = (p_hbm, c_hbm, s_hbm)[i], arrays[i]
        begin = half * (tile_rows - SUB)
        into = SUB if half else 2 * SUB
        copies.append(
            pltpu.make_async_copy(
                src.at[:, pl.ds(begin, tile_rows + SUB), :],
                dst.at[own, pl.ds(into, tile_rows + SUB), :],
                sem.at[i, 0],
            )
        )
        copies.append(
            pltpu.make_async_copy(
                edge_hbm.at[i], dst.at[own, pl.ds(edge * SUB, SUB), :], sem.at[i, 1]
            )
        )
    for copy in copies:
        copy.start()
    zero = jnp.zeros((SUB, LANES), jnp.float32)
    for t in (0, last + 1):
        for ref in (c_v, pa_v, pb_v, ws_v):
            for l in range(layers + FOLD):
                ref[l, t * SUB : (t + 1) * SUB, :] = zero

    def at(t, shift=0):
        if shift:
            return pl.ds(t * SUB + shift, SUB)
        return pl.ds(pl.multiple_of(t * SUB, SUB), SUB)

    def join_windows(t, odd, src, at_u, kept_rows, left_rows, right_rows):
        for i, dst in enumerate(arrays):
            left = left_rows[2 if i == 2 else odd, at_u, :]
            right = right_rows[2 if i == 2 else odd, at_u, :]
            apart = (0, FOLD, FOLD * odd)[i]
            for m in range(FOLD):
                kept = kept_rows[i, m, src, :]
                still = i == 0
                west = left if still and m == 1 else turn(left, LANES + BLK - BLK * m - apart)
                east = right if still and m == 0 else turn(right, LANES + apart - BLK * m)
                inner = turn(kept, BLK)
                value = jnp.where(place < 20, east, west)
                value = jnp.where((place >= 4) & (place < 16), kept, value)
                value = jnp.where((place >= 24) | (place < 4), inner, value)
                dst[layers + m, at(t), :] = value

    def join_own(n, carry):
        at_u = pl.ds(pl.multiple_of(lax.div(n, 2) * SUB, SUB), SUB)
        src = pl.ds(pl.multiple_of(n * SUB, SUB), SUB)
        join_windows(n + 2, lax.rem(n, 2), src, at_u, kept_ref, left_ref, right_ref)
        return carry

    lax.fori_loop(0, tiles, join_own, 0)
    every = slice(None)
    join_windows(edge, half, every, every, kept_edge_ref, left_edge_ref, right_edge_ref)
    join_windows(
        first + last - edge, half, every, every, kept_inner_ref, left_inner_ref, right_inner_ref
    )
    for copy in copies[:2]:
        copy.wait()

    def prepare(t, carry):
        def faces(n, here, above):
            we = 0.5 * (here + turn(here, -1))
            ws = 0.5 * (here + c_v[n, at(t, 1), :])
            wn = 0.5 * (here + c_v[n, at(t, -1), :])
            we_v[n, at(t), :] = we
            ws_v[n, at(t), :] = ws
            weight = we + turn(we, 1) + ws + wn
            if above is None:
                return weight, None
            wu = (0.5 * vertical_ratio) * (here + above)
            wu_v[n, at(t), :] = wu
            return weight + wu, wu

        def finish(n, here, weight):
            inside = here > 0.0
            inv_v[n, at(t), :] = jnp.where(inside, 1.0 / jnp.where(inside, weight, 1.0), 0.0)

        here = c_v[0, at(t), :]
        below = None
        for l in range(layers):
            above = c_v[l + 1, at(t), :] if l + 1 < layers else None
            weight, wu = faces(l, here, above)
            finish(l, here, weight if below is None else weight + below)
            here, below = above, wu
        bands = [c_v[layers + m, at(t), :] for m in range(FOLD)]
        weights = []
        for m in range(FOLD - 1):
            weights.append(faces(layers + m, bands[m], bands[m + 1]))
        weight, _ = faces(layers + FOLD - 1, bands[-1], None)
        wu = (0.5 * vertical_ratio) * (bands[-1] + turn(bands[0], -WIDE))
        wu = jnp.where(topmost, 0.0, wu)
        wu_v[layers + FOLD - 1, at(t), :] = wu
        weights.append((weight + wu, wu))
        below = jnp.where(bottommost, 0.0, turn(wu, WIDE))
        for m in range(FOLD):
            finish(layers + m, bands[m], weights[m][0] + below)
            below = weights[m][1]
        return carry

    group = ((lane + WIDE // 2 + LANES - 4) % LANES) // WIDE
    topmost = group == LANES // WIDE - 1
    bottommost = group == 0
    lax.fori_loop(first, last + 1, prepare, 0, unroll=UNROLL)
    for copy in copies[2:]:
        copy.wait()

    def make_sweep(old, store):
        def flat(n, t, here):
            we = we_v[n, at(t), :]
            total = s_v[n, at(t), :] + we * turn(here, -1) + turn(we * here, 1)
            total = total + ws_v[n, at(t), :] * old[n, at(t, 1), :]
            return total + ws_v[n, at(t, -1), :] * old[n, at(t, -1), :]

        def sweep(t, carry):
            values = []
            bands = [old[layers + m, at(t), :] for m in range(FOLD)]
            wus = [wu_v[layers + m, at(t), :] for m in range(FOLD)]
            ups = bands[1:] + [turn(bands[0], -WIDE)]
            downs = [turn(wus[-1] * bands[-1], WIDE)]
            downs += [wus[m] * bands[m] for m in range(FOLD - 1)]
            for m in range(FOLD):
                total = flat(layers + m, t, bands[m]) + wus[m] * ups[m] + downs[m]
                values.append(total * inv_v[layers + m, at(t), :])
            extra = store.windows(t, values)
            below = None
            here = old[0, at(t), :]
            for l in range(layers):
                total = flat(l, t, here)
                if l:
                    total = total + below
                if l + 1 < layers:
                    above = old[l + 1, at(t), :]
                    wu = wu_v[l, at(t), :]
                    total = total + wu * above
                    below, here = wu * here, above
                store.layer(l, t, total * inv_v[l, at(t), :], extra)
            return carry

        return sweep

    class Keep:
        def __init__(self, new):
            self.new = new

        def windows(self, t, values):
            for m in range(FOLD):
                self.new[layers + m, at(t), :] = values[m]

        def layer(self, l, t, value, extra):
            self.new[l, at(t), :] = value

    class Finish:
        def windows(self, t, values):
            return [jnp.where(place < 16, value, turn(value, -BLK)) for value in values]

        def layer(self, l, t, value, extra):
            outer = extra[l % FOLD]
            if l >= FOLD:
                outer = turn(outer, -WIDE * (l // FOLD))
            value = jnp.where((lane >= 4) & (lane < LANES - 4), value, outer)
            out_ref[l, pl.ds(pl.multiple_of(t * SUB - 2 * SUB, SUB), SUB), :] = value

    pairs = (pa_v, pb_v)
    for k in range(SWEEPS - 1):
        lax.fori_loop(
            first, last + 1, make_sweep(pairs[k % 2], Keep(pairs[(k + 1) % 2])), 0, unroll=6
        )
    lax.fori_loop(
        first + 1, last, make_sweep(pairs[(SWEEPS - 1) % 2], Finish()), 0, unroll=UNROLL
    )


def polarize_kernel(
    tile_ref, me_ref, resist_ref, got_ref, depth_ref, girth_ref, bare_ref, current_ref, sent_ref, near_v, drive_v, sum_v
):
    layers = depth_ref.shape[0]
    rows, girth = bare_ref.shape[1:]
    step = pl.program_id(0)
    highest = lax.Precision.HIGHEST
    resist = resist_ref[0]
    lane = lane_ids(layers)
    row = lax.broadcasted_iota(jnp.int32, (layers, LANES), 0)

    @pl.when(step == 0)
    def _():
        packet = got_ref[tile_ref[me_ref[0]]]
        shell = jnp.zeros((layers, LANES), jnp.float32)
        for x in range(BLK):
            spread = jnp.broadcast_to(packet[x : x + 1, :], (layers, LANES))
            spread = pltpu.roll(spread, 0, 1, stride=BLK, stride_axis=0)
            spread = turn(spread, BLK * (x + 1) - BLK * layers)
            shell = jnp.where(lane // BLK == x, spread, shell)
        near_v[...] = jnp.dot(
            shell[:, : BLK * BLK],
            girth_ref[...],
            precision=highest,
            preferred_element_type=jnp.float32,
        )
        sum_v[...] = jnp.zeros_like(sum_v)

    drive_v[...] = lax.dot_general(
        depth_ref[...],
        near_v[...],
        (((0,), (0,)), ((), ())),
        precision=lax.Precision.HIGH,
        preferred_element_type=jnp.float32,
    )
    up = math.log2(math.e) / anodic_slope
    down = -math.log2(math.e) / cathodic_slope
    steep = resist / anodic_slope
    steep_down = resist / cathodic_slope
    coated = coated_conductance / (1.0 + coated_conductance * resist)
    chunk = 128

    def body(i, carry):
        at = pl.ds(pl.multiple_of(i * chunk, chunk), chunk)
        driving = drive_v[at, :]
        value = driving
        for n in range(NEWTON):
            anodic = jnp.exp2(value * up)
            cathodic = jnp.exp2(value * down)
            excess = resist * (anodic - cathodic)
            if n:
                excess = excess + (value - driving)
            slope = 1.0 + (steep * anodic + steep_down * cathodic)
            value = value - excess / slope
        bare_current = jnp.exp2(value * up) - jnp.exp2(value * down)
        current_ref[0, at, :] = jnp.where(bare_ref[0, at, :] != 0, bare_current, coated * driving)
        return carry

    lax.fori_loop(0, rows // chunk, body, 0)
    sum_v[...] += lax.dot_general(
        depth_ref[...],
        current_ref[0],
        (((1,), (0,)), ((), ())),
        precision=lax.Precision.HIGH,
        preferred_element_type=jnp.float32,
    )

    @pl.when(step == pl.num_programs(0) - 1)
    def _():
        cells = layers * BLK * BLK
        scale = math.sqrt(cells / (rows * girth * pl.num_programs(0)))
        back = scale * lax.dot_general(
            sum_v[...],
            girth_ref[...],
            (((1,), (1,)), ((), ())),
            precision=lax.Precision.HIGH,
            preferred_element_type=jnp.float32,
        )
        back = jnp.concatenate([back, jnp.zeros_like(back)], axis=1)
        lines = []
        for x in range(BLK):
            spread = turn(back, -BLK * x) if x else back
            spread = pltpu.roll(spread, 0, 1, stride=BLK, stride_axis=0)
            spread = jnp.where(lane // BLK == row, spread, 0.0)
            lines.append(jnp.sum(spread, axis=0, keepdims=True))
        sent_ref[...] = jnp.broadcast_to(jnp.concatenate(lines, axis=0)[None], sent_ref.shape)


def inject_kernel(table_ref, block_ref, got_ref, p_hbm, out_hbm, work_v, sem):
    layers = p_hbm.shape[0]
    per_row = LANES // BLK
    lane = lane_ids()
    piles = [table_ref[j] for j in range(CAP)]
    blocks = [block_ref[jnp.maximum(k, 0)] for k in piles]
    def window(ref, j):
        return ref.at[:, pl.ds(pl.multiple_of(blocks[j] // per_row * BLK, BLK), BLK), :]

    heads = []
    for j in range(CAP):
        head = piles[j] >= 0
        for i in range(j):
            head = head & jnp.logical_not(
                (piles[i] >= 0) & (blocks[i] // per_row == blocks[j] // per_row)
            )
        heads.append(head)
    for j in range(CAP):

        @pl.when(heads[j])
        def _():
            pltpu.make_async_copy(window(p_hbm, j), work_v.at[j], sem.at[0, j]).start()

    for j in range(CAP):

        @pl.when(heads[j])
        def _():
            pltpu.make_async_copy(window(p_hbm, j), work_v.at[j], sem.at[0, j]).wait()
            for i in range(j, CAP):

                @pl.when((piles[i] >= 0) & (blocks[i] // per_row == blocks[j] // per_row))
                def _():
                    start = blocks[i] % per_row * BLK
                    packet = inject_gain * got_ref[jnp.maximum(piles[i], 0)]
                    for l in range(layers):
                        moved = pltpu.roll(packet, (start + LANES - BLK * l) % LANES, 1)
                        inside = (lane >= start) & (lane < start + BLK)
                        work_v[j, l] = work_v[j, l] - jnp.where(inside, moved, 0.0)

            pltpu.make_async_copy(work_v.at[j], window(out_hbm, j), sem.at[1, j]).start()

    for j in range(CAP):

        @pl.when(heads[j])
        def _():
            pltpu.make_async_copy(work_v.at[j], window(out_hbm, j), sem.at[1, j]).wait()


def on_device(
    conductivity,
    source,
    potential_start,
    shell_to_depth,
    shell_to_girth,
    pile_resistance,
    coating_mask,
    pile_tile,
    pile_block,
):
    layers, rows, cols = conductivity.shape
    piles = pile_tile.shape[0]
    depth_cells, girth = coating_mask.shape[1:]
    both = ("gx", "gy")
    me = (lax.axis_index("gx") * lax.axis_size("gy") + lax.axis_index("gy")).astype(jnp.int32)
    me = me.reshape(1)
    smem = pl.BlockSpec(memory_space=pltpu.SMEM)
    vmem = pl.BlockSpec(memory_space=pltpu.VMEM)
    anywhere = pl.BlockSpec(memory_space=pl.ANY)
    f32 = jnp.float32
    three = (potential_start, conductivity, source)

    def pass_on(value, axis, up):
        count = lax.axis_size(axis)
        pairs = [(i, i + 1) for i in range(count - 1)]
        return lax.ppermute(value, axis, pairs if up else [(b, a) for a, b in pairs])

    edge_shape = jax.ShapeDtypeStruct((3, layers, SUB, cols), f32)
    corner = [
        pl.BlockSpec((layers, SUB, cols), lambda i, r=r: (0, r, 0)) for r in (rows // SUB - 1, 0)
    ]
    high, low = pl.pallas_call(
        edges_kernel,
        grid=(1,),
        in_specs=[corner[0]] * 3 + [corner[1]] * 3,
        out_specs=[pl.BlockSpec((3, layers, SUB, cols), lambda i: (0, 0, 0, 0))] * 2,
        out_shape=[edge_shape] * 2,
        name="edges",
    )(*three, *three)
    top = pass_on(high, "gx", True)
    bottom = pass_on(low, "gx", False)

    steps = 4
    packed_rows = rows + 2 * SUB
    part = pl.BlockSpec((layers, rows // steps, cols), lambda i: (0, i, 0))
    kept_shape = jax.ShapeDtypeStruct((3, FOLD, packed_rows, cols), f32)
    sent_shape = jax.ShapeDtypeStruct((3, packed_rows // 2, cols), f32)
    message = pl.BlockSpec((3, rows // steps // 2, cols), lambda i: (0, i, 0))
    kept, rightward, leftward = pl.pallas_call(
        pack_kernel,
        grid=(steps,),
        in_specs=[part, part, part],
        out_specs=[
            pl.BlockSpec((3, FOLD, rows // steps, cols), lambda i: (0, 0, i, 0)),
            message,
            message,
        ],
        out_shape=[kept_shape, sent_shape, sent_shape],
        cost_estimate=pl.CostEstimate(
            flops=6 * rows * cols * layers, bytes_accessed=16 * rows * cols * layers, transcendentals=0
        ),
        name="pack_strips",
    )(*three)
    whole = pl.BlockSpec((3, layers, SUB, cols), lambda i: (0, 0, 0, 0))
    message = pl.BlockSpec((3, SUB, cols), lambda i: (0, rows // SUB // 2, 0))
    kept, rightward, leftward = pl.pallas_call(
        pack_edge_kernel,
        grid=(1,),
        in_specs=[whole, whole, anywhere, anywhere, anywhere],
        out_specs=[
            pl.BlockSpec((3, FOLD, 2 * SUB, cols), lambda i: (0, 0, rows // SUB // 2, 0)),
            message,
            message,
        ],
        out_shape=[kept_shape, sent_shape, sent_shape],
        input_output_aliases={2: 0, 3: 1, 4: 2},
        compiler_params=pltpu.CompilerParams(vmem_limit_bytes=53 << 20),
        name="pack_edges",
    )(top, bottom, kept, rightward, leftward)
    rightward, tile_later = lax.optimization_barrier((rightward, pile_tile))
    table = pl.pallas_call(
        table_kernel,
        in_specs=[smem, smem],
        out_specs=smem,
        out_shape=jax.ShapeDtypeStruct((SUB,), jnp.int32),
        cost_estimate=pl.CostEstimate(flops=piles, bytes_accessed=8 * piles, transcendentals=0),
        name="table",
    )(tile_later, me)
    near = pl.pallas_call(
        near_kernel,
        in_specs=[smem, smem] + [anywhere] * 5,
        out_specs=vmem,
        out_shape=jax.ShapeDtypeStruct((3, layers // 2, 3 * SUB, LANES), f32),
        scratch_shapes=[
            pltpu.VMEM((CAP, 3, 3, layers, SUB, LANES), f32),
            pltpu.SemaphoreType.DMA((CAP, 3, 3)),
        ],
        compiler_params=pltpu.CompilerParams(vmem_limit_bytes=SHELLS_LIMIT),
        cost_estimate=pl.CostEstimate(
            flops=40 * 24 * cols * layers, bytes_accessed=150 * 24 * cols * layers, transcendentals=0
        ),
        name="near",
    )(table, pile_block, *three, top, bottom)
    left = pass_on(rightward, "gy", True)
    right = pass_on(leftward, "gy", False)

    sent = pl.pallas_call(
        shells_kernel,
        in_specs=[smem, smem, vmem, anywhere, anywhere],
        out_specs=vmem,
        out_shape=jax.ShapeDtypeStruct((piles, SUB, LANES), f32),
        scratch_shapes=[
            pltpu.VMEM((CAP, 3, 3, SUB, LANES), f32),
            pltpu.VMEM((8, layers // 2, 5 * SUB, LANES), f32),
            pltpu.SemaphoreType.DMA((CAP, 3)),
        ],
        compiler_params=pltpu.CompilerParams(vmem_limit_bytes=SHELLS_LIMIT),
        name="shells",
    )(table, pile_block, near, left, right)

    half_rows = rows // 2
    padded = pltpu.VMEM((layers + FOLD, half_rows + 5 * SUB, cols), f32)

    def sweep_half(half, edge, kept, left, right, before=None):
        def parts(lead, height, *blocks):
            zeros = (0,) * len(lead)

            def spec(height, index):
                return pl.BlockSpec(lead + (height, cols), lambda i: zeros + (index, 0))

            return [spec(height, half), spec(SUB, blocks[0]), spec(SUB, blocks[1])]

        tiles = rows // SUB
        kept_parts = parts((3, FOLD), half_rows, tiles + half, tiles // 2 - half)
        sent_parts = parts((3,), half_rows // 2, tiles // 2, tiles // 4 - half)
        operands = [*three, edge] + [kept] * 3 + [left] * 3 + [right] * 3
        specs = [anywhere] * 4 + kept_parts + sent_parts + sent_parts
        aliases = {}
        if before is not None:
            aliases = {len(operands): 0}
            operands.append(before)
            specs.append(anywhere)
        return pl.pallas_call(
            functools.partial(sweep_kernel, half),
            grid=(1,),
            in_specs=specs,
            out_specs=pl.BlockSpec((layers, half_rows, cols), lambda i: (0, half, 0)),
            out_shape=jax.ShapeDtypeStruct((layers, rows, cols), f32),
            input_output_aliases=aliases,
            scratch_shapes=[padded] * 8 + [pltpu.SemaphoreType.DMA((3, 2))],
            compiler_params=pltpu.CompilerParams(vmem_limit_bytes=VMEM_LIMIT),
            cost_estimate=pl.CostEstimate(
                flops=80 * half_rows * cols * layers,
                bytes_accessed=16 * half_rows * cols * layers,
                transcendentals=0,
            ),
            name="sweeps",
        )(*operands)

    sent, top, left_now, right_now = lax.optimization_barrier((sent, top, left, right))
    got = lax.all_to_all(sent, both, 0, 0, tiled=True)
    potential = sweep_half(0, top, kept, left_now, right_now)

    steps = 2
    part = pl.BlockSpec((1, depth_cells // steps, girth), lambda i: (0, i, 0))

    def full(*shape):
        return pl.BlockSpec(shape, lambda i: (0,) * len(shape))

    current, sent_back = pl.pallas_call(
        polarize_kernel,
        grid=(steps,),
        in_specs=[
            smem,
            smem,
            smem,
            full(piles, SUB, LANES),
            pl.BlockSpec((layers, depth_cells // steps), lambda i: (0, i)),
            full(BLK * BLK, girth),
            part,
        ],
        out_specs=[part, full(piles, SUB, LANES)],
        out_shape=[
            jax.ShapeDtypeStruct((1, depth_cells, girth), f32),
            jax.ShapeDtypeStruct((piles, SUB, LANES), f32),
        ],
        scratch_shapes=[
            pltpu.VMEM((layers, girth), f32),
            pltpu.VMEM((depth_cells // steps, girth), f32),
            pltpu.VMEM((layers, girth), f32),
        ],
        compiler_params=pltpu.CompilerParams(vmem_limit_bytes=SHELLS_LIMIT),
        name="polarize",
    )(pile_tile, me, pile_resistance, got, shell_to_depth.T, shell_to_girth, coating_mask)

    sent_back, bottom, potential = lax.optimization_barrier((sent_back, bottom, potential))
    got_back = lax.all_to_all(sent_back, both, 0, 0, tiled=True)
    potential = sweep_half(1, bottom, kept, left_now, right_now, potential)

    potential = pl.pallas_call(
        inject_kernel,
        in_specs=[smem, smem, vmem, anywhere],
        out_specs=anywhere,
        out_shape=jax.ShapeDtypeStruct((layers, rows, cols), f32),
        input_output_aliases={3: 0},
        scratch_shapes=[
            pltpu.VMEM((CAP, layers, SUB, LANES), f32),
            pltpu.SemaphoreType.DMA((2, CAP)),
        ],
        compiler_params=pltpu.CompilerParams(vmem_limit_bytes=8 << 20),
        name="inject",
    )(table, pile_block, got_back, potential)
    return (potential, current)


def solution(mesh):
    placed = (
        P(None, "gx", "gy"),
        P(None, "gx", "gy"),
        P(None, "gx", "gy"),
        P(),
        P(),
        P(("gx", "gy")),
        P(("gx", "gy"), None, None),
        P(),
        P(),
    )
    return jax.shard_map(
        on_device,
        mesh=mesh,
        in_specs=placed,
        out_specs=(P(None, "gx", "gy"), P(("gx", "gy"), None, None)),
        check_vma=False,
    )
```
